32 devices in a mesh: dp: 4 (over z), expert: 8 (over y, x, core).
Axes of the slice: x: 2, y: 2, z: 4, core: 2. Of those that a mesh axis runs over, the one named last changes fastest.
Arguments:
- tokens: bfloat16 [8192, 768], P(('dp', 'expert')), may hold values from -6 to 6
- segment_ids: int32 [32, 256], P(('dp', 'expert')), may hold values from 0 to 7, never falling along the last dimension, each value on 1 to 128 neighbouring positions
- padding: int32 [32, 256], P(('dp', 'expert')), may hold values from 0 to 1, as said below
- routes: int32 [8192, 2], P(('dp', 'expert')), may hold values from 0 to 15, all different within a row; in each aligned block of 256 rows (0 to 255, 256 to 511, ...) at most 64 rows name the same one
- w_query: float32 [768, 768], P('expert'), may hold values from -0.21875 to 0.21875
- w_key: float32 [768, 768], P('expert'), may hold values from -0.21875 to 0.21875
- w_value: float32 [768, 768], P('expert'), may hold values from -0.21875 to 0.21875
- w_out: float32 [768, 768], P('expert'), may hold values from -0.875 to 0.875
- w_router: float32 [768, 16], P('expert'), may hold values from -0.4375 to 0.4375
- shared_gate: float32 [768, 2048], P('expert'), may hold values from -0.21875 to 0.21875
- shared_up: float32 [768, 2048], P('expert'), may hold values from -0.21875 to 0.21875
- shared_down: float32 [2048, 768], P('expert'), may hold values from -0.125 to 0.125
- gain_attn: float32 [768], replicated, may hold values from 0.25 to 1.75
- gain_ffn: float32 [768], replicated, may hold values from 0.25 to 1.75
- expert_gate: bfloat16 [16, 768, 2048], P('expert'), may hold values from -0.21875 to 0.21875
- expert_up: bfloat16 [16, 768, 2048], P('expert'), may hold values from -0.21875 to 0.21875
- expert_down: bfloat16 [16, 2048, 768], P('expert'), may hold values from -0.125 to 0.125
- cotangent: bfloat16 [8192, 768], P(('dp', 'expert')), may hold values from -6 to 6
Outputs:
- output: bfloat16 [8192, 768], P(('dp', 'expert'))
- grad_tokens: bfloat16 [8192, 768], P(('dp', 'expert'))
- grad_query: float32 [768, 768], P('expert')
- grad_key: float32 [768, 768], P('expert')
- grad_value: float32 [768, 768], P('expert')
- grad_out: float32 [768, 768], P('expert')
- grad_router: float32 [768, 16], P('expert')
- grad_shared_gate: float32 [768, 2048], P('expert')
- grad_shared_up: float32 [768, 2048], P('expert')
- grad_shared_down: float32 [2048, 768], P('expert')
- grad_gain_attn: float32 [768], P('expert')
- grad_gain_ffn: float32 [768], P('expert')
- grad_expert_gate: float32 [16, 768, 2048], P('expert', 'dp')
- grad_expert_up: float32 [16, 768, 2048], P('expert', 'dp')
- grad_expert_down: float32 [16, 2048, 768], P('expert', 'dp')
The draws below stay inside these ranges and needn't reach their ends.
Inputs may be any that keep to these rules, and one draw needn't show every extreme that they name: A token's 2 experts differ. Among the routes of one sequence's 256 tokens no expert is named more than 64 times, and in every draw some sequence names some expert exactly 64 times. `segment_ids`: within a sequence ids never fall; each document has 1 to 128 positions, and some document has exactly that many. `padding`: each sequence ends in 0 to 64 padded positions (0) after its real ones (1); some sequence has none.
All inputs are finite; a program needn't handle non-finite values.
Results may differ from the reference program's by a relative error of at most 0.02.
The reference program's roundings to bfloat16 on the way count: a program that leaves them out, or rounds other values in their place, can miss the bound.
Values may be sent and summed in bfloat16 or wider, within the bound.
No kernel may reach another device: no remote copies, remote signals or barrier semaphores. Data moves between devices by JAX's collectives and lax.ppermute only.
A program may use at most 192 MiB of HBM per device.

```python
import math
import jax
import jax.numpy as jnp
import numpy as np
from jax import lax

D = 768
HEADS = 12
HEAD_DIM = 64
FF = 2048
SFF = 2048
TOP = 2
TOK_DEV = 256
EXPERTS = 16
SEQS = 32
TOKENS = 8192
CAP = 64
DOCS = 8


def draw_padding(key, part):
    tail_key, row_key = jax.random.split(jax.random.fold_in(key, 11))
    padded_count = jax.random.randint(tail_key, (SEQS, 1), 0, TOK_DEV // 4 + 1)
    full_row = jax.random.randint(row_key, (), 0, SEQS)
    padded_count = jnp.where(jnp.arange(SEQS)[:, None] == full_row, 0, padded_count)
    return (jnp.arange(TOK_DEV)[None, :] < TOK_DEV - padded_count).astype(jnp.int32)


def shard_levels(own_key, extent, cuts, smallest, high):
    gain = 1.0
    for dim, blocks in cuts:
        steps = jax.random.uniform(jax.random.fold_in(jax.random.fold_in(own_key, 6), dim), (blocks,), jnp.float32, smallest / len(cuts), high / len(cuts))
        gain = gain * jnp.repeat(jnp.exp(steps), extent[dim] // blocks).reshape((-1,) + (1,) * (len(extent) - 1 - dim))
    return gain


def split_up(amount, total, limit, lean):
    weights = [(1 << 20) // math.isqrt(standing ** lean) + 1 for standing in range(2, amount + 1)]
    surplus, counts = total - limit - (amount - 1), [1] * (amount - 1)
    while surplus > 0:
        free = [i for i in range(amount - 1) if counts[i] < limit]
        whole, left = sum([weights[i] for i in free]), surplus
        for i in free:
            addition = min(limit - counts[i], max(1, left * weights[i] // whole), surplus)
            counts[i] = counts[i] + addition
            surplus = surplus - addition
    return np.array([limit] + counts)


def uneven(rng, count, total, most, skew):
    if count == 2:
        one = jax.random.randint(rng, (), max(1, total - most), min(most, total - 1) + 1)
        return jnp.stack([one, total - one])
    sizes = jnp.asarray(split_up(count, total, most, skew), jnp.int32)
    couples = (count - 1) // 2
    donor, sink = sizes[1:1 + 2 * couples:2], sizes[2:2 + 2 * couples:2]
    margin = jnp.minimum(donor - 1, most - sink)
    shifted = jax.random.randint(jax.random.fold_in(rng, 1), (couples,), 0, 1 << 20) % (margin + 1)
    sizes = sizes.at[1:1 + 2 * couples:2].set(donor - shifted).at[2:2 + 2 * couples:2].set(sink + shifted)
    return sizes[jax.random.permutation(jax.random.fold_in(rng, 2), count)]


def routed_block(stream_key, own, number, rows, count, top, bound, skew):
    sequence = jax.random.permutation(stream_key, count)
    heavy_load, usual = shares(count, rows * top, bound, skew, True), shares(count, rows * top, bound, skew, False)
    places = jnp.arange(count)

    def named(sizes, offset_by):
        used = int((sizes > 0).sum())
        fixed = max(1, used // 4)
        passed = fixed + (places - fixed + offset_by * (used - fixed)) % max(1, count - fixed)
        return jnp.zeros((count,), jnp.int32).at[sequence[jnp.where(places < fixed, places, passed)]].set(jnp.asarray(sizes, jnp.int32))

    sizes = jnp.where(number % 4 == 0, named(heavy_load, number // 4), named(usual, number - number // 4 - 1))
    mixed = jax.random.permutation(jax.random.fold_in(own, 3), count)
    donor, taker = mixed[0:count // 2 * 2:2], mixed[1:count // 2 * 2:2]
    margin = jnp.minimum(sizes[donor] - 1, bound - sizes[taker]) // 2
    margin = jnp.where((donor == sequence[0]) | (taker == sequence[0]) | (sizes[taker] == 0), 0, jnp.maximum(margin, 0))
    passed = jax.random.randint(jax.random.fold_in(own, 4), (count // 2,), 0, 1 << 20) % (margin + 1)
    sizes = sizes.at[donor].add(-passed).at[taker].add(passed)
    labels = jnp.searchsorted(jnp.cumsum(sizes), jnp.arange(rows * top), side="right").astype(jnp.int32)
    grid = labels.reshape(top, rows).T
    grid = grid[jax.random.permutation(jax.random.fold_in(own, 1), rows)]
    offset_by = jax.random.randint(jax.random.fold_in(own, 2), (rows, 1), 0, top)
    return jnp.take_along_axis(grid, (jnp.arange(top)[None, :] + offset_by) % top, axis=1)


def shares(amount, total, limit, skew, full):
    portions = [(1 << 20) // math.isqrt(grade ** skew) + 1 for grade in range(1, amount + 1)]
    largest = limit if full else min(limit, max(-(-total // amount), total * portions[0] // sum(portions)))
    least = 1 if total - largest >= amount - 1 else 0
    given, rest = [largest] + [least] * (amount - 1), total - largest - least * (amount - 1)
    while rest > 0:
        free = [i for i in range(1, amount) if given[i] < largest] or [i for i in range(1, amount) if given[i] < limit]
        pool, remaining = sum([portions[i] for i in free]), rest
        for i in free:
            addition = min(limit - given[i], max(1, remaining * portions[i] // pool), rest)
            given[i] = given[i] + addition
            rest = rest - addition
    return np.array(given)


def noise(rng, shape, scale, limit, shards=(), kind=jnp.bfloat16):
    values = scale * jax.random.normal(rng, shape, jnp.float32)
    if shards:
        values = values * shard_levels(rng, shape, shards, -0.22, 0.18)
    return jnp.clip(values, -limit, limit).astype(kind)


def setup_inputs(seed: int = 0) -> dict:
    seeds = jax.random.split(jax.random.key(seed), 19)
    tokens = noise(seeds[0], (TOKENS, D), 1.0, 6.0, ((0, 32),))
    segment_ids = jax.vmap(lambda own: jnp.searchsorted(jnp.cumsum(uneven(own, DOCS, TOK_DEV, TOK_DEV // 2, 2)), jnp.arange(TOK_DEV), side="right"))(jax.random.split(seeds[1], SEQS)).reshape((SEQS, TOK_DEV)).astype(jnp.int32)
    padding = draw_padding(jax.random.fold_in(seeds[18], 71), 0)
    routes_keys = jax.random.split(jax.random.fold_in(seeds[3], 1), TOKENS // TOK_DEV)
    routes_turns = jax.random.permutation(jax.random.fold_in(seeds[3], 3), TOKENS // TOK_DEV)
    routes = jax.vmap(lambda own, number: routed_block(jax.random.fold_in(seeds[3], 2), own, number, TOK_DEV, EXPERTS, TOP, CAP, 2))(routes_keys, routes_turns).reshape((TOKENS, TOP))
    w_query = noise(seeds[4], (D, D), D ** -0.5, 0.21875, ((0, 8),), jnp.float32)
    w_key = noise(seeds[5], (D, D), D ** -0.5, 0.21875, ((0, 8),), jnp.float32)
    w_value = noise(seeds[6], (D, D), D ** -0.5, 0.21875, ((0, 8),), jnp.float32)
    w_out = noise(seeds[7], (D, D), (D // 16) ** -0.5, 0.875, ((0, 8),), jnp.float32)
    w_router = noise(seeds[8], (D, EXPERTS), (D // 4) ** -0.5, 0.4375, ((0, 8),), jnp.float32)
    shared_gate = noise(seeds[9], (D, SFF), D ** -0.5, 0.21875, ((0, 8),), jnp.float32)
    shared_up = noise(seeds[10], (D, SFF), D ** -0.5, 0.21875, ((0, 8),), jnp.float32)
    shared_down = noise(seeds[11], (SFF, D), SFF ** -0.5, 0.125, ((0, 8),), jnp.float32)
    gain_attn = jnp.clip(1.0 + 0.15 * jax.random.normal(seeds[12], (D,), jnp.float32), 0.25, 1.75)
    gain_ffn = jnp.clip(1.0 + 0.15 * jax.random.normal(seeds[13], (D,), jnp.float32), 0.25, 1.75)
    expert_gate = noise(seeds[14], (EXPERTS, D, FF), D ** -0.5, 0.21875, ((0, 8),))
    expert_up = noise(seeds[15], (EXPERTS, D, FF), D ** -0.5, 0.21875, ((0, 8),))
    expert_down = noise(seeds[16], (EXPERTS, FF, D), FF ** -0.5, 0.125, ((0, 8),))
    cotangent = noise(seeds[17], (TOKENS, D), 1.0, 6.0, ((0, 32),))
    return dict(tokens=tokens, segment_ids=segment_ids, padding=padding, routes=routes, w_query=w_query, w_key=w_key, w_value=w_value, w_out=w_out, w_router=w_router, shared_gate=shared_gate, shared_up=shared_up, shared_down=shared_down, gain_attn=gain_attn, gain_ffn=gain_ffn, expert_gate=expert_gate, expert_up=expert_up, expert_down=expert_down, cotangent=cotangent)


@jax.custom_vjp
def low(v):
    return lax.optimization_barrier(v.astype(jnp.bfloat16)).astype(jnp.float32)

@jax.custom_vjp
def low_back(v):
    return v

def low_keep(v):
    return (low(v), None)

def low_pass(kept, grad):
    return (grad,)

def back_keep(v):
    return (v, None)

def back_low(kept, grad):
    return (low(grad),)
low.defvjp(low_keep, low_pass)
low_back.defvjp(back_keep, back_low)
epsilon = 1e-06
rope_base = 10000.0
masked_score = -1e+30
highest = lax.Precision.HIGHEST

def matmul(left_side, right_side):
    return jnp.dot(left_side, right_side, precision=highest, preferred_element_type=jnp.float32)

def rms_norm(values, gain_vector):
    return values * lax.rsqrt(lax.optimization_barrier(jnp.mean(values * values, axis=-1, keepdims=True)) + epsilon) * gain_vector

def silu_product(gate_pre, up_pre):
    return gate_pre * jax.nn.sigmoid(gate_pre) * up_pre

def rope_tables(row_count):
    half_dim = HEAD_DIM // 2
    frequency = rope_base ** (-(2.0 * jnp.arange(half_dim, dtype=jnp.float32)) / HEAD_DIM)
    angles = jnp.arange(row_count, dtype=jnp.float32)[:, None] * frequency[None, :]
    return (jnp.cos(angles)[:, None, :], jnp.sin(angles)[:, None, :])

def rotate(values, cosine_table, sine_table):
    half_dim = HEAD_DIM // 2
    leading = values[..., :half_dim]
    trailing = values[..., half_dim:]
    return jnp.concatenate([leading * cosine_table - trailing * sine_table, trailing * cosine_table + leading * sine_table], axis=-1)

def attend(query, key_rot, value_heads, segment, key_live):
    raw_scores = low_back(jnp.einsum('qhd,khd->hqk', query, key_rot, precision=highest))
    places = jnp.arange(TOK_DEV)
    allowed = (places[None, :] <= places[:, None]) & (segment[None, :] == segment[:, None]) & (key_live[None, :] > 0)
    allowed = allowed | (places[None, :] == places[:, None])
    scores = jnp.where(allowed[None], raw_scores * HEAD_DIM ** (-0.5), masked_score)
    attn_probs = jax.nn.softmax(scores, axis=-1)
    return jnp.einsum('hqk,khd->qhd', low(attn_probs), value_heads, precision=highest)

def attend_items(items):
    return jax.vmap(attend)(items[0], items[1], items[2], items[3], items[4])

def expert_rows(items):
    route_rows, w_gate, w_up, w_down = items
    gate_pre = low_back(matmul(route_rows, w_gate))
    up_pre = low_back(matmul(route_rows, w_up))
    activation = low(silu_product(gate_pre, up_pre))
    return low(low_back(matmul(activation, w_down)))

def whole_layer(floats, segment_ids, padding, routes):
    tokens, w_query, w_key, w_value, w_out, w_router, shared_gate, shared_up, shared_down, gain_attn, gain_ffn, expert_gate, expert_up, expert_down = floats
    key_live = padding.reshape(TOKENS).astype(jnp.float32)
    h_one = low(rms_norm(tokens, gain_attn))
    cosine_table, sine_table = rope_tables(TOK_DEV)

    def split_heads(values):
        return values.reshape(SEQS, TOK_DEV, HEADS, HEAD_DIM)
    query = low(rotate(split_heads(low_back(matmul(h_one, low(w_query)))), cosine_table, sine_table))
    key_rot = low(rotate(split_heads(low_back(matmul(h_one, low(w_key)))), cosine_table, sine_table))
    value_heads = split_heads(low(low_back(matmul(h_one, low(w_value)))))
    group_size = min(SEQS, max(1, 4096 // TOK_DEV))

    def grouped(values):
        return values.reshape((SEQS // group_size, group_size) + values.shape[1:])
    mixed_all = lax.map(jax.checkpoint(attend_items), (grouped(query), grouped(key_rot), grouped(value_heads), grouped(segment_ids), grouped(key_live.reshape(SEQS, TOK_DEV))))
    mixed_all = low(low_back(mixed_all.reshape(TOKENS, D)))
    attn_branch = low_back(matmul(mixed_all, low(w_out)))
    residual = tokens + attn_branch
    h_two = low(rms_norm(residual, gain_ffn))
    logits = low_back(matmul(h_two, low(w_router)))
    router_probs = jax.nn.softmax(logits, axis=-1)
    chosen = jnp.take_along_axis(router_probs, routes, axis=1) * key_live[:, None]
    shared_gate_pre = low_back(matmul(h_two, low(shared_gate)))
    shared_up_pre = low_back(matmul(h_two, low(shared_up)))
    shared_act = low(silu_product(shared_gate_pre, shared_up_pre))
    shared_outcome = low_back(matmul(shared_act, low(shared_down)))
    flat_expert = routes.reshape(SEQS, TOK_DEV * TOP)
    onehot = (flat_expert[:, :, None] == jnp.arange(EXPERTS, dtype=jnp.int32)[None, None, :]).astype(jnp.int32)
    slot_index = lax.optimization_barrier(jnp.sum(jnp.cumsum(onehot, axis=1) * onehot, axis=2)) - 1
    sequence_index = jnp.arange(SEQS, dtype=jnp.int32)[:, None]
    target = (flat_expert * (SEQS * CAP) + sequence_index * CAP + slot_index).reshape(TOKENS * TOP).astype(jnp.int32)
    route_rows = low_back(jnp.repeat(h_two, TOP, axis=0))
    buffer = jnp.zeros((EXPERTS * SEQS * CAP, D), jnp.float32).at[target].set(route_rows)
    outputs = lax.map(jax.checkpoint(expert_rows), (buffer.reshape(EXPERTS, SEQS * CAP, D), expert_gate, expert_up, expert_down))
    picked = outputs.reshape(EXPERTS * SEQS * CAP, D)[target].reshape(TOKENS, TOP, D)
    expert_sum = lax.optimization_barrier(jnp.sum(chosen[:, :, None] * picked, axis=1))
    return residual + shared_outcome + expert_sum

def reference(tokens, segment_ids, padding, routes, w_query, w_key, w_value, w_out, w_router, shared_gate, shared_up, shared_down, gain_attn, gain_ffn, expert_gate, expert_up, expert_down, cotangent):
    floats = (tokens.astype(jnp.float32), w_query, w_key, w_value, w_out, w_router, shared_gate, shared_up, shared_down, gain_attn, gain_ffn, expert_gate.astype(jnp.float32), expert_up.astype(jnp.float32), expert_down.astype(jnp.float32))

    def bound_layer(values):
        return whole_layer(values, segment_ids, padding, routes)
    result, pullback = jax.vjp(bound_layer, floats)
    grads = pullback(cotangent.astype(jnp.float32))[0]
    return (result.astype(jnp.bfloat16), grads[0].astype(jnp.bfloat16), grads[1], grads[2], grads[3], grads[4], grads[5], grads[6], grads[7], grads[8], grads[9], grads[10], grads[11], grads[12], grads[13])
```

```python
import numpy as np

import jax
import jax.numpy as jnp
from jax import lax
from jax.experimental import pallas as pl
from jax.experimental.pallas import tpu as pltpu
from jax.sharding import PartitionSpec as P

HEADS = 12
HEAD_DIM = 64
CAP = 64
EPS = 1e-06
ROPE_BASE = 10000.0
MASKED = -1e30
SCALE = HEAD_DIM**-0.5
F32 = jnp.float32
BF16 = jnp.bfloat16
MIB = 1 << 20
VMEM_SPEC = pl.BlockSpec(memory_space=pltpu.VMEM)
SMEM_SPEC = pl.BlockSpec(memory_space=pltpu.SMEM)
ANY_SPEC = pl.BlockSpec(memory_space=pl.ANY)


def nn(a, b):
    return jnp.dot(a, b, preferred_element_type=F32)


def nt(a, b):
    return lax.dot_general(a, b, (((1,), (1,)), ((), ())), preferred_element_type=F32)


def tn(a, b):
    return lax.dot_general(a, b, (((0,), (0,)), ((), ())), preferred_element_type=F32)


def sds(shape, dtype):
    return jax.ShapeDtypeStruct(shape, dtype)


def cost(flops, nbytes):
    return pl.CostEstimate(flops=int(flops), bytes_accessed=int(nbytes), transcendentals=0)


def params(mib, semantics=None):
    return pltpu.CompilerParams(vmem_limit_bytes=mib * MIB, dimension_semantics=semantics)


def swap(x, k):
    n = lax.axis_size("expert")
    return lax.ppermute(x, "expert", [(j, j ^ k) for j in range(n)])


def shift(x, k):
    n = lax.axis_size("dp")
    return lax.ppermute(x, "dp", [(j, (j + k) % n) for j in range(n)])


def plane_gather(x):
    rows = x.shape[0]
    half = rows // 32 * 16
    a = swap(x, 2)
    b = swap(x, 4)
    d0 = swap(a[:half], 4)
    d1 = swap(b[half:], 2)
    near = [(0, 0, x), (2, 0, a), (4, 0, b), (6, 0, d0), (6, half, d1)]
    return near + [(k + 1, at, swap(piece, 1)) for k, at, piece in near]


def plane_scatter(odd, even):
    came = swap(odd, 1)
    sums = [(even[j].astype(F32) + came[j].astype(F32)).astype(odd.dtype) for j in range(4)]
    return [sums[0], swap(sums[1], 2), swap(sums[2], 4), swap(sums[3], 6)]


def dp_sum(quarters):
    n = lax.axis_size("dp")
    if n != 4:
        whole = lax.psum(quarters, "dp")
        return [whole[0], whole[3], whole[2], whole[1]], jnp.int32(0)
    z = lax.axis_index("dp")
    total = lax.dynamic_index_in_dim(quarters, z, 0, False).astype(F32)
    for k in (1, 2, 3):
        piece = lax.dynamic_index_in_dim(quarters, (z + k) % 4, 0, False)
        total = total + shift(piece, k).astype(F32)
    total = total.astype(quarters.dtype)
    return [total] + [shift(total, k) for k in (1, 2, 3)], z


def norm_scale(values):
    return lax.rsqrt(jnp.mean(values * values, axis=-1, keepdims=True) + EPS)


def silu_parts(gate):
    logistic = 1.0 / (1.0 + jnp.exp(-gate))
    return gate * logistic, logistic * (1.0 + gate * (1.0 - logistic))


def half_swap(x):
    lane = lax.broadcasted_iota(jnp.int32, x.shape, 1)
    half = HEAD_DIM // 2
    return jnp.where(
        lane % HEAD_DIM < half, pltpu.roll(x, x.shape[1] - half, 1), pltpu.roll(x, half, 1)
    )


def place_copies(i, layout, step, refs, target, sems):
    copies = []
    for n, ((k, at, rows), ref) in enumerate(zip(layout, refs)):
        start = pl.multiple_of((i ^ k) * step + at, 16)
        copies.append(pltpu.make_async_copy(ref, target.at[pl.ds(start, rows), :], sems.at[n]))
    return copies


def layout_of(pieces):
    return tuple((k, at, piece.shape[0]) for k, at, piece in pieces)


def rope_tables(length):
    half = HEAD_DIM // 2
    frequency = (ROPE_BASE ** (-(2.0 * np.arange(half, dtype=np.float32)) / HEAD_DIM)).astype(
        np.float32
    )
    angles = (np.arange(length, dtype=np.float32)[:, None] * frequency[None, :]).astype(np.float32)
    cosine, sine = np.cos(angles), np.sin(angles)
    return (
        np.concatenate([cosine] * 4, 1).astype(np.float32),
        np.concatenate([-sine, sine, -sine, sine], 1).astype(np.float32),
    )


def assemble(idx, pieces, step):
    layout = layout_of(pieces)
    width = pieces[0][2].shape[1]
    rows = step * 8

    def kernel(idx_ref, *refs):
        n = len(layout)
        copies = place_copies(idx_ref[0], layout, step, refs[:n], refs[n], refs[n + 1])
        for c in copies:
            c.start()
        for c in copies:
            c.wait()

    return pl.pallas_call(
        kernel,
        out_shape=sds((rows, width), pieces[0][2].dtype),
        in_specs=[SMEM_SPEC] + [ANY_SPEC] * len(layout),
        out_specs=VMEM_SPEC,
        scratch_shapes=[pltpu.SemaphoreType.DMA((len(layout),))],
        compiler_params=params(8),
        name="assemble",
    )(idx, *[p for _, _, p in pieces])


def attention_forward(idx, tokens, seg_row, seg_col, live_row, gain1, gain2, pieces):
    layout = layout_of(pieces)
    n = len(layout)
    length, width = tokens.shape
    step = width // 8
    cosine, sine = rope_tables(length)

    def kernel(idx_ref, x_ref, sr_ref, sc_ref, lv_ref, g1_ref, g2_ref, cos_ref, sin_ref, *refs):
        piece_refs, refs = refs[:n], refs[n:]
        h1_ref, q_ref, k_ref, v_ref, o_ref, p_ref, x1_ref, h2_ref = refs[:8]
        wbuf, pre, sems = refs[8:]
        copies = place_copies(idx_ref[0], layout, step, piece_refs, wbuf, sems)
        for c in copies:
            c.start()
        x = x_ref[...].astype(F32)
        h1 = (x * norm_scale(x) * g1_ref[...]).astype(BF16)
        h1_ref[...] = h1
        row = lax.broadcasted_iota(jnp.int32, (length, length), 0)
        col = lax.broadcasted_iota(jnp.int32, (length, length), 1)
        allowed = (col == row) | (
            (col <= row) & (sr_ref[...] == sc_ref[...]) & (lv_ref[...] > 0.0)
        )
        bias = jnp.where(allowed, 0.0, MASKED)
        for c in copies:
            c.wait()
        pre[...] = nn(h1, wbuf[:, : 3 * width])
        first = lax.broadcasted_iota(jnp.int32, (length, 128), 1) < HEAD_DIM

        def pair(hp, carry):
            at = pl.multiple_of(hp * 128, 128)
            qp = pre[:, pl.ds(at, 128)]
            kp = pre[:, pl.ds(at + width, 128)]
            v = pre[:, pl.ds(at + 2 * width, 128)].astype(BF16)
            cosv, sinv = cos_ref[...], sin_ref[...]
            q = (qp * cosv + half_swap(qp) * sinv).astype(BF16)
            k = (kp * cosv + half_swap(kp) * sinv).astype(BF16)
            q_ref[:, pl.ds(at, 128)] = q
            k_ref[:, pl.ds(at, 128)] = k
            v_ref[:, pl.ds(at, 128)] = v
            mixed = jnp.zeros((length, 128), F32)
            zero = jnp.zeros_like(q)
            for h in range(2):
                mine = first if h == 0 else jnp.logical_not(first)
                s = nt(jnp.where(mine, q, zero), k) * SCALE + bias
                e = jnp.exp(s - jnp.max(s, axis=-1, keepdims=True))
                p = e / jnp.sum(e, axis=-1, keepdims=True)
                p_ref[2 * hp + h] = p
                mixed = mixed + nn(p.astype(BF16), jnp.where(mine, v, zero))
            o_ref[:, pl.ds(at, 128)] = mixed.astype(BF16)
            return carry

        lax.fori_loop(0, HEADS // 2, pair, 0)
        x1 = x + nn(o_ref[...], wbuf[:, 3 * width :])
        x1_ref[...] = x1
        h2_ref[...] = (x1 * norm_scale(x1) * g2_ref[...]).astype(BF16)

    flat = sds((length, width), BF16)
    return pl.pallas_call(
        kernel,
        out_shape=(
            flat, flat, flat, flat, flat,
            sds((HEADS, length, length), F32),
            sds((length, width), F32),
            flat,
        ),
        in_specs=[SMEM_SPEC] + [VMEM_SPEC] * 8 + [ANY_SPEC] * n,
        out_specs=(VMEM_SPEC,) * 8,
        scratch_shapes=[
            pltpu.VMEM((width, 4 * width), BF16),
            pltpu.VMEM((length, 3 * width), F32),
            pltpu.SemaphoreType.DMA((n,)),
        ],
        compiler_params=params(32),
        cost_estimate=cost(8 * length * width * width, 12 << 20),
        name="attention_forward",
    )(idx, tokens, seg_row, seg_col, live_row, gain1, gain2, cosine, sine,
      *[p for _, _, p in pieces])


def route_rows(meta, prob, le, i, upper, length):
    expert = (2 * i + le).astype(F32)
    hit = (meta[:, :length] == expert) | (meta[:, length : 2 * length] == expert)
    hot = jnp.where(hit, 1.0, 0.0)
    rank = nn(jnp.broadcast_to(hot, (16, length)).astype(BF16), upper)[0:1]
    slot = lax.broadcasted_iota(jnp.int32, (CAP, length), 0).astype(F32) + 1.0
    one = jnp.where((slot == rank) & hit, 1.0, 0.0)
    which = lax.broadcasted_iota(jnp.int32, prob.shape, 0) == 2 * i + le
    weight = jnp.sum(jnp.where(which, prob, 0.0), axis=0, keepdims=True)
    return one, weight * meta[:, 2 * length :]


def router_probs(router_t, rows):
    logits = nt(router_t, rows)
    e = jnp.exp(logits - jnp.max(logits, axis=0, keepdims=True))
    return e / jnp.sum(e, axis=0, keepdims=True)


def upper_ones(length):
    return jnp.where(
        lax.broadcasted_iota(jnp.int32, (length, length), 0)
        <= lax.broadcasted_iota(jnp.int32, (length, length), 1),
        1.0,
        0.0,
    ).astype(BF16)


def dispatch_plane(idx, router_t, h_pieces, g_pieces, length, width):
    h_layout, g_layout = layout_of(h_pieces), layout_of(g_pieces)
    nh, ng = len(h_layout), len(g_layout)
    slots = 8 * CAP
    ext = length + 16

    def kernel(idx_ref, wr_ref, *refs):
        hp, gp, refs = refs[:nh], refs[nh : nh + ng], refs[nh + ng :]
        hall, gall, x_ref, gs_ref, cs_ref, hot_ref, sems = refs
        i = idx_ref[0]
        copies = []
        for n, ((k, at, rows), ref) in enumerate(zip(h_layout, hp)):
            copies.append(pltpu.make_async_copy(ref, hall.at[k, pl.ds(at, rows)], sems.at[n]))
        for n, ((k, at, rows), ref) in enumerate(zip(g_layout, gp)):
            copies.append(pltpu.make_async_copy(ref, gall.at[k, pl.ds(at, rows)], sems.at[nh + n]))
        for c in copies:
            c.start()
        upper = upper_ones(length)
        for c in copies:
            c.wait()

        def sequence(k, carry):
            h = hall[k]
            prob = router_probs(wr_ref[...], h)
            meta = gall[k, length : length + 16][0:1].astype(F32)
            at = pl.multiple_of(k * CAP, CAP)
            ones = []
            for le in range(2):
                one, weight = route_rows(meta, prob, le, i, upper, length)
                col = jnp.sum(one * weight, axis=1, keepdims=True)
                cs_ref[le, pl.ds(at, CAP), :] = jnp.broadcast_to(col, (CAP, 128))
                ones.append(one.astype(BF16))
            hot = jnp.concatenate(ones, axis=0)
            hot_ref[k] = hot
            picked = nn(hot, h).astype(BF16)
            grads = nn(hot, gall[k, 0:length]).astype(BF16)
            for le in range(2):
                x_ref[le, pl.ds(at, CAP), :] = picked[le * CAP : (le + 1) * CAP]
                gs_ref[le, pl.ds(at, CAP), :] = grads[le * CAP : (le + 1) * CAP]
            return carry

        lax.fori_loop(0, 8, sequence, 0)

    return pl.pallas_call(
        kernel,
        out_shape=(
            sds((8, length, width), BF16),
            sds((8, ext, width), BF16),
            sds((2, slots, width), BF16),
            sds((2, slots, width), BF16),
            sds((2, slots, 128), F32),
            sds((8, 2 * CAP, length), BF16),
        ),
        in_specs=[SMEM_SPEC, VMEM_SPEC] + [ANY_SPEC] * (nh + ng),
        out_specs=(VMEM_SPEC,) * 6,
        scratch_shapes=[pltpu.SemaphoreType.DMA((nh + ng,))],
        compiler_params=params(24),
        cost_estimate=cost(8 * 4 * 2 * CAP * length * width, 16 << 20),
        name="dispatch_plane",
    )(idx, router_t, *[p for _, _, p in h_pieces], *[p for _, _, p in g_pieces])


def dispatch_others(idx, router_t, h_pieces, g_pieces, length, width, planes):
    h_layout, g_layout = layout_of(h_pieces), layout_of(g_pieces)
    nh, ng = len(h_layout), len(g_layout)
    slots = 8 * planes * CAP
    ext = length + 16

    def kernel(idx_ref, wr_ref, *refs):
        hp, gp, refs = refs[:nh], refs[nh : nh + ng], refs[nh + ng :]
        x_ref, dy_ref, hall, gall, hsems, gsems = refs
        i = idx_ref[0]

        def copies(k, slot):
            out = []
            for n, ((kk, at, rows), ref) in enumerate(zip(h_layout, hp)):
                if kk == k:
                    out.append(
                        pltpu.make_async_copy(ref, hall.at[slot, pl.ds(at, rows)], hsems.at[n])
                    )
            for n, ((kk, at, rows), ref) in enumerate(zip(g_layout, gp)):
                if kk == k:
                    out.append(
                        pltpu.make_async_copy(ref, gall.at[slot, pl.ds(at, rows)], gsems.at[n])
                    )
            return out

        upper = upper_ones(length)
        flight = copies(0, 0)
        for c in flight:
            c.start()
        for k in range(8):
            slot = k % 2
            for c in flight:
                c.wait()
            if k < 7:
                flight = copies(k + 1, 1 - slot)
                for c in flight:
                    c.start()

            def sequence(s, carry):
                h = hall[slot, pl.ds(pl.multiple_of(s * length, length), length)]
                base = pl.multiple_of(s * ext, 16)
                g = gall[slot, pl.ds(base, length)]
                meta = gall[slot, pl.ds(pl.multiple_of(base + length, 16), 16)][0:1].astype(F32)
                prob = router_probs(wr_ref[...], h)
                at = pl.multiple_of((k * planes + s) * CAP, CAP)
                ones, cols = [], []
                for le in range(2):
                    one, weight = route_rows(meta, prob, le, i, upper, length)
                    cols.append(jnp.sum(one * weight, axis=1, keepdims=True))
                    ones.append(one.astype(BF16))
                hot = jnp.concatenate(ones, axis=0)
                picked = nn(hot, h).astype(BF16)
                grads = (nn(hot, g) * jnp.concatenate(cols, axis=0)).astype(BF16)
                for le in range(2):
                    x_ref[le, pl.ds(at, CAP), :] = picked[le * CAP : (le + 1) * CAP]
                    dy_ref[le, pl.ds(at, CAP), :] = grads[le * CAP : (le + 1) * CAP]
                return carry

            lax.fori_loop(0, planes, sequence, 0)

    return pl.pallas_call(
        kernel,
        out_shape=(sds((2, slots, width), BF16), sds((2, slots, width), BF16)),
        in_specs=[SMEM_SPEC, VMEM_SPEC] + [ANY_SPEC] * (nh + ng),
        out_specs=(VMEM_SPEC,) * 2,
        scratch_shapes=[
            pltpu.VMEM((2, planes * length, width), BF16),
            pltpu.VMEM((2, planes * ext, width), BF16),
            pltpu.SemaphoreType.DMA((nh,)),
            pltpu.SemaphoreType.DMA((ng,)),
        ],
        compiler_params=params(32),
        cost_estimate=cost(8 * planes * 4 * 2 * CAP * length * width, 28 << 20),
        name="dispatch_others",
    )(idx, router_t, *[p for _, _, p in h_pieces], *[p for _, _, p in g_pieces])


def experts(x, gs, cs, w_gate, w_up, w_down):
    local, slots, width = x.shape
    hidden = w_gate.shape[2]
    fc = 512
    steps = hidden // fc

    def kernel(x_ref, gs_ref, cs_ref, wg_ref, wu_ref, wd_ref,
               a_ref, dg_ref, du_ref, dy_ref, yc_ref, dr_ref, dc_ref, yacc, dracc):
        f = pl.program_id(1)

        @pl.when(f == 0)
        def _():
            weight = cs_ref[0][:, 0:1]
            dy_ref[0] = (weight * gs_ref[0].astype(F32)).astype(BF16)
            yacc[...] = jnp.zeros_like(yacc)
            dracc[...] = jnp.zeros_like(dracc)

        rows, dy = x_ref[0], dy_ref[0]
        wg, wu, wd = wg_ref[0], wu_ref[0], wd_ref[0]
        g = nn(rows, wg)
        u = nn(rows, wu)
        da = nt(dy, wd)
        silu, slope = silu_parts(g)
        a = (silu * u).astype(BF16)
        dg = (da * u * slope).astype(BF16)
        du = (da * silu).astype(BF16)
        a_ref[0] = a
        dg_ref[0] = dg
        du_ref[0] = du
        yacc[...] += nn(a, wd)
        dracc[...] += nt(dg, wg) + nt(du, wu)

        @pl.when(f == steps - 1)
        def _():
            y = yacc[...].astype(BF16).astype(F32)
            weight = cs_ref[0][:, 0:1]
            yc_ref[0] = (weight * y).astype(BF16)
            dr_ref[0] = dracc[...].astype(BF16)
            dc = jnp.sum(gs_ref[0].astype(F32) * y, axis=1, keepdims=True)
            dc_ref[0] = jnp.broadcast_to(dc, (slots, 128))

    def per_expert(block):
        return pl.BlockSpec((1,) + block, lambda e, f: (e, 0, 0))

    chunk = pl.BlockSpec((1, slots, fc), lambda e, f: (e, 0, f))
    wide = sds((local, slots, hidden), BF16)
    row = sds((local, slots, width), BF16)
    return pl.pallas_call(
        kernel,
        grid=(local, steps),
        out_shape=(wide, wide, wide, row, row, row, sds((local, slots, 128), F32)),
        in_specs=[
            per_expert((slots, width)),
            per_expert((slots, width)),
            per_expert((slots, 128)),
            pl.BlockSpec((1, width, fc), lambda e, f: (e, 0, f)),
            pl.BlockSpec((1, width, fc), lambda e, f: (e, 0, f)),
            pl.BlockSpec((1, fc, width), lambda e, f: (e, f, 0)),
        ],
        out_specs=(
            chunk, chunk, chunk,
            per_expert((slots, width)), per_expert((slots, width)), per_expert((slots, width)),
            per_expert((slots, 128)),
        ),
        scratch_shapes=[pltpu.VMEM((slots, width), F32), pltpu.VMEM((slots, width), F32)],
        compiler_params=params(48, ("arbitrary", "arbitrary")),
        cost_estimate=cost(12 * local * slots * width * hidden, 40 << 20),
        name="experts",
    )(x, gs, cs, w_gate, w_up, w_down)


def combine(idx, hall, gall, hot, yc, dr, dc, shared, down):
    _, length, width = hall.shape
    ext = gall.shape[1]
    part = down.shape[0]
    step = width // 8

    def order(g):
        return jnp.where(g < 4, 2 * g + 1, 2 * (g - 4))

    def kernel(idx_ref, h_ref, g_ref, hot_ref, yc_ref, dr_ref, dc_ref, ws_ref, wd_ref,
               oo_ref, oe_ref, do_ref, de_ref, po_ref, pe_ref, gd_ref, gs_ref, gdacc, gsacc):
        s = pl.program_id(0)
        i = idx_ref[0]

        @pl.when(s == 0)
        def _():
            gdacc[...] = jnp.zeros_like(gdacc)
            gsacc[...] = jnp.zeros_like(gsacc)

        h, grad = h_ref[0], g_ref[0][:length]
        wsg, wsu, wd = ws_ref[:, :part], ws_ref[:, part : 2 * part], wd_ref[...]
        gate = nn(h, wsg)
        up = nn(h, wsu)
        da = nt(grad, wd)
        silu, slope = silu_parts(gate)
        a = (silu * up).astype(BF16)
        dg = (da * up * slope).astype(BF16)
        du = (da * silu).astype(BF16)
        both = jnp.concatenate([dg, du], axis=1)
        gdacc[...] += tn(a, grad)
        gsacc[...] += tn(h, both)
        one = hot_ref[0]
        out = (nn(a, wd) + tn(one, yc_ref[...].reshape(2 * CAP, width))).astype(BF16)
        dh = nt(dg, wsg) + nt(du, wsu) + tn(one, dr_ref[...].reshape(2 * CAP, width))
        dh = dh.astype(BF16)
        dcv = dc_ref[...].reshape(2 * CAP, 128)[:, 0:1] * one.astype(F32)
        expert = lax.broadcasted_iota(jnp.int32, (16, length), 0)
        dp = jnp.zeros((16, length), F32)
        for le in range(2):
            row = jnp.sum(dcv[le * CAP : (le + 1) * CAP], axis=0, keepdims=True)
            dp = dp + jnp.where(expert == 2 * i + le, row, 0.0)

        @pl.when(s < 4)
        def _():
            oo_ref[0] = out
            do_ref[0] = dh
            po_ref[0] = dp

        @pl.when(s >= 4)
        def _():
            oe_ref[0] = out
            de_ref[0] = dh
            pe_ref[0] = dp

        @pl.when(s == 7)
        def _():
            gd_ref[...] = gdacc[...].astype(BF16)
            for k in range(8):
                start = pl.multiple_of((i ^ k) * step, 8)
                gs_ref[k] = gsacc[pl.ds(start, step), :].astype(BF16)

    def odd(block):
        return pl.BlockSpec((1,) + block, lambda g: (jnp.minimum(g, 3), 0, 0))

    def even(block):
        return pl.BlockSpec((1,) + block, lambda g: (jnp.maximum(g - 4, 0), 0, 0))

    def whole(shape):
        return pl.BlockSpec(shape, lambda g: (0,) * len(shape))

    slot_spec = pl.BlockSpec((2, CAP, width), lambda g: (0, order(g), 0))
    rows4 = sds((4, length, width), BF16)
    prob4 = sds((4, 16, length), F32)
    return pl.pallas_call(
        kernel,
        grid=(8,),
        out_shape=(
            rows4, rows4, rows4, rows4, prob4, prob4,
            sds((part, width), BF16),
            sds((8, step, 2 * part), BF16),
        ),
        in_specs=[
            SMEM_SPEC,
            pl.BlockSpec((1, length, width), lambda g: (order(g), 0, 0)),
            pl.BlockSpec((1, ext, width), lambda g: (order(g), 0, 0)),
            pl.BlockSpec((1, 2 * CAP, length), lambda g: (order(g), 0, 0)),
            slot_spec,
            slot_spec,
            pl.BlockSpec((2, CAP, 128), lambda g: (0, order(g), 0)),
            whole((width, 2 * part)),
            whole((part, width)),
        ],
        out_specs=(
            odd((length, width)), even((length, width)),
            odd((length, width)), even((length, width)),
            odd((16, length)), even((16, length)),
            whole((part, width)), whole((8, step, 2 * part)),
        ),
        scratch_shapes=[pltpu.VMEM((part, width), F32), pltpu.VMEM((width, 2 * part), F32)],
        compiler_params=params(40, ("arbitrary",)),
        cost_estimate=cost(22 * 8 * length * width * part, 24 << 20),
        name="combine",
    )(idx, hall, gall, hot, yc, dr, dc, shared, down)


def attention_backward(idx, tokens, grad, live_row, gain1, gain2, saved, router_t, dh_parts,
                       dp_parts, pieces):
    layout = layout_of(pieces)
    n = len(layout)
    length, width = tokens.shape
    step = width // 8
    cosine, sine = rope_tables(length)
    h1, q, k, v, o, prob, x1, h2 = saved
    total = 4 * width + 128

    def kernel(idx_ref, x_ref, g_ref, lv_ref, g1_ref, g2_ref, cos_ref, sin_ref, h1_ref, q_ref,
               k_ref, v_ref, o_ref, p_ref, x1_ref, h2_ref, wr_ref, d0, d1, d2, d3, p0, p1, p2, p3,
               *refs):
        piece_refs, refs = refs[:n], refs[n:]
        gt_ref, odd_ref, even_ref, wbuf, dmix, dqkv, gbuf, sems = refs
        i = idx_ref[0]
        copies = place_copies(i, layout, step, piece_refs, wbuf, sems)
        for c in copies:
            c.start()
        x1v = x1_ref[...]
        r2 = norm_scale(x1v)
        wr = wr_ref[...]
        pr = router_probs(wr, h2_ref[...])
        dp = (p0[...] + p1[...] + p2[...] + p3[...]) * lv_ref[...]
        dl = (pr * (dp - jnp.sum(pr * dp, axis=0, keepdims=True))).astype(BF16)
        router_grad = nn(dl, h2_ref[...])
        dh2 = d0[...].astype(F32) + d1[...].astype(F32) + d2[...].astype(F32) + d3[...].astype(F32)
        dh2 = dh2 + tn(dl, wr)
        gain2_grad = jnp.sum(dh2 * x1v * r2, axis=0, keepdims=True)
        weighted = dh2 * g2_ref[...]
        inner = jnp.mean(x1v * weighted, axis=-1, keepdims=True)
        dx1 = g_ref[...].astype(F32) + r2 * weighted - x1v * (r2 * r2 * r2) * inner
        da = dx1.astype(BF16)
        for c in copies:
            c.wait()
        gbuf[:, 3 * width : 4 * width] = tn(o_ref[...], da).astype(BF16)
        dmix[...] = nt(da, wbuf[:, 3 * width :]).astype(BF16)
        first = lax.broadcasted_iota(jnp.int32, (length, 128), 1) < HEAD_DIM

        def pair(hp, carry):
            at = pl.multiple_of(hp * 128, 128)
            qv, kv, vv = (ref[:, pl.ds(at, 128)] for ref in (q_ref, k_ref, v_ref))
            dov = dmix[:, pl.ds(at, 128)]
            zero = jnp.zeros_like(qv)
            dq = jnp.zeros((length, 128), F32)
            dk = jnp.zeros((length, 128), F32)
            dv = jnp.zeros((length, 128), F32)
            for h in range(2):
                mine = first if h == 0 else jnp.logical_not(first)
                p = p_ref[2 * hp + h]
                dom = jnp.where(mine, dov, zero)
                dp = nt(dom, vv)
                dv = dv + tn(p.astype(BF16), dom)
                ds = p * (dp - jnp.sum(p * dp, axis=-1, keepdims=True))
                ds = (ds * SCALE).astype(BF16)
                dq = dq + nn(ds, jnp.where(mine, kv, zero))
                dk = dk + tn(ds, jnp.where(mine, qv, zero))
            cosv, sinv = cos_ref[...], sin_ref[...]
            dqkv[:, pl.ds(at, 128)] = (dq * cosv - half_swap(dq) * sinv).astype(BF16)
            dqkv[:, pl.ds(at + width, 128)] = (dk * cosv - half_swap(dk) * sinv).astype(BF16)
            dqkv[:, pl.ds(at + 2 * width, 128)] = dv.astype(BF16)
            return carry

        lax.fori_loop(0, HEADS // 2, pair, 0)
        gbuf[:, : 3 * width] = tn(h1_ref[...], dqkv[...]).astype(BF16)
        dh1 = nt(dqkv[...], wbuf[:, : 3 * width])
        x = x_ref[...].astype(F32)
        r1 = norm_scale(x)
        gain1_grad = jnp.sum(dh1 * x * r1, axis=0, keepdims=True)
        weighted = dh1 * g1_ref[...]
        inner = jnp.mean(x * weighted, axis=-1, keepdims=True)
        gt_ref[...] = (dx1 + r1 * weighted - x * (r1 * r1 * r1) * inner).astype(BF16)
        small = jnp.concatenate(
            [router_grad, gain1_grad, gain2_grad, jnp.zeros((110, width), F32)], axis=0
        )
        gbuf[:, 4 * width :] = small.T.astype(BF16)
        for kk in range(8):
            rows = gbuf[pl.ds(pl.multiple_of((i ^ kk) * step, 16), step), :]
            if kk % 2:
                odd_ref[kk // 2] = rows
            else:
                even_ref[kk // 2] = rows

    blocks = sds((4, step, total), BF16)
    return pl.pallas_call(
        kernel,
        out_shape=(sds((length, width), BF16), blocks, blocks),
        in_specs=[SMEM_SPEC] + [VMEM_SPEC] * 24 + [ANY_SPEC] * n,
        out_specs=(VMEM_SPEC,) * 3,
        scratch_shapes=[
            pltpu.VMEM((width, 4 * width), BF16),
            pltpu.VMEM((length, width), BF16),
            pltpu.VMEM((length, 3 * width), BF16),
            pltpu.VMEM((width, total), BF16),
            pltpu.SemaphoreType.DMA((n,)),
        ],
        compiler_params=params(44),
        cost_estimate=cost(20 * length * width * width, 24 << 20),
        name="attention_backward",
    )(idx, tokens, grad, live_row, gain1, gain2, cosine, sine, h1, q, k, v, o, prob, x1, h2,
      router_t, *dh_parts, *dp_parts, *[p for _, _, p in pieces])


def expert_grads(idx, own, others, w_gate, w_up, w_down):
    a, dg, du, dy, xd = own
    x_o, dy_o, xd_o = others
    local, slots, hidden = a.shape
    many = x_o.shape[1]
    width = x_o.shape[2]
    piece = xd.shape[2]
    fc = 512
    steps = hidden // fc
    tile = 512

    def kernel(idx_ref, a_ref, dg_ref, du_ref, dy_ref, xd_ref, xo_ref, dyo_ref, xdo_ref,
               wg_ref, wu_ref, wd_ref, gg_ref, gu_ref, gd_ref, ao, dgo, duo):
        f = pl.program_id(1)
        wg, wu, wd = wg_ref[0], wu_ref[0], wd_ref[0]

        def rows(t, carry):
            at = pl.ds(pl.multiple_of(t * tile, tile), tile)
            g = nn(xo_ref[0, at], wg)
            u = nn(xo_ref[0, at], wu)
            da = nt(dyo_ref[0, at], wd)
            silu, slope = silu_parts(g)
            ao[at] = (silu * u).astype(BF16)
            dgo[at] = (da * u * slope).astype(BF16)
            duo[at] = (da * silu).astype(BF16)
            return carry

        lax.fori_loop(0, many // tile, rows, 0)
        gg_ref[0] = tn(xdo_ref[0], dgo[...]) + tn(xd_ref[0], dg_ref[0])
        gu_ref[0] = tn(xdo_ref[0], duo[...]) + tn(xd_ref[0], du_ref[0])

        @pl.when(f == idx_ref[1])
        def _():
            gd_ref[0] = tn(ao[...], dyo_ref[0]) + tn(a_ref[0], dy_ref[0])

    def per_expert(block):
        return pl.BlockSpec((1,) + block, lambda e, f, i: (e, 0, 0))

    def chunk(rows):
        return pl.BlockSpec((1, rows, fc), lambda e, f, i: (e, 0, f))

    return pl.pallas_call(
        kernel,
        out_shape=(
            sds((local, piece, hidden), F32),
            sds((local, piece, hidden), F32),
            sds((local, fc, width), F32),
        ),
        grid_spec=pltpu.PrefetchScalarGridSpec(
            num_scalar_prefetch=1,
            grid=(local, steps),
            in_specs=[
                pl.BlockSpec((1, slots, fc), lambda e, f, i: (e, 0, i[1])),
                chunk(slots),
                chunk(slots),
                per_expert((slots, width)),
                per_expert((slots, piece)),
                per_expert((many, width)),
                per_expert((many, width)),
                per_expert((many, piece)),
                chunk(width),
                chunk(width),
                pl.BlockSpec((1, fc, width), lambda e, f, i: (e, f, 0)),
            ],
            out_specs=(chunk(piece), chunk(piece), per_expert((fc, width))),
            scratch_shapes=[pltpu.VMEM((many, fc), BF16) for _ in range(3)],
        ),
        compiler_params=params(56, ("arbitrary", "arbitrary")),
        cost_estimate=cost(local * hidden * width * (6 * many + 2 * (many + slots)), 60 << 20),
        name="expert_grads",
    )(idx, a, dg, du, dy, xd, x_o, dy_o, xd_o, w_gate, w_up, w_down)


def finish_shared(order, sides, downs):
    step, part = sides[0].shape[1], sides[0].shape[2] // 2
    rows, width = downs[0].shape

    def kernel(order_ref, s0, s1, s2, s3, d0, d1, d2, d3, gate_ref, up_ref, down_ref):
        i, z = order_ref[0], order_ref[1]
        for r, (s, d) in enumerate(zip((s0, s1, s2, s3), (d0, d1, d2, d3))):
            quarter = (z - r + 4) & 3
            for b in range(2):
                col = pl.multiple_of((i ^ (2 * quarter + b)) * part, part)
                gate_ref[:, pl.ds(col, part)] = s[b, :, :part].astype(F32)
                up_ref[:, pl.ds(col, part)] = s[b, :, part:].astype(F32)
            down_ref[pl.ds(pl.multiple_of(quarter * rows, rows), rows), :] = d[...].astype(F32)

    wide = sds((step, 8 * part), F32)
    return pl.pallas_call(
        kernel,
        out_shape=(wide, wide, sds((4 * rows, width), F32)),
        in_specs=[SMEM_SPEC] + [VMEM_SPEC] * 8,
        out_specs=(VMEM_SPEC,) * 3,
        compiler_params=params(12),
        name="finish_shared",
    )(order, *sides, *downs)


def finish_attention(order, parts, smalls):
    rows, width = parts[0].shape

    def kernel(order_ref, s0, s1, s2, s3, m0, m1, m2, m3, q_ref, k_ref, v_ref, o_ref, m_ref):
        z = order_ref[1]
        for r, s in enumerate((s0, s1, s2, s3)):
            for m, ref in enumerate((q_ref, k_ref, v_ref, o_ref)):

                @pl.when(((z - r + 4) & 3) == m)
                def _(ref=ref, s=s):
                    ref[...] = s[...].astype(F32)

        m_ref[...] = m0[...] + m1[...] + m2[...] + m3[...]

    flat = sds((rows, width), F32)
    return pl.pallas_call(
        kernel,
        out_shape=(flat, flat, flat, flat, sds((rows, 128), F32)),
        in_specs=[SMEM_SPEC] + [VMEM_SPEC] * 8,
        out_specs=(VMEM_SPEC,) * 5,
        compiler_params=params(8),
        name="finish_attention",
    )(order, *parts, *smalls)


def on_device(
    tokens,
    segment_ids,
    padding,
    routes,
    w_query,
    w_key,
    w_value,
    w_out,
    w_router,
    shared_gate,
    shared_up,
    shared_down,
    gain_attn,
    gain_ffn,
    expert_gate,
    expert_up,
    expert_down,
    cotangent,
):
    length, width = tokens.shape
    planes = lax.axis_size("dp")
    i = lax.axis_index("expert").astype(jnp.int32)
    z = lax.axis_index("dp").astype(jnp.int32)
    idx = jnp.stack([i, z])
    step = width // 8
    part = shared_down.shape[0]
    spread = planes == 4

    attn_shard = jnp.concatenate([w_query, w_key, w_value, w_out], axis=1).astype(BF16)
    attn_pieces = plane_gather(attn_shard)

    live_row = padding.astype(F32)
    meta = jnp.concatenate([routes[:, 0], routes[:, 1], padding[0]]).astype(BF16)[None, :]
    grad_ext = jnp.concatenate(
        [cotangent, meta, jnp.zeros((15, width), BF16)], axis=0
    )
    g_pieces = plane_gather(grad_ext)

    router_pad = jnp.pad(w_router, ((0, 0), (0, 128 - w_router.shape[1]))).astype(BF16)
    side = jnp.concatenate([shared_gate, shared_up], axis=1).astype(BF16)
    shared_pieces = []
    for k in range(8):
        col = (i ^ k) * part
        mine = jnp.concatenate(
            [
                lax.dynamic_slice_in_dim(side, col, part, 1),
                lax.dynamic_slice_in_dim(side, col + 8 * part, part, 1),
                router_pad,
            ],
            axis=1,
        )
        shared_pieces.append((k, 0, swap(mine, k) if k else mine))
    shared_all = assemble(idx, shared_pieces, step)
    router_t = shared_all[:, 2 * part :].T[:16]
    shared_w = shared_all[:, : 2 * part]
    down_w = shared_down.astype(BF16)

    gain1, gain2 = gain_attn[None, :], gain_ffn[None, :]
    saved = attention_forward(
        idx, tokens, segment_ids, segment_ids.reshape(length, 1), live_row, gain1, gain2,
        attn_pieces,
    )
    x1, h2 = saved[6], saved[7]

    h_pieces = plane_gather(h2)
    hall, gall, x_own, gs_own, cs_own, hot = dispatch_plane(
        idx, router_t, h_pieces, g_pieces, length, width
    )
    a, dg, du, dy, yc, dr, dc = experts(x_own, gs_own, cs_own, expert_gate, expert_up, expert_down)
    out_odd, out_even, dh_odd, dh_even, dp_odd, dp_even, gsd, gside = combine(
        idx, hall, gall, hot, yc, dr, dc, shared_w, down_w
    )
    dp_parts = plane_scatter(dp_odd, dp_even)
    dh_parts = plane_scatter(dh_odd, dh_even)
    grad_tokens, att_odd, att_even = attention_backward(
        idx, tokens, cotangent, live_row, gain1, gain2, saved, router_t, dh_parts, dp_parts,
        attn_pieces,
    )

    out_parts = plane_scatter(out_odd, out_even)
    output = (x1 + sum(p.astype(F32) for p in out_parts)).astype(BF16)

    att_parts = plane_scatter(att_odd, att_even)
    att = sum(p.astype(F32) for p in att_parts)
    att_low = att[:, : 4 * width].astype(BF16)
    quarters = jnp.stack([att_low[:, m * width : (m + 1) * width] for m in range(4)])
    att_quarters, att_z = dp_sum(quarters)
    small = att[:, 4 * width :]
    if spread:
        smalls = [small] + [shift(small, k) for k in (1, 2, 3)]
    else:
        nil = jnp.zeros_like(small)
        smalls = [lax.psum(small, "dp"), nil, nil, nil]
    gq, gk, gv, go, small = finish_attention(jnp.stack([i, att_z]), att_quarters, smalls)

    gside = jnp.stack([gside[0]] + [swap(gside[k], k) for k in range(1, 8)])
    side_quarters, side_z = dp_sum(gside.reshape(4, 2, step, 2 * part))
    down_quarters, _ = dp_sum(gsd.reshape(4, part // 4, width))
    g_sgate, g_sup, g_sdown = finish_shared(
        jnp.stack([i, side_z]), side_quarters, down_quarters
    )

    if spread:
        h_far = jnp.concatenate([shift(h2, k) for k in (1, 2, 3)], axis=0)
        g_far = jnp.concatenate([shift(grad_ext, k) for k in (1, 2, 3)], axis=0)
        x_far, dy_far = dispatch_others(
            idx, router_t, plane_gather(h_far), plane_gather(g_far), length, width, 3
        )
        rows = width // 4
        xd = lax.dynamic_slice_in_dim(x_own, z * rows, rows, 2)
        xd_far = lax.dynamic_slice_in_dim(x_far, z * rows, rows, 2)
        g_gate, g_up, g_down = expert_grads(
            idx, (a, dg, du, dy, xd), (x_far, dy_far, xd_far), expert_gate, expert_up, expert_down
        )
    else:

        def scattered(left, right):
            local = jnp.einsum("end,enf->edf", left, right, preferred_element_type=F32)
            return lax.psum_scatter(
                local.astype(BF16), "dp", scatter_dimension=1, tiled=True
            ).astype(F32)

        g_gate, g_up, g_down = scattered(x_own, dg), scattered(x_own, du), scattered(a, dy)

    experts_all = w_router.shape[1]
    return (
        output,
        grad_tokens,
        gq,
        gk,
        gv,
        go,
        small[:, :experts_all],
        g_sgate,
        g_sup,
        g_sdown,
        small[:, experts_all],
        small[:, experts_all + 1],
        g_gate,
        g_up,
        g_down,
    )


def solution(mesh):
    both = P(("dp", "expert"), None)
    one = P("expert", None)
    three = P("expert", None, None)
    sliced = P("expert", "dp", None)
    return jax.shard_map(
        on_device,
        mesh=mesh,
        in_specs=(both,) * 4 + (one,) * 8 + (P(), P()) + (three,) * 3 + (both,),
        out_specs=(both, both) + (one,) * 8 + (P("expert"), P("expert")) + (sliced,) * 3,
        check_vma=False,
    )
```

```python
import numpy as np

import jax
import jax.numpy as jnp
from jax import lax
from jax.experimental import pallas as pl
from jax.experimental.pallas import tpu as pltpu
from jax.sharding import PartitionSpec as P

HEADS = 12
HEAD_DIM = 64
CAP = 64
EPS = 1e-06
ROPE_BASE = 10000.0
MASKED = -1e30
SCALE = HEAD_DIM**-0.5
F32 = jnp.float32
BF16 = jnp.bfloat16
MIB = 1 << 20
VMEM_SPEC = pl.BlockSpec(memory_space=pltpu.VMEM)
SMEM_SPEC = pl.BlockSpec(memory_space=pltpu.SMEM)
ANY_SPEC = pl.BlockSpec(memory_space=pl.ANY)


def nn(a, b):
    return jnp.dot(a, b, preferred_element_type=F32)


def nt(a, b):
    return lax.dot_general(a, b, (((1,), (1,)), ((), ())), preferred_element_type=F32)


def tn(a, b):
    return lax.dot_general(a, b, (((0,), (0,)), ((), ())), preferred_element_type=F32)


def sds(shape, dtype):
    return jax.ShapeDtypeStruct(shape, dtype)


def cost(flops, nbytes):
    return pl.CostEstimate(
        flops=int(flops * 0.02), bytes_accessed=int(nbytes * 0.02), transcendentals=0
    )


def params(mib, semantics=None):
    return pltpu.CompilerParams(vmem_limit_bytes=mib * MIB, dimension_semantics=semantics)


def swap(x, k):
    n = lax.axis_size("expert")
    return lax.ppermute(x, "expert", [(j, j ^ k) for j in range(n)])


def shift(x, k):
    n = lax.axis_size("dp")
    return lax.ppermute(x, "dp", [(j, (j + k) % n) for j in range(n)])


def after(value, *first):
    return lax.optimization_barrier((value, first))[0]


def relay_gather(x):
    half = x.shape[0] // 32 * 16
    a, b = swap(x, 2), swap(x, 4)
    d0, d1 = swap(a[:half], 4), swap(b[half:], 2)
    near = [(0, 0, x), (2, 0, a), (4, 0, b), (6, 0, d0), (6, half, d1)]
    return near + [(k + 1, at, swap(piece, 1)) for k, at, piece in near]


def same_core():
    n = lax.axis_size("expert")
    return [list(range(c, n, 2)) for c in range(2)]


def chips_exchange(blocks):
    return lax.all_to_all(
        blocks, "expert", split_axis=0, concat_axis=0, tiled=True, axis_index_groups=same_core()
    )


def both_cores(near):
    other = [swap(p, 1) for p in near]
    return [p for pair in zip(near, other) for p in pair]


def plane_near(even, came):
    return [add([even[j], came[j]]).astype(even.dtype) for j in range(4)]


def plane_far(sums):
    return [sums[0], swap(sums[1], 2), swap(sums[2], 4), swap(sums[3], 6)]


def dp_scatter(quarters):
    z = lax.axis_index("dp")
    parts = [lax.dynamic_index_in_dim(quarters, (z + k) % 4, 0, False) for k in range(4)]
    return [parts[0]] + [shift(parts[k], k) for k in (1, 2, 3)]


def dp_spread(parts):
    total = add(parts).astype(parts[0].dtype)
    return [total] + [shift(total, k) for k in (1, 2, 3)]


def dp_whole(quarters):
    whole = lax.psum(quarters, "dp")
    return [whole[0], whole[3], whole[2], whole[1]]


def add(parts):
    total = parts[0].astype(F32)
    for p in parts[1:]:
        total = total + p.astype(F32)
    return total


def norm_scale(values):
    return lax.rsqrt(jnp.mean(values * values, axis=-1, keepdims=True) + EPS)


def silu_parts(gate):
    logistic = 1.0 / (1.0 + jnp.exp(-gate))
    return gate * logistic, logistic * (1.0 + gate * (1.0 - logistic))


def half_swap(x):
    lane = lax.broadcasted_iota(jnp.int32, x.shape, 1)
    half = HEAD_DIM // 2
    return jnp.where(
        lane % HEAD_DIM < half, pltpu.roll(x, x.shape[1] - half, 1), pltpu.roll(x, half, 1)
    )


def place_copies(i, layout, step, refs, target, sems):
    copies = []
    for n, ((k, at, rows), ref) in enumerate(zip(layout, refs)):
        start = pl.multiple_of((i ^ k) * step + at, 16)
        copies.append(pltpu.make_async_copy(ref, target.at[pl.ds(start, rows), :], sems.at[n]))
    return copies


def layout_of(pieces):
    return tuple((k, at, piece.shape[0]) for k, at, piece in pieces)


def rope_tables(length):
    half = HEAD_DIM // 2
    frequency = (ROPE_BASE ** (-(2.0 * np.arange(half, dtype=np.float32)) / HEAD_DIM)).astype(
        np.float32
    )
    angles = (np.arange(length, dtype=np.float32)[:, None] * frequency[None, :]).astype(np.float32)
    cosine, sine = np.cos(angles), np.sin(angles)
    return (
        np.concatenate([cosine] * 4, 1).astype(np.float32),
        np.concatenate([-sine, sine, -sine, sine], 1).astype(np.float32),
    )


def assemble(idx, pieces, step):
    layout = layout_of(pieces)
    width = pieces[0][2].shape[1]
    rows = step * 8

    def kernel(idx_ref, *refs):
        n = len(layout)
        copies = place_copies(idx_ref[0], layout, step, refs[:n], refs[n], refs[n + 1])
        for c in copies:
            c.start()
        for c in copies:
            c.wait()

    return pl.pallas_call(
        kernel,
        out_shape=sds((rows, width), pieces[0][2].dtype),
        in_specs=[SMEM_SPEC] + [ANY_SPEC] * len(layout),
        out_specs=VMEM_SPEC,
        scratch_shapes=[pltpu.SemaphoreType.DMA((len(layout),))],
        compiler_params=params(8),
        name="assemble",
    )(idx, *[p for _, _, p in pieces])


def attention_forward(idx, tokens, seg_row, live_row, gain1, gain2, pieces):
    layout = layout_of(pieces)
    n = len(layout)
    length, width = tokens.shape
    step = width // 8
    cosine, sine = rope_tables(length)

    def kernel(idx_ref, x_ref, sr_ref, lv_ref, g1_ref, g2_ref, cos_ref, sin_ref, *refs):
        piece_refs, refs = refs[:n], refs[n:]
        h1_ref, q_ref, k_ref, v_ref, o_ref, p_ref, x1_ref, h2_ref, wr_ref, h4_ref = refs[:10]
        wbuf, pre, sems = refs[10:]
        copies = place_copies(idx_ref[0], layout, step, piece_refs, wbuf, sems)
        for c in copies:
            c.start()
        x = x_ref[...].astype(F32)
        h1 = (x * norm_scale(x) * g1_ref[...]).astype(BF16)
        h1_ref[...] = h1
        row = lax.broadcasted_iota(jnp.int32, (length, length), 0)
        col = lax.broadcasted_iota(jnp.int32, (length, length), 1)
        seg = sr_ref[...].astype(F32)
        seg_col = jnp.broadcast_to(seg, (8, length)).T[:, 0:1]
        allowed = (col == row) | ((col <= row) & (seg == seg_col) & (lv_ref[...] > 0.0))
        bias = jnp.where(allowed, 0.0, MASKED)
        for c in copies:
            c.wait()
        pre[...] = nn(h1, wbuf[:, : 3 * width])
        first = lax.broadcasted_iota(jnp.int32, (length, 128), 1) < HEAD_DIM

        def pair(hp, carry):
            at = pl.multiple_of(hp * 128, 128)
            qp = pre[:, pl.ds(at, 128)]
            kp = pre[:, pl.ds(at + width, 128)]
            v = pre[:, pl.ds(at + 2 * width, 128)].astype(BF16)
            cosv, sinv = cos_ref[...], sin_ref[...]
            q = (qp * cosv + half_swap(qp) * sinv).astype(BF16)
            k = (kp * cosv + half_swap(kp) * sinv).astype(BF16)
            q_ref[:, pl.ds(at, 128)] = q
            k_ref[:, pl.ds(at, 128)] = k
            v_ref[:, pl.ds(at, 128)] = v
            mixed = jnp.zeros((length, 128), F32)
            zero = jnp.zeros_like(q)
            for h in range(2):
                mine = first if h == 0 else jnp.logical_not(first)
                s = nt(jnp.where(mine, q, zero), k) * SCALE + bias
                e = jnp.exp(s - jnp.max(s, axis=-1, keepdims=True))
                p = e / jnp.sum(e, axis=-1, keepdims=True)
                p_ref[2 * hp + h] = p
                mixed = mixed + nn(p.astype(BF16), jnp.where(mine, v, zero))
            o_ref[:, pl.ds(at, 128)] = mixed.astype(BF16)
            return carry

        lax.fori_loop(0, HEADS // 2, pair, 0)
        x1 = x + nn(o_ref[...], wbuf[:, 3 * width : 4 * width])
        x1_ref[...] = x1
        h2 = (x1 * norm_scale(x1) * g2_ref[...]).astype(BF16)
        h2_ref[...] = h2
        for chip in range(4):
            h4_ref[chip] = h2
        wr_ref[...] = wbuf[:, 4 * width :].astype(F32).T[:16].astype(BF16)

    flat = sds((length, width), BF16)
    return pl.pallas_call(
        kernel,
        out_shape=(
            flat, flat, flat, flat, flat,
            sds((HEADS, length, length), F32),
            sds((length, width), F32),
            flat,
            sds((16, width), BF16),
            sds((4, length, width), BF16),
        ),
        in_specs=[SMEM_SPEC] + [VMEM_SPEC] * 7 + [ANY_SPEC] * n,
        out_specs=(VMEM_SPEC,) * 10,
        scratch_shapes=[
            pltpu.VMEM((width, pieces[0][2].shape[1]), BF16),
            pltpu.VMEM((length, 3 * width), F32),
            pltpu.SemaphoreType.DMA((n,)),
        ],
        compiler_params=params(60),
        cost_estimate=cost(8 * length * width * width, 12 << 20),
        name="attention_forward",
    )(idx, tokens, seg_row, live_row, gain1, gain2, cosine, sine,
      *[p for _, _, p in pieces])


def route_rows(meta, prob, le, i, upper, length):
    expert = (2 * i + le).astype(F32)
    hit = (meta[:, :length] == expert) | (meta[:, length : 2 * length] == expert)
    hot = jnp.where(hit, 1.0, 0.0)
    rank = nn(jnp.broadcast_to(hot, (16, length)).astype(BF16), upper)[0:1]
    slot = lax.broadcasted_iota(jnp.int32, (CAP, length), 0).astype(F32) + 1.0
    one = jnp.where((slot == rank) & hit, 1.0, 0.0)
    which = lax.broadcasted_iota(jnp.int32, prob.shape, 0) == 2 * i + le
    weight = jnp.sum(jnp.where(which, prob, 0.0), axis=0, keepdims=True)
    return one, weight * meta[:, 2 * length :]


def router_probs(router_t, rows):
    logits = nt(router_t, rows)
    e = jnp.exp(logits - jnp.max(logits, axis=0, keepdims=True))
    return e / jnp.sum(e, axis=0, keepdims=True)


def upper_ones(length):
    return jnp.where(
        lax.broadcasted_iota(jnp.int32, (length, length), 0)
        <= lax.broadcasted_iota(jnp.int32, (length, length), 1),
        1.0,
        0.0,
    ).astype(BF16)


def dispatch_plane(idx, router_t, rows, grads, piece):
    _, length, width = rows[0].shape
    slots = 8 * CAP
    ext = length + 16

    def kernel(idx_ref, wr_ref, *refs):
        hp, gp, refs = refs[:2], refs[2:4], refs[4:]
        x_ref, xd_ref, gs_ref, cs_ref, hot_ref, hall, gall, sems = refs
        i = idx_ref[0]
        copies = []
        for c in range(2):
            copies.append(pltpu.make_async_copy(hp[c], hall.at[pl.ds(4 * c, 4)], sems.at[c]))
            copies.append(pltpu.make_async_copy(gp[c], gall.at[pl.ds(4 * c, 4)], sems.at[2 + c]))
        for c in copies:
            c.start()
        upper = upper_ones(length)
        turn = (width - idx_ref[1] * piece) % width
        for c in copies:
            c.wait()

        def sequences(pair, carry):
            for k in (2 * pair, 2 * pair + 1):
                h = hall[k]
                prob = router_probs(wr_ref[...], h)
                meta = gall[k, length:ext][0:1].astype(F32)
                at = pl.multiple_of(k * CAP, CAP)
                ones = []
                for le in range(2):
                    one, weight = route_rows(meta, prob, le, i, upper, length)
                    col = jnp.sum(one * weight, axis=1, keepdims=True)
                    cs_ref[le, pl.ds(at, CAP), :] = jnp.broadcast_to(col, (CAP, 128))
                    ones.append(one.astype(BF16))
                hot = jnp.concatenate(ones, axis=0)
                hot_ref[k] = hot
                picked = nn(hot, h)
                cut = pltpu.roll(picked, turn, 1)[:, :piece].astype(BF16)
                picked = picked.astype(BF16)
                grads = nn(hot, gall[k, 0:length]).astype(BF16)
                for le in range(2):
                    mine = slice(le * CAP, (le + 1) * CAP)
                    x_ref[le, pl.ds(at, CAP), :] = picked[mine]
                    xd_ref[le, pl.ds(at, CAP), :] = cut[mine]
                    gs_ref[le, pl.ds(at, CAP), :] = grads[mine]
            return carry

        lax.fori_loop(0, 4, sequences, 0)

    return pl.pallas_call(
        kernel,
        out_shape=(
            sds((2, slots, width), BF16),
            sds((2, slots, piece), BF16),
            sds((2, slots, width), BF16),
            sds((2, slots, 128), F32),
            sds((8, 2 * CAP, length), BF16),
        ),
        in_specs=[SMEM_SPEC, VMEM_SPEC] + [ANY_SPEC] * 4,
        out_specs=(VMEM_SPEC,) * 5,
        scratch_shapes=[
            pltpu.VMEM((8, length, width), BF16),
            pltpu.VMEM((8, ext, width), BF16),
            pltpu.SemaphoreType.DMA((4,)),
        ],
        compiler_params=params(60),
        cost_estimate=cost(8 * 4 * 2 * CAP * length * width, 16 << 20),
        name="dispatch_plane",
    )(idx, router_t, *rows, *grads)


def dispatch_others(idx, router_t, h_pieces, g_pieces, corners, planes, piece):
    width = h_pieces[0].shape[1]
    length = h_pieces[0].shape[0] // planes
    ext = length + 16
    slots = 8 * planes * CAP

    def kernel(idx_ref, wr_ref, *refs):
        hp, gp, both, refs = refs[:6], refs[6:12], refs[12:14], refs[14:]
        x_ref, xd_ref, dy_ref, hall, gall, hsems, gsems = refs
        i = idx_ref[0]

        def copies(k):
            if k < 6:
                yield pltpu.make_async_copy(hp[k], hall.at[k], hsems.at[k, 0])
                yield pltpu.make_async_copy(gp[k], gall.at[k], gsems.at[k, 0])
                return
            for s in range(planes):
                base = s * (ext + length)
                yield pltpu.make_async_copy(
                    both[k - 6].at[pl.ds(base, ext)], gall.at[k, pl.ds(s * ext, ext)], gsems.at[k, s]
                )
                yield pltpu.make_async_copy(
                    both[k - 6].at[pl.ds(base + ext, length)],
                    hall.at[k, pl.ds(s * length, length)],
                    hsems.at[k, s],
                )

        for k in range(8):
            for c in copies(k):
                c.start()
        upper = upper_ones(length)
        turn = (width - idx_ref[1] * piece) % width

        def column(k, carry):
            @pl.when(k < 6)
            def _():
                pltpu.make_async_copy(hall.at[k], hall.at[k], hsems.at[k, 0]).wait()
                pltpu.make_async_copy(gall.at[k], gall.at[k], gsems.at[k, 0]).wait()

            @pl.when(k >= 6)
            def _():
                for s in range(planes):
                    h = hall.at[k, pl.ds(s * length, length)]
                    g = gall.at[k, pl.ds(s * ext, ext)]
                    pltpu.make_async_copy(h, h, hsems.at[k, s]).wait()
                    pltpu.make_async_copy(g, g, gsems.at[k, s]).wait()

            for s in range(planes):
                h = hall[k, s * length : (s + 1) * length]
                g = gall[k, s * ext : s * ext + length]
                meta = gall[k, s * ext + length : (s + 1) * ext][0:1].astype(F32)
                prob = router_probs(wr_ref[...], h)
                ones, cols = [], []
                for le in range(2):
                    one, weight = route_rows(meta, prob, le, i, upper, length)
                    cols.append(jnp.sum(one * weight, axis=1, keepdims=True))
                    ones.append(one.astype(BF16))
                hot = jnp.concatenate(ones, axis=0)
                picked = nn(hot, h)
                cut = pltpu.roll(picked, turn, 1)[:, :piece].astype(BF16)
                picked = picked.astype(BF16)
                dy = (nn(hot, g) * jnp.concatenate(cols, axis=0)).astype(BF16)
                at = pl.ds(pl.multiple_of((k * planes + s) * CAP, CAP), CAP)
                for le in range(2):
                    mine = slice(le * CAP, (le + 1) * CAP)
                    x_ref[le, at] = picked[mine]
                    xd_ref[le, at] = cut[mine]
                    dy_ref[le, at] = dy[mine]
            return carry

        lax.fori_loop(0, 8, column, 0)

    return pl.pallas_call(
        kernel,
        out_shape=(
            sds((2, slots, width), BF16),
            sds((2, slots, piece), BF16),
            sds((2, slots, width), BF16),
        ),
        in_specs=[SMEM_SPEC, VMEM_SPEC] + [ANY_SPEC] * 14,
        out_specs=(VMEM_SPEC,) * 3,
        scratch_shapes=[
            pltpu.VMEM((8, planes * length, width), BF16),
            pltpu.VMEM((8, planes * ext, width), BF16),
            pltpu.SemaphoreType.DMA((8, planes)),
            pltpu.SemaphoreType.DMA((8, planes)),
        ],
        compiler_params=params(60),
        cost_estimate=cost(8 * planes * 4 * 2 * CAP * length * width, 28 << 20),
        name="dispatch_others",
    )(idx, router_t, *h_pieces, *g_pieces, *corners)


def experts(e, x, gs, cs, w_gate, w_up, w_down):
    _, slots, width = x.shape
    hidden = w_gate.shape[2]
    fc = 512
    steps = hidden // fc

    def kernel(x_ref, gs_ref, cs_ref, wg_ref, wu_ref, wd_ref,
               a_ref, dg_ref, du_ref, dy_ref, yc_ref, dr_ref, dc_ref, yacc, dracc):
        f = pl.program_id(0)

        @pl.when(f == 0)
        def _():
            weight = cs_ref[0][:, 0:1]
            dy_ref[...] = (weight * gs_ref[0].astype(F32)).astype(BF16)
            yacc[...] = jnp.zeros_like(yacc)
            dracc[...] = jnp.zeros_like(dracc)

        rows, dy = x_ref[0], dy_ref[...]
        wg, wu, wd = wg_ref[0], wu_ref[0], wd_ref[0]
        g = nn(rows, wg)
        u = nn(rows, wu)
        da = nt(dy, wd)
        silu, slope = silu_parts(g)
        a = (silu * u).astype(BF16)
        dg = (da * u * slope).astype(BF16)
        du = (da * silu).astype(BF16)
        a_ref[...] = a
        dg_ref[...] = dg
        du_ref[...] = du
        yacc[...] += nn(a, wd)
        dracc[...] += nt(dg, wg) + nt(du, wu)

        @pl.when(f == steps - 1)
        def _():
            y = yacc[...].astype(BF16).astype(F32)
            weight = cs_ref[0][:, 0:1]
            yc_ref[...] = (weight * y).astype(BF16)
            dr_ref[...] = dracc[...].astype(BF16)
            dc = jnp.sum(gs_ref[0].astype(F32) * y, axis=1, keepdims=True)
            dc_ref[...] = jnp.broadcast_to(dc, (slots, 128))

    def mine(last):
        return pl.BlockSpec((1, slots, last), lambda f: (e, 0, 0))

    def whole(last):
        return pl.BlockSpec((slots, last), lambda f: (0, 0))

    chunk = pl.BlockSpec((slots, fc), lambda f: (0, f))
    wide = sds((slots, hidden), BF16)
    row = sds((slots, width), BF16)
    return pl.pallas_call(
        kernel,
        grid=(steps,),
        out_shape=(wide, wide, wide, row, row, row, sds((slots, 128), F32)),
        in_specs=[
            mine(width),
            mine(width),
            mine(128),
            pl.BlockSpec((1, width, fc), lambda f: (e, 0, f)),
            pl.BlockSpec((1, width, fc), lambda f: (e, 0, f)),
            pl.BlockSpec((1, fc, width), lambda f: (e, f, 0)),
        ],
        out_specs=(chunk, chunk, chunk, whole(width), whole(width), whole(width), whole(128)),
        scratch_shapes=[pltpu.VMEM((slots, width), F32), pltpu.VMEM((slots, width), F32)],
        compiler_params=params(60, ("arbitrary",)),
        cost_estimate=cost(12 * slots * width * hidden, 20 << 20),
        name="experts",
    )(x, gs, cs, w_gate, w_up, w_down)


def chip_order(g, i):
    return jnp.where(g < 4, 4, 0) + ((g & 3) ^ (i[0] >> 1))


def other_block(shape):
    return pl.BlockSpec((1,) + shape, lambda g, i: (jnp.minimum(g, 3) ^ (i[0] >> 1), 0, 0))


def mine_block(shape):
    return pl.BlockSpec((1,) + shape, lambda g, i: (jnp.maximum(g - 4, 0) ^ (i[0] >> 1), 0, 0))


def whole_block(shape):
    return pl.BlockSpec(shape, lambda g, i: (0,) * len(shape))


def shared_branch(idx, rows, grads, shared, down):
    _, length, width = rows[0].shape
    ext = grads[0].shape[1]
    part = down.shape[0]
    step = width // 8

    def kernel(idx_ref, h_mine, h_other, g_mine, g_other, wg_ref, wu_ref, wd_ref,
               act_ref, gd_ref, gs_ref, gdacc, gsacc, wdown):
        s = pl.program_id(0)

        @pl.when(s == 0)
        def _():
            gdacc[...] = jnp.zeros_like(gdacc)
            gsacc[...] = jnp.zeros_like(gsacc)
            wdown[...] = wd_ref[...].astype(BF16)

        h = jnp.where(s < 4, h_other[0], h_mine[0])
        grad = jnp.where(s < 4, g_other[0], g_mine[0])[:length]
        gate = nn(h, wg_ref[...])
        up = nn(h, wu_ref[...])
        da = nt(grad, wdown[...])
        silu, slope = silu_parts(gate)
        a = (silu * up).astype(BF16)
        dg = (da * up * slope).astype(BF16)
        du = (da * silu).astype(BF16)
        act_ref[0, :, :part] = a
        act_ref[0, :, part : 2 * part] = dg
        act_ref[0, :, 2 * part :] = du
        gdacc[...] += tn(a, grad)
        gsacc[...] += tn(h, jnp.concatenate([dg, du], axis=1))

        @pl.when(s == 7)
        def _():
            gd_ref[...] = gdacc[...].astype(BF16)
            for k in range(8):
                gs_ref[k] = gsacc[k * step : (k + 1) * step, :].astype(BF16)

    return pl.pallas_call(
        kernel,
        out_shape=(
            sds((8, length, 3 * part), BF16),
            sds((part, width), BF16),
            sds((8, step, 2 * part), BF16),
        ),
        grid_spec=pltpu.PrefetchScalarGridSpec(
            num_scalar_prefetch=1,
            grid=(8,),
            in_specs=[
                mine_block((length, width)),
                other_block((length, width)),
                mine_block((ext, width)),
                other_block((ext, width)),
                whole_block((width, part)),
                whole_block((width, part)),
                whole_block((part, width)),
            ],
            out_specs=(
                pl.BlockSpec((1, length, 3 * part), lambda g, i: (g, 0, 0)),
                whole_block((part, width)),
                whole_block((8, step, 2 * part)),
            ),
            scratch_shapes=[
                pltpu.VMEM((part, width), F32),
                pltpu.VMEM((width, 2 * part), F32),
                pltpu.VMEM((part, width), BF16),
            ],
        ),
        compiler_params=params(60, ("arbitrary",)),
        cost_estimate=cost(12 * 8 * length * width * part, 14 << 20),
        name="shared_branch",
    )(idx, *rows, *grads, *shared, down)


def combine(idx, act, hot, yc, dr, dc, shared, down):
    _, length, _ = act.shape
    part, width = down.shape
    ext = length + 16

    def kernel(idx_ref, act_ref, hot_ref, yc0, yc1, dr0, dr1, dc0, dc1, wg_ref, wu_ref, wd_ref,
               oo_ref, oe_ref, do_ref, de_ref, wdown):
        s = pl.program_id(0)
        i = idx_ref[0]

        def both_of(first, second):
            return jnp.concatenate([first[...], second[...]], axis=0)

        @pl.when(s == 0)
        def _():
            wdown[...] = wd_ref[...].astype(BF16)

        one = hot_ref[0]
        a, dg, du = (act_ref[0, :, m * part : (m + 1) * part] for m in range(3))
        out = (nn(a, wdown[...]) + tn(one, both_of(yc0, yc1))).astype(BF16)
        dh = nt(dg, wg_ref[...]) + nt(du, wu_ref[...]) + tn(one, both_of(dr0, dr1))
        dh = dh.astype(BF16)
        dcv = both_of(dc0, dc1)[:, 0:1] * one.astype(F32)
        expert = lax.broadcasted_iota(jnp.int32, (16, length), 0)
        dp = jnp.zeros((16, length), F32)
        for le in range(2):
            row = jnp.sum(dcv[le * CAP : (le + 1) * CAP], axis=0, keepdims=True)
            dp = dp + jnp.where(expert == 2 * i + le, row, 0.0)

        def put(ref):
            ref[0, :length] = dh
            ref[0, length:] = jnp.zeros((16, width), BF16)
            ref[0, length:, :length] = dp.astype(BF16)

        @pl.when(s < 4)
        def _():
            oo_ref[0] = out
            put(do_ref)

        @pl.when(s >= 4)
        def _():
            oe_ref[0] = out
            put(de_ref)

    def odd(block):
        return pl.BlockSpec((1,) + block, lambda g, i: (jnp.minimum(g, 3), 0, 0))

    def even(block):
        return pl.BlockSpec((1,) + block, lambda g, i: (jnp.maximum(g - 4, 0), 0, 0))

    def slot_spec(last):
        return pl.BlockSpec((CAP, last), lambda g, i: (chip_order(g, i), 0))

    rows4 = sds((4, length, width), BF16)
    ext4 = sds((4, ext, width), BF16)
    return pl.pallas_call(
        kernel,
        out_shape=(rows4, rows4, ext4, ext4),
        grid_spec=pltpu.PrefetchScalarGridSpec(
            num_scalar_prefetch=1,
            grid=(8,),
            in_specs=[
                pl.BlockSpec((1, length, 3 * part), lambda g, i: (g, 0, 0)),
                pl.BlockSpec((1, 2 * CAP, length), lambda g, i: (chip_order(g, i), 0, 0)),
                slot_spec(width),
                slot_spec(width),
                slot_spec(width),
                slot_spec(width),
                slot_spec(128),
                slot_spec(128),
                whole_block((width, part)),
                whole_block((width, part)),
                whole_block((part, width)),
            ],
            out_specs=(
                odd((length, width)), even((length, width)),
                odd((ext, width)), even((ext, width)),
            ),
            scratch_shapes=[pltpu.VMEM((part, width), BF16)],
        ),
        compiler_params=params(60, ("arbitrary",)),
        cost_estimate=cost(10 * 8 * length * width * part, 18 << 20),
        name="combine",
    )(idx, act, hot, *yc, *dr, *dc, *shared, down)


def attention_backward(idx, tokens, grad, live_row, gain1, gain2, saved, router_t, dh_parts,
                       pieces):
    layout = layout_of(pieces)
    n = len(layout)
    length, width = tokens.shape
    step = width // 8
    cosine, sine = rope_tables(length)
    h1, q, k, v, o, prob, x1, h2 = saved
    total = 4 * width + 128

    def kernel(idx_ref, x_ref, g_ref, lv_ref, g1_ref, g2_ref, cos_ref, sin_ref, h1_ref, q_ref,
               k_ref, v_ref, o_ref, p_ref, x1_ref, h2_ref, wr_ref, d0, d1, d2, d3, *refs):
        piece_refs, refs = refs[:n], refs[n:]
        gt_ref, odd_ref, even_ref, wbuf, dmix, dqkv, gbuf, sems = refs
        i = idx_ref[0]
        copies = place_copies(i, layout, step, piece_refs, wbuf, sems)
        for c in copies:
            c.start()
        x1v = x1_ref[...]
        r2 = norm_scale(x1v)
        wr = wr_ref[...]
        pr = router_probs(wr, h2_ref[...])
        came = add([d0[...], d1[...], d2[...], d3[...]])
        dp = came[length:, :length] * lv_ref[...]
        dl = (pr * (dp - jnp.sum(pr * dp, axis=0, keepdims=True))).astype(BF16)
        router_grad = nn(dl, h2_ref[...])
        dh2 = came[:length] + tn(dl, wr)
        gain2_grad = jnp.sum(dh2 * x1v * r2, axis=0, keepdims=True)
        weighted = dh2 * g2_ref[...]
        inner = jnp.mean(x1v * weighted, axis=-1, keepdims=True)
        dx1 = g_ref[...].astype(F32) + r2 * weighted - x1v * (r2 * r2 * r2) * inner
        da = dx1.astype(BF16)
        for c in copies:
            c.wait()
        gbuf[:, 3 * width : 4 * width] = tn(o_ref[...], da).astype(BF16)
        dmix[...] = nt(da, wbuf[:, 3 * width : 4 * width]).astype(BF16)
        first = lax.broadcasted_iota(jnp.int32, (length, 128), 1) < HEAD_DIM

        def pair(hp, carry):
            at = pl.multiple_of(hp * 128, 128)
            qv, kv, vv = (ref[:, pl.ds(at, 128)] for ref in (q_ref, k_ref, v_ref))
            dov = dmix[:, pl.ds(at, 128)]
            zero = jnp.zeros_like(qv)
            dq = jnp.zeros((length, 128), F32)
            dk = jnp.zeros((length, 128), F32)
            dv = jnp.zeros((length, 128), F32)
            for h in range(2):
                mine = first if h == 0 else jnp.logical_not(first)
                p = p_ref[2 * hp + h]
                dom = jnp.where(mine, dov, zero)
                dp = nt(dom, vv)
                dv = dv + tn(p.astype(BF16), dom)
                ds = p * (dp - jnp.sum(p * dp, axis=-1, keepdims=True))
                ds = (ds * SCALE).astype(BF16)
                dq = dq + nn(ds, jnp.where(mine, kv, zero))
                dk = dk + tn(ds, jnp.where(mine, qv, zero))
            cosv, sinv = cos_ref[...], sin_ref[...]
            dqkv[:, pl.ds(at, 128)] = (dq * cosv - half_swap(dq) * sinv).astype(BF16)
            dqkv[:, pl.ds(at + width, 128)] = (dk * cosv - half_swap(dk) * sinv).astype(BF16)
            dqkv[:, pl.ds(at + 2 * width, 128)] = dv.astype(BF16)
            return carry

        lax.fori_loop(0, HEADS // 2, pair, 0)
        gbuf[:, : 3 * width] = tn(h1_ref[...], dqkv[...]).astype(BF16)
        dh1 = nt(dqkv[...], wbuf[:, : 3 * width])
        x = x_ref[...].astype(F32)
        r1 = norm_scale(x)
        gain1_grad = jnp.sum(dh1 * x * r1, axis=0, keepdims=True)
        weighted = dh1 * g1_ref[...]
        inner = jnp.mean(x * weighted, axis=-1, keepdims=True)
        gt_ref[...] = (dx1 + r1 * weighted - x * (r1 * r1 * r1) * inner).astype(BF16)
        small = jnp.concatenate(
            [router_grad, gain1_grad, gain2_grad, jnp.zeros((110, width), F32)], axis=0
        )
        gbuf[:, 4 * width :] = small.T.astype(BF16)
        for kk in range(8):
            rows = gbuf[pl.ds(pl.multiple_of((i ^ kk) * step, 16), step), :]
            if kk % 2:
                odd_ref[kk // 2] = rows
            else:
                even_ref[kk // 2] = rows

    blocks = sds((4, step, total), BF16)
    return pl.pallas_call(
        kernel,
        out_shape=(sds((length, width), BF16), blocks, blocks),
        in_specs=[SMEM_SPEC] + [VMEM_SPEC] * 20 + [ANY_SPEC] * n,
        out_specs=(VMEM_SPEC,) * 3,
        scratch_shapes=[
            pltpu.VMEM((width, pieces[0][2].shape[1]), BF16),
            pltpu.VMEM((length, width), BF16),
            pltpu.VMEM((length, 3 * width), BF16),
            pltpu.VMEM((width, total), BF16),
            pltpu.SemaphoreType.DMA((n,)),
        ],
        compiler_params=params(60),
        cost_estimate=cost(20 * length * width * width, 24 << 20),
        name="attention_backward",
    )(idx, tokens, grad, live_row, gain1, gain2, cosine, sine, h1, q, k, v, o, prob, x1, h2,
      router_t, *dh_parts, *[p for _, _, p in pieces])


def expert_grads(idx, e, base, steps, own, others, weights, done=()):
    w_gate, w_up, w_down = weights
    a, dg, du, dy, xd = own
    x_o, dy_o, xd_o = others
    slots, hidden = a.shape
    local = x_o.shape[0]
    many = x_o.shape[1]
    width = x_o.shape[2]
    piece = xd.shape[2]
    fc = 512
    tile = 512

    def kernel(idx_ref, a_ref, dg_ref, du_ref, dy_ref, xd_ref, xo_ref, dyo_ref, xdo_ref,
               wg_ref, wu_ref, wd_ref, *refs):
        gg_ref, gu_ref, gd_ref, ao, dgo, duo, gds, gsem = refs[len(done) :]
        f = pl.program_id(0)
        wg, wu, wd = wg_ref[0], wu_ref[0], wd_ref[0]

        def rows(t, carry):
            at = pl.ds(pl.multiple_of(t * tile, tile), tile)
            g = nn(xo_ref[0, at], wg)
            u = nn(xo_ref[0, at], wu)
            da = nt(dyo_ref[0, at], wd)
            silu, slope = silu_parts(g)
            ao[at] = (silu * u).astype(BF16)
            dgo[at] = (da * u * slope).astype(BF16)
            duo[at] = (da * silu).astype(BF16)
            return carry

        lax.fori_loop(0, many // tile, rows, 0)
        gg_ref[0] = tn(xdo_ref[0], dgo[...]) + tn(xd_ref[0], dg_ref[...])
        gu_ref[0] = tn(xdo_ref[0], duo[...]) + tn(xd_ref[0], du_ref[...])

        @pl.when(base + f == idx_ref[1])
        def _():
            gds[...] = tn(ao[...], dyo_ref[0]) + tn(a_ref[...], dy_ref[...])
            copy = pltpu.make_async_copy(gds, gd_ref.at[e], gsem)
            copy.start()
            copy.wait()

    def mine(block):
        return pl.BlockSpec((1,) + block, lambda f, i: (e, 0, 0))

    def chunk(rows):
        return pl.BlockSpec((1, rows, fc), lambda f, i: (e, 0, base + f))

    return pl.pallas_call(
        kernel,
        out_shape=(
            sds((local, piece, hidden), F32),
            sds((local, piece, hidden), F32),
            sds((local, fc, width), F32),
        ),
        grid_spec=pltpu.PrefetchScalarGridSpec(
            num_scalar_prefetch=1,
            grid=(steps,),
            in_specs=[
                pl.BlockSpec((slots, fc), lambda f, i: (0, i[1])),
                pl.BlockSpec((slots, fc), lambda f, i: (0, base + f)),
                pl.BlockSpec((slots, fc), lambda f, i: (0, base + f)),
                pl.BlockSpec((slots, width), lambda f, i: (0, 0)),
                mine((slots, piece)),
                mine((many, width)),
                mine((many, width)),
                mine((many, piece)),
                chunk(width),
                chunk(width),
                pl.BlockSpec((1, fc, width), lambda f, i: (e, base + f, 0)),
            ]
            + [ANY_SPEC] * len(done),
            out_specs=(chunk(piece), chunk(piece), ANY_SPEC),
            scratch_shapes=[pltpu.VMEM((many, fc), BF16) for _ in range(3)]
            + [pltpu.VMEM((fc, width), F32), pltpu.SemaphoreType.DMA],
        ),
        compiler_params=params(60, ("arbitrary",)),
        cost_estimate=cost(steps * fc * width * (6 * many + 2 * (many + slots)), 15 << 20),
        input_output_aliases={12 + m: m for m in range(len(done))},
        name="expert_grads",
    )(idx, a, dg, du, dy, xd, x_o, dy_o, xd_o, w_gate, w_up, w_down, *done)


def finish_shared(blocks, part):
    n, step, _ = blocks.shape

    def kernel(s_ref, gate_ref, up_ref):
        for k in range(n):
            block = s_ref[k].astype(F32)
            gate_ref[:, k * part : (k + 1) * part] = block[:, :part]
            up_ref[:, k * part : (k + 1) * part] = block[:, part:]

    wide = sds((step, n * part), F32)
    return pl.pallas_call(
        kernel,
        out_shape=(wide, wide),
        in_specs=[VMEM_SPEC],
        out_specs=(VMEM_SPEC,) * 2,
        compiler_params=params(60),
        name="finish_shared",
    )(blocks)


def finish_attention(idx, parts, width):
    rows, total = parts[0].shape
    rest = total - width

    def kernel(idx_ref, s0, s1, s2, s3, q_ref, k_ref, v_ref, o_ref, m_ref):
        z = idx_ref[1]
        for r, s in enumerate((s0, s1, s2, s3)):
            m_ref[(z - r + 4) & 3] = s[:, width:].astype(F32)
            for m, ref in enumerate((q_ref, k_ref, v_ref, o_ref)):

                @pl.when(((z - r + 4) & 3) == m)
                def _(ref=ref, s=s):
                    ref[...] = s[:, :width].astype(F32)

    flat = sds((rows, width), F32)
    return pl.pallas_call(
        kernel,
        out_shape=(flat, flat, flat, flat, sds((4, rows, rest), F32)),
        in_specs=[SMEM_SPEC] + [VMEM_SPEC] * 4,
        out_specs=(VMEM_SPEC,) * 5,
        compiler_params=params(60),
        name="finish_attention",
    )(idx, *parts)


def on_device(
    tokens,
    segment_ids,
    padding,
    routes,
    w_query,
    w_key,
    w_value,
    w_out,
    w_router,
    shared_gate,
    shared_up,
    shared_down,
    gain_attn,
    gain_ffn,
    expert_gate,
    expert_up,
    expert_down,
    cotangent,
):
    length, width = tokens.shape
    planes = lax.axis_size("dp")
    i = lax.axis_index("expert").astype(jnp.int32)
    z = lax.axis_index("dp").astype(jnp.int32)
    idx = jnp.stack([i, z])
    step = width // 8
    part = shared_down.shape[0]
    spread = planes == 4

    router_pad = jnp.pad(w_router, ((0, 0), (0, 128 - w_router.shape[1])))
    attn_shard = jnp.concatenate([w_query, w_key, w_value, w_out, router_pad], axis=1).astype(BF16)
    live_row = padding.astype(F32)
    meta = jnp.concatenate([routes[:, 0], routes[:, 1], padding[0]]).astype(BF16)[None, :]
    grad_ext = jnp.concatenate([cotangent, meta, jnp.zeros((15, width), BF16)], axis=0)
    ext = grad_ext.shape[0]

    def others(columns):
        at = [(z - r) % planes for r in (1, 2, 3)]
        return jnp.concatenate([lax.dynamic_index_in_dim(columns, a, 0, False) for a in at], axis=0)

    def copies(rows):
        return jnp.broadcast_to(rows[None], (planes,) + rows.shape)

    def columns(blocks):
        return lax.all_to_all(blocks, "dp", split_axis=0, concat_axis=0, tiled=True)

    def dp_gather(rows):
        return lax.all_gather(rows, "dp", axis=0)

    g_mine = lax.all_gather(grad_ext, "expert", axis=0, axis_index_groups=same_core())
    if spread:
        g_columns = dp_gather(grad_ext)
    attn_pieces = relay_gather(attn_shard)

    side = jnp.stack([shared_gate.astype(BF16), shared_up.astype(BF16)])
    side = side.reshape(2, step, 8, part).transpose(2, 0, 1, 3)
    side = after(side, attn_pieces[3][2], attn_pieces[4][2])
    side = lax.all_to_all(side, "expert", split_axis=0, concat_axis=0, tiled=True)

    gain1, gain2 = gain_attn[None, :], gain_ffn[None, :]
    *saved, router_t, h2_copies = attention_forward(
        idx, tokens, segment_ids, live_row, gain1, gain2, attn_pieces,
    )
    x1, h2 = saved[6], saved[7]

    g_plane = [g_mine, swap(g_mine, 1)]
    side = after(side, h2)
    h_mine = chips_exchange(after(h2_copies, side))
    h_plane = [h_mine, swap(h_mine, 1)]
    if spread:
        h_columns = dp_gather(h2)
        at = (i // 2) ^ 3
        corner = [
            lax.dynamic_index_in_dim(rows, at, 0, False) for rows in after((g_mine, h_mine), h_plane)
        ]
        corner = dp_gather(jnp.concatenate(corner, axis=0))
        g_far = others(after(g_columns, h_plane))
        g_far = [g_far, swap(g_far, 2), swap(g_far, 4)]

    cut = width // 4
    x_own, xd_own, gs_own, cs_own, hot = dispatch_plane(
        idx, router_t, h_plane, g_plane, cut
    )

    weights = (expert_gate, expert_up, expert_down)
    a0, dg0, du0, dy0, yc0, dr0, dc0 = experts(0, x_own, gs_own, cs_own, *weights)
    x_next = after(x_own, yc0)
    if spread:
        g_far, h_columns = after((g_far, h_columns), yc0)
        x_next = after(x_next, g_far, h_columns)
        g_far = both_cores(g_far)
        h_far = others(h_columns)
        h_far = [h_far, swap(h_far, 2), swap(h_far, 4)]
    a1, dg1, du1, dy1, yc1, dr1, dc1 = experts(1, x_next, gs_own, cs_own, *weights)
    shared_w = [after(side, yc1)[:, m].reshape(width, part) for m in range(2)]
    if spread:
        g_far = after(g_far, yc1)
        shared_w = after(shared_w, g_far)
    act, gsd, gside = shared_branch(idx, h_plane, g_plane, shared_w, shared_down)
    gsd, gside = lax.psum((gsd, gside), "dp")
    if spread:
        h_far = after(h_far, act)
        act = after(act, h_far)
        h_far = both_cores(h_far)
    out_other, out_mine, dh_other, dh_mine = combine(
        idx, act, hot, (yc0, yc1), (dr0, dr1), (dc0, dc1), shared_w, shared_down
    )
    dh_came = swap(dh_other, 1)
    if spread:
        h_far, corner = after((h_far, corner), dh_came)
        dh_came = after(dh_came, h_far, corner)
        corners = both_cores([others(corner)])
    dh_sums = plane_near(dh_mine, dh_came)
    dh_parts = plane_far(dh_sums)
    if spread:
        h_far, g_far = after((h_far, g_far), dh_sums)
        x_far, xd_far, dy_far = dispatch_others(idx, router_t, h_far, g_far, corners, 3, cut)
        dh_parts = after(dh_parts, x_far)
    grad_tokens, att_other, att_mine = attention_backward(
        idx, tokens, cotangent, live_row, gain1, gain2, saved, router_t, dh_parts, attn_pieces,
    )
    att_sums = plane_near(att_mine, swap(att_other, 1))
    att_parts = plane_far(att_sums)
    def att_quarters(parts):
        att = add(parts).astype(BF16)
        small = att[:, 4 * width :]
        return jnp.stack(
            [
                jnp.concatenate(
                    [att[:, m * width : (m + 1) * width], small[:, 32 * m : 32 * (m + 1)]], axis=1
                )
                for m in range(4)
            ]
        )

    if spread:
        xs = (x_far, dy_far, xd_far)
        own = (a0, dg0, du0, dy0, xd_own), (a1, dg1, du1, dy1, xd_own)
        chunks = expert_gate.shape[2] // 512
        done = expert_grads(idx, 0, 0, chunks, own[0], after(xs, att_sums), weights)
        att_parts = after(att_parts, done)
        xs = after(xs, att_parts)
        att_scattered = dp_scatter(att_quarters(att_parts))
        out_came = swap(after(out_other, done), 1)
        done = expert_grads(idx, 1, 0, chunks // 2, own[1], xs, weights, done)
        att_scattered, out_came = after((att_scattered, out_came), done)
        xs = after(xs, att_scattered, out_came)
        att_spread = dp_spread(att_scattered)
        out_parts = plane_far(plane_near(out_mine, out_came))
        gsd, gside = after((gsd, gside), done)
        gside = lax.all_to_all(gside, "expert", split_axis=0, concat_axis=0, tiled=True)
        done = expert_grads(idx, 1, chunks // 2, chunks // 2, own[1], xs, weights, done)
        g_gate, g_up, g_down = done
        order = idx
    else:
        att_spread = dp_whole(att_quarters(att_parts))
        gside = lax.all_to_all(gside, "expert", split_axis=0, concat_axis=0, tiled=True)
        out_parts = plane_far(plane_near(out_mine, swap(after(out_other, att_parts), 1)))
        order = idx * jnp.array([1, 0], jnp.int32)

        def scattered(left, right):
            local = jnp.einsum("end,enf->edf", left, right, preferred_element_type=F32)
            return lax.psum_scatter(
                local.astype(BF16), "dp", scatter_dimension=1, tiled=True
            ).astype(F32)

        g_gate = scattered(x_own, jnp.stack([dg0, dg1]))
        g_up = scattered(x_own, jnp.stack([du0, du1]))
        g_down = scattered(jnp.stack([a0, a1]), jnp.stack([dy0, dy1]))

    gq, gk, gv, go, small = finish_attention(order, att_spread, width)
    small = jnp.concatenate([small[0], small[1], small[2], small[3]], axis=1)
    g_sgate, g_sup = finish_shared(gside, part)
    g_sdown = gsd.astype(F32)
    output = (x1 + add(out_parts)).astype(BF16)

    experts_all = w_router.shape[1]
    return (
        output,
        grad_tokens,
        gq,
        gk,
        gv,
        go,
        small[:, :experts_all],
        g_sgate,
        g_sup,
        g_sdown,
        small[:, experts_all],
        small[:, experts_all + 1],
        g_gate,
        g_up,
        g_down,
    )


def solution(mesh):
    both = P(("dp", "expert"), None)
    one = P("expert", None)
    three = P("expert", None, None)
    sliced = P("expert", "dp", None)
    return jax.shard_map(
        on_device,
        mesh=mesh,
        in_specs=(both,) * 4 + (one,) * 8 + (P(), P()) + (three,) * 3 + (both,),
        out_specs=(both, both) + (one,) * 8 + (P("expert"), P("expert")) + (sliced,) * 3,
        check_vma=False,
    )
```

```python
import numpy as np

import jax
import jax.numpy as jnp
from jax import lax
from jax.experimental import pallas as pl
from jax.experimental.pallas import tpu as pltpu
from jax.sharding import PartitionSpec as P

HEADS = 12
HEAD_DIM = 64
CAP = 64
TILE = 1536
EPS = 1e-06
ROPE_BASE = 10000.0
MASKED = -1e30
SCALE = HEAD_DIM**-0.5
F32 = jnp.float32
BF16 = jnp.bfloat16
MIB = 1 << 20
VMEM_SPEC = pl.BlockSpec(memory_space=pltpu.VMEM)
SMEM_SPEC = pl.BlockSpec(memory_space=pltpu.SMEM)
ANY_SPEC = pl.BlockSpec(memory_space=pl.ANY)


def nn(a, b):
    return jnp.dot(a, b, preferred_element_type=F32)


def nt(a, b):
    return lax.dot_general(a, b, (((1,), (1,)), ((), ())), preferred_element_type=F32)


def tn(a, b):
    return lax.dot_general(a, b, (((0,), (0,)), ((), ())), preferred_element_type=F32)


def sds(shape, dtype):
    return jax.ShapeDtypeStruct(shape, dtype)


def cost(flops, nbytes):
    return pl.CostEstimate(
        flops=int(flops * 0.02), bytes_accessed=int(nbytes * 0.02), transcendentals=0
    )


def params(mib, semantics=None):
    return pltpu.CompilerParams(vmem_limit_bytes=mib * MIB, dimension_semantics=semantics)


def swap(x, k):
    n = lax.axis_size("expert")
    return lax.ppermute(x, "expert", [(j, j ^ k) for j in range(n)])


def shift(x, k):
    n = lax.axis_size("dp")
    return lax.ppermute(x, "dp", [(j, (j + k) % n) for j in range(n)])


def after(value, *first):
    return lax.optimization_barrier((value, first))[0]


def relay_gather(x):
    half = x.shape[0] // 32 * 16
    a, b = swap(x, 2), swap(x, 4)
    d0, d1 = swap(a[:half], 4), swap(b[half:], 2)
    near = [(0, 0, x), (2, 0, a), (4, 0, b), (6, 0, d0), (6, half, d1)]
    return near + [(k + 1, at, swap(piece, 1)) for k, at, piece in near]


def same_core():
    n = lax.axis_size("expert")
    return [list(range(c, n, 2)) for c in range(2)]


def chips_exchange(blocks):
    return lax.all_to_all(
        blocks, "expert", split_axis=0, concat_axis=0, tiled=True, axis_index_groups=same_core()
    )


def both_cores(near):
    other = [swap(p, 1) for p in near]
    return [p for pair in zip(near, other) for p in pair]


def plane_near(even, came):
    return [add([even[j], came[j]]).astype(even.dtype) for j in range(4)]


def plane_far(sums):
    return [sums[0], swap(sums[1], 2), swap(sums[2], 4), swap(sums[3], 6)]


def dp_scatter(quarters):
    z = lax.axis_index("dp")
    parts = [lax.dynamic_index_in_dim(quarters, (z + k) % 4, 0, False) for k in range(4)]
    return [parts[0]] + [shift(parts[k], k) for k in (1, 2, 3)]


def dp_spread(parts):
    total = add(parts).astype(parts[0].dtype)
    return [total] + [shift(total, k) for k in (1, 2, 3)]


def dp_whole(quarters):
    whole = lax.psum(quarters, "dp")
    return [whole[0], whole[3], whole[2], whole[1]]


def add(parts):
    total = parts[0].astype(F32)
    for p in parts[1:]:
        total = total + p.astype(F32)
    return total


def norm_scale(values):
    return lax.rsqrt(jnp.mean(values * values, axis=-1, keepdims=True) + EPS)


def silu_parts(gate):
    logistic = 0.5 * jnp.tanh(0.5 * gate) + 0.5
    silu = gate * logistic
    return silu, logistic + silu * (1.0 - logistic)


def split_heads(x, first):
    zero = jnp.zeros_like(x)
    return jnp.concatenate([jnp.where(first, x, zero), jnp.where(first, zero, x)], axis=0)


def half_swap(x):
    lane = lax.broadcasted_iota(jnp.int32, x.shape, 1)
    half = HEAD_DIM // 2
    return jnp.where(
        lane % HEAD_DIM < half, pltpu.roll(x, x.shape[1] - half, 1), pltpu.roll(x, half, 1)
    )


def place_copies(i, layout, step, refs, target, sems):
    copies = []
    for n, ((k, at, rows), ref) in enumerate(zip(layout, refs)):
        start = pl.multiple_of((i ^ k) * step + at, 16)
        copies.append(pltpu.make_async_copy(ref, target.at[pl.ds(start, rows), :], sems.at[n]))
    return copies


def layout_of(pieces):
    return tuple((k, at, piece.shape[0]) for k, at, piece in pieces)


def rope_tables(length):
    half = HEAD_DIM // 2
    frequency = (ROPE_BASE ** (-(2.0 * np.arange(half, dtype=np.float32)) / HEAD_DIM)).astype(
        np.float32
    )
    angles = (np.arange(length, dtype=np.float32)[:, None] * frequency[None, :]).astype(np.float32)
    cosine, sine = np.cos(angles), np.sin(angles)
    return (
        np.concatenate([cosine] * 4, 1).astype(np.float32),
        np.concatenate([-sine, sine, -sine, sine], 1).astype(np.float32),
    )


def pack_shard(projections, router):
    rows, width = projections[0].shape
    n = len(projections)

    def kernel(*refs):
        out = refs[-1]
        for m in range(n):
            out[:, m * width : (m + 1) * width] = refs[m][...].astype(BF16)
        out[:, n * width :] = jnp.zeros((rows, 128), BF16)
        out[:, n * width : n * width + router.shape[1]] = refs[n][...].astype(BF16)

    return pl.pallas_call(
        kernel,
        out_shape=sds((rows, n * width + 128), BF16),
        in_specs=[VMEM_SPEC] * (n + 1),
        out_specs=VMEM_SPEC,
        compiler_params=params(60),
        cost_estimate=cost(1, 1 << 20),
        name="pack_shard",
    )(*projections, router)


def attention_forward(idx, tokens, seg_row, live_row, gain1, gain2, pieces):
    layout = layout_of(pieces)
    n = len(layout)
    length, width = tokens.shape
    step = width // 8
    cosine, sine = rope_tables(length)

    def kernel(idx_ref, x_ref, sr_ref, lv_ref, g1_ref, g2_ref, cos_ref, sin_ref, *refs):
        piece_refs, refs = refs[:n], refs[n:]
        h1_ref, q_ref, k_ref, v_ref, o_ref, p_ref, x1_ref, h2_ref, wr_ref, h4_ref = refs[:10]
        wbuf, pre, probs, sems, psem = refs[10:]
        copies = place_copies(idx_ref[0], layout, step, piece_refs, wbuf, sems)
        for c in copies:
            c.start()
        x = x_ref[...].astype(F32)
        h1 = (x * norm_scale(x) * g1_ref[...]).astype(BF16)
        h1_ref[...] = h1
        row = lax.broadcasted_iota(jnp.int32, (length, length), 0)
        col = lax.broadcasted_iota(jnp.int32, (length, length), 1)
        seg = sr_ref[...].astype(F32)
        seg_col = jnp.broadcast_to(seg, (8, length)).T[:, 0:1]
        allowed = (col == row) | ((col <= row) & (seg == seg_col) & (lv_ref[...] > 0.0))
        bias = jnp.where(allowed, 0.0, MASKED)
        for c in copies:
            c.wait()
        pre[...] = nn(h1, wbuf[:, : 3 * width])
        first = lax.broadcasted_iota(jnp.int32, (length, 128), 1) < HEAD_DIM

        def pair(hp, carry):
            at = pl.multiple_of(hp * 128, 128)
            qp = pre[:, pl.ds(at, 128)]
            kp = pre[:, pl.ds(at + width, 128)]
            v = pre[:, pl.ds(at + 2 * width, 128)].astype(BF16)
            cosv, sinv = cos_ref[...], sin_ref[...]
            q = (qp * cosv + half_swap(qp) * sinv).astype(BF16)
            k = (kp * cosv + half_swap(kp) * sinv).astype(BF16)
            q_ref[:, pl.ds(at, 128)] = q
            k_ref[:, pl.ds(at, 128)] = k
            v_ref[:, pl.ds(at, 128)] = v
            scores = nt(split_heads(q, first), k) * SCALE
            scores = scores.reshape(2, length, length) + bias
            e = jnp.exp(scores - jnp.max(scores, axis=-1, keepdims=True))
            p = e / jnp.sum(e, axis=-1, keepdims=True)
            probs[pl.ds(2 * hp, 2)] = p
            pltpu.make_async_copy(
                probs.at[pl.ds(2 * hp, 2)], p_ref.at[pl.ds(2 * hp, 2)], psem.at[hp]
            ).start()
            low = p.astype(BF16)
            mixed = nn(jnp.concatenate([low[0], low[1]], axis=1), split_heads(v, first))
            o_ref[:, pl.ds(at, 128)] = mixed.astype(BF16)
            return carry

        lax.fori_loop(0, HEADS // 2, pair, 0)
        x1 = x + nn(o_ref[...], wbuf[:, 3 * width : 4 * width])
        x1_ref[...] = x1
        h2 = (x1 * norm_scale(x1) * g2_ref[...]).astype(BF16)
        h2_ref[...] = h2
        for chip in range(4):
            h4_ref[chip] = h2
        wr_ref[...] = wbuf[:, 4 * width :].astype(F32).T[:16].astype(BF16)
        for hp in range(HEADS // 2):
            pltpu.make_async_copy(
                probs.at[pl.ds(2 * hp, 2)], p_ref.at[pl.ds(2 * hp, 2)], psem.at[hp]
            ).wait()

    flat = sds((length, width), BF16)
    return pl.pallas_call(
        kernel,
        out_shape=(
            flat, flat, flat, flat, flat,
            sds((HEADS, length, length), F32),
            sds((length, width), F32),
            flat,
            sds((16, width), BF16),
            sds((4, length, width), BF16),
        ),
        in_specs=[SMEM_SPEC] + [VMEM_SPEC] * 7 + [ANY_SPEC] * n,
        out_specs=(VMEM_SPEC,) * 5 + (ANY_SPEC,) + (VMEM_SPEC,) * 4,
        scratch_shapes=[
            pltpu.VMEM((width, pieces[0][2].shape[1]), BF16),
            pltpu.VMEM((length, 3 * width), F32),
            pltpu.VMEM((HEADS, length, length), F32),
            pltpu.SemaphoreType.DMA((n,)),
            pltpu.SemaphoreType.DMA((HEADS // 2,)),
        ],
        compiler_params=params(60),
        cost_estimate=cost(8 * length * width * width, 12 << 20),
        name="attention_forward",
    )(idx, tokens, seg_row, live_row, gain1, gain2, cosine, sine,
      *[p for _, _, p in pieces])


def route_rows(meta, prob, le, i, upper, length):
    expert = (2 * i + le).astype(F32)
    hit = (meta[:, :length] == expert) | (meta[:, length : 2 * length] == expert)
    hot = jnp.where(hit, 1.0, 0.0)
    rank = nn(jnp.broadcast_to(hot, (16, length)).astype(BF16), upper)[0:1]
    slot = lax.broadcasted_iota(jnp.int32, (CAP, length), 0).astype(F32) + 1.0
    one = jnp.where((slot == rank) & hit, 1.0, 0.0)
    which = lax.broadcasted_iota(jnp.int32, prob.shape, 0) == 2 * i + le
    weight = jnp.sum(jnp.where(which, prob, 0.0), axis=0, keepdims=True)
    return one, weight * meta[:, 2 * length :]


def router_probs(router_t, rows):
    logits = nt(router_t, rows)
    e = jnp.exp(logits - jnp.max(logits, axis=0, keepdims=True))
    return e / jnp.sum(e, axis=0, keepdims=True)


def upper_ones(length):
    return jnp.where(
        lax.broadcasted_iota(jnp.int32, (length, length), 0)
        <= lax.broadcasted_iota(jnp.int32, (length, length), 1),
        1.0,
        0.0,
    ).astype(BF16)


def dispatch_plane(idx, router_t, rows, grads, piece):
    _, length, width = rows[0].shape
    slots = 8 * CAP
    ext = length + 16

    def kernel(idx_ref, wr_ref, *refs):
        hp, gp, refs = refs[:2], refs[2:4], refs[4:]
        x_ref, xd_ref, gs_ref, cs_ref, hot_ref, hall, gall, sems = refs
        i = idx_ref[0]
        copies = []
        for c in range(2):
            copies.append(pltpu.make_async_copy(hp[c], hall.at[pl.ds(4 * c, 4)], sems.at[c]))
            copies.append(pltpu.make_async_copy(gp[c], gall.at[pl.ds(4 * c, 4)], sems.at[2 + c]))
        for c in copies:
            c.start()
        upper = upper_ones(length)
        turn = (width - idx_ref[1] * piece) % width
        for c in copies:
            c.wait()

        def sequences(pair, carry):
            for k in (2 * pair, 2 * pair + 1):
                h = hall[k]
                prob = router_probs(wr_ref[...], h)
                meta = gall[k, length:ext][0:1].astype(F32)
                at = pl.multiple_of(k * CAP, CAP)
                ones = []
                for le in range(2):
                    one, weight = route_rows(meta, prob, le, i, upper, length)
                    col = jnp.sum(one * weight, axis=1, keepdims=True)
                    cs_ref[le, pl.ds(at, CAP), :] = jnp.broadcast_to(col, (CAP, 128))
                    ones.append(one.astype(BF16))
                hot = jnp.concatenate(ones, axis=0)
                hot_ref[k] = hot
                picked = nn(hot, h)
                cut = pltpu.roll(picked, turn, 1)[:, :piece].astype(BF16)
                picked = picked.astype(BF16)
                grads = nn(hot, gall[k, 0:length]).astype(BF16)
                for le in range(2):
                    mine = slice(le * CAP, (le + 1) * CAP)
                    x_ref[le, pl.ds(at, CAP), :] = picked[mine]
                    xd_ref[le, pl.ds(at, CAP), :] = cut[mine]
                    gs_ref[le, pl.ds(at, CAP), :] = grads[mine]
            return carry

        lax.fori_loop(0, 4, sequences, 0)

    return pl.pallas_call(
        kernel,
        out_shape=(
            sds((2, slots, width), BF16),
            sds((2, slots, piece), BF16),
            sds((2, slots, width), BF16),
            sds((2, slots, 128), F32),
            sds((8, 2 * CAP, length), BF16),
        ),
        in_specs=[SMEM_SPEC, VMEM_SPEC] + [ANY_SPEC] * 4,
        out_specs=(VMEM_SPEC,) * 5,
        scratch_shapes=[
            pltpu.VMEM((8, length, width), BF16),
            pltpu.VMEM((8, ext, width), BF16),
            pltpu.SemaphoreType.DMA((4,)),
        ],
        compiler_params=params(60),
        cost_estimate=cost(8 * 4 * 2 * CAP * length * width, 16 << 20),
        name="dispatch_plane",
    )(idx, router_t, *rows, *grads)


def dispatch_others(idx, router_t, h_pieces, g_pieces, corners, planes, piece):
    width = h_pieces[0].shape[1]
    length = h_pieces[0].shape[0] // planes
    ext = length + 16
    slots = 8 * planes * CAP

    def kernel(idx_ref, wr_ref, *refs):
        hp, gp, both, refs = refs[:6], refs[6:12], refs[12:14], refs[14:]
        x_out, xd_out, dy_out, hall, gall, hsems, gsems, x_ref, xd_ref, dy_ref, osems = refs
        i = idx_ref[0]

        def leaving(k):
            rows = pl.ds(pl.multiple_of(k * planes * CAP, CAP), planes * CAP)
            for m, (a, b) in enumerate(((x_ref, x_out), (xd_ref, xd_out), (dy_ref, dy_out))):
                yield pltpu.make_async_copy(a.at[:, rows], b.at[:, rows], osems.at[k, m])

        def copies(k):
            if k < 6:
                yield pltpu.make_async_copy(hp[k], hall.at[k], hsems.at[k, 0])
                yield pltpu.make_async_copy(gp[k], gall.at[k], gsems.at[k, 0])
                return
            for s in range(planes):
                base = s * (ext + length)
                yield pltpu.make_async_copy(
                    both[k - 6].at[pl.ds(base, ext)], gall.at[k, pl.ds(s * ext, ext)], gsems.at[k, s]
                )
                yield pltpu.make_async_copy(
                    both[k - 6].at[pl.ds(base + ext, length)],
                    hall.at[k, pl.ds(s * length, length)],
                    hsems.at[k, s],
                )

        for k in range(8):
            for c in copies(k):
                c.start()
        upper = upper_ones(length)
        turn = (width - idx_ref[1] * piece) % width

        def column(k, carry):
            @pl.when(k < 6)
            def _():
                pltpu.make_async_copy(hall.at[k], hall.at[k], hsems.at[k, 0]).wait()
                pltpu.make_async_copy(gall.at[k], gall.at[k], gsems.at[k, 0]).wait()

            @pl.when(k >= 6)
            def _():
                for s in range(planes):
                    h = hall.at[k, pl.ds(s * length, length)]
                    g = gall.at[k, pl.ds(s * ext, ext)]
                    pltpu.make_async_copy(h, h, hsems.at[k, s]).wait()
                    pltpu.make_async_copy(g, g, gsems.at[k, s]).wait()

            for s in range(planes):
                h = hall[k, s * length : (s + 1) * length]
                g = gall[k, s * ext : s * ext + length]
                meta = gall[k, s * ext + length : (s + 1) * ext][0:1].astype(F32)
                prob = router_probs(wr_ref[...], h)
                ones, cols = [], []
                for le in range(2):
                    one, weight = route_rows(meta, prob, le, i, upper, length)
                    cols.append(jnp.sum(one * weight, axis=1, keepdims=True))
                    ones.append(one.astype(BF16))
                hot = jnp.concatenate(ones, axis=0)
                picked = nn(hot, h)
                cut = pltpu.roll(picked, turn, 1)[:, :piece].astype(BF16)
                picked = picked.astype(BF16)
                dy = (nn(hot, g) * jnp.concatenate(cols, axis=0)).astype(BF16)
                at = pl.ds(pl.multiple_of((k * planes + s) * CAP, CAP), CAP)
                for le in range(2):
                    mine = slice(le * CAP, (le + 1) * CAP)
                    x_ref[le, at] = picked[mine]
                    xd_ref[le, at] = cut[mine]
                    dy_ref[le, at] = dy[mine]
            for c in leaving(k):
                c.start()
            return carry

        lax.fori_loop(0, 8, column, 0)
        for k in range(8):
            for c in leaving(k):
                c.wait()

    return pl.pallas_call(
        kernel,
        out_shape=(
            sds((2, slots, width), BF16),
            sds((2, slots, piece), BF16),
            sds((2, slots, width), BF16),
        ),
        in_specs=[SMEM_SPEC, VMEM_SPEC] + [ANY_SPEC] * 14,
        out_specs=(ANY_SPEC,) * 3,
        scratch_shapes=[
            pltpu.VMEM((8, planes * length, width), BF16),
            pltpu.VMEM((8, planes * ext, width), BF16),
            pltpu.SemaphoreType.DMA((8, planes)),
            pltpu.SemaphoreType.DMA((8, planes)),
            pltpu.VMEM((2, slots, width), BF16),
            pltpu.VMEM((2, slots, piece), BF16),
            pltpu.VMEM((2, slots, width), BF16),
            pltpu.SemaphoreType.DMA((8, 3)),
        ],
        compiler_params=params(60),
        cost_estimate=cost(8 * planes * 4 * 2 * CAP * length * width, 28 << 20),
        name="dispatch_others",
    )(idx, router_t, *h_pieces, *g_pieces, *corners)


def experts(x, gs, cs, w_gate, w_up, w_down):
    local, slots, width = x.shape
    hidden = w_gate.shape[2]
    fc = 512
    steps = hidden // fc

    def kernel(x_ref, gs_ref, cs_ref, wg_ref, wu_ref, wd_ref,
               a_ref, dg_ref, du_ref, dy_ref, yc_ref, dr_ref, dc_ref, yacc, dracc):
        f = pl.program_id(1)

        @pl.when(f == 0)
        def _():
            weight = cs_ref[0][:, 0:1]
            dy_ref[0] = (weight * gs_ref[0].astype(F32)).astype(BF16)
            yacc[...] = jnp.zeros_like(yacc)
            dracc[...] = jnp.zeros_like(dracc)

        rows, dy = x_ref[0], dy_ref[0]
        wg, wu, wd = wg_ref[0], wu_ref[0], wd_ref[0]
        g = nn(rows, wg)
        u = nn(rows, wu)
        da = nt(dy, wd)
        silu, slope = silu_parts(g)
        a = (silu * u).astype(BF16)
        dg = (da * u * slope).astype(BF16)
        du = (da * silu).astype(BF16)
        a_ref[0] = a
        dg_ref[0] = dg
        du_ref[0] = du
        yacc[...] += nn(a, wd)
        dracc[...] += nt(dg, wg) + nt(du, wu)

        @pl.when(f == steps - 1)
        def _():
            y = yacc[...].astype(BF16).astype(F32)
            weight = cs_ref[0][:, 0:1]
            yc_ref[0] = (weight * y).astype(BF16)
            dr_ref[0] = dracc[...].astype(BF16)
            dc = jnp.sum(gs_ref[0].astype(F32) * y, axis=1, keepdims=True)
            dc_ref[0] = jnp.broadcast_to(dc, (slots, 128))

    def whole(last):
        return pl.BlockSpec((1, slots, last), lambda e, f: (e, 0, 0))

    chunk = pl.BlockSpec((1, slots, fc), lambda e, f: (e, 0, f))
    wide = sds((local, slots, hidden), BF16)
    row = sds((local, slots, width), BF16)
    return pl.pallas_call(
        kernel,
        grid=(local, steps),
        out_shape=(wide, wide, wide, row, row, row, sds((local, slots, 128), F32)),
        in_specs=[
            whole(width),
            whole(width),
            whole(128),
            pl.BlockSpec((1, width, fc), lambda e, f: (e, 0, f)),
            pl.BlockSpec((1, width, fc), lambda e, f: (e, 0, f)),
            pl.BlockSpec((1, fc, width), lambda e, f: (e, f, 0)),
        ],
        out_specs=(chunk, chunk, chunk, whole(width), whole(width), whole(width), whole(128)),
        scratch_shapes=[pltpu.VMEM((slots, width), F32), pltpu.VMEM((slots, width), F32)],
        compiler_params=params(60, ("arbitrary", "arbitrary")),
        cost_estimate=cost(12 * local * slots * width * hidden, 40 << 20),
        name="experts",
    )(x, gs, cs, w_gate, w_up, w_down)


def chip_order(g, i):
    return jnp.where(g < 4, 4, 0) + ((g & 3) ^ (i[0] >> 1))


def whole_block(shape):
    return pl.BlockSpec(shape, lambda g, i: (0,) * len(shape))


def shared_branch(idx, rows, grads, shared, down):
    _, length, width = rows[0].shape
    ext = grads[0].shape[1]
    part = down.shape[0]
    step = width // 8

    def kernel(idx_ref, h_mine, h_other, g_mine, g_other, wg_ref, wu_ref, wd_ref,
               act_ref, gs_ref, gdacc, gsacc, wdown):
        s = pl.program_id(0)

        @pl.when(s == 0)
        def _():
            gdacc[...] = jnp.zeros_like(gdacc)
            gsacc[...] = jnp.zeros_like(gsacc)
            wdown[...] = wd_ref[...].astype(BF16)

        h = jnp.where(s == 0, h_mine[...], h_other[...]).reshape(4 * length, width)
        grad = jnp.where(s == 0, g_mine[...], g_other[...])[:, :length].reshape(4 * length, width)
        gate = nn(h, wg_ref[...])
        up = nn(h, wu_ref[...])
        da = nt(grad, wdown[...])
        silu, slope = silu_parts(gate)
        a = (silu * up).astype(BF16)
        dg = (da * up * slope).astype(BF16)
        du = (da * silu).astype(BF16)
        both = jnp.concatenate([dg, du], axis=1)
        act_ref[:, :, :part] = a.reshape(4, length, part)
        act_ref[:, :, part:] = both.reshape(4, length, 2 * part)
        gdacc[...] += tn(a, grad)
        gsacc[...] += tn(h, both)

        @pl.when(s == 1)
        def _():
            rows, wide = part // 4, 2 * part
            for q in range(4):
                for b in range(2):
                    block = gsacc[(2 * q + b) * step : (2 * q + b + 1) * step, :]
                    gs_ref[q, b * step : (b + 1) * step] = block.astype(BF16)
                low = gdacc[q * rows : (q + 1) * rows, :].astype(BF16)
                rest = [low[: rows // 2, wide:], low[rows // 2 :, wide:]]
                gs_ref[q, 2 * step : 2 * step + rows] = low[:, :wide]
                gs_ref[q, 2 * step + rows :] = jnp.concatenate(rest, axis=1)

    return pl.pallas_call(
        kernel,
        out_shape=(
            sds((8, length, 3 * part), BF16),
            sds((4, 2 * step + 3 * part // 8, 2 * part), BF16),
        ),
        grid_spec=pltpu.PrefetchScalarGridSpec(
            num_scalar_prefetch=1,
            grid=(2,),
            in_specs=[
                whole_block((4, length, width)),
                whole_block((4, length, width)),
                whole_block((4, ext, width)),
                whole_block((4, ext, width)),
                whole_block((width, part)),
                whole_block((width, part)),
                whole_block((part, width)),
            ],
            out_specs=(
                pl.BlockSpec((4, length, 3 * part), lambda g, i: (g, 0, 0)),
                whole_block((4, 2 * step + 3 * part // 8, 2 * part)),
            ),
            scratch_shapes=[
                pltpu.VMEM((part, width), F32),
                pltpu.VMEM((width, 2 * part), F32),
                pltpu.VMEM((part, width), BF16),
            ],
        ),
        compiler_params=params(60, ("arbitrary",)),
        cost_estimate=cost(12 * 8 * length * width * part, 14 << 20),
        name="shared_branch",
    )(idx, *rows, *grads, *shared, down)


def combine(idx, act, hot, yc, dr, dc, shared, down):
    _, length, _ = act.shape
    part, width = down.shape
    ext = length + 16

    def kernel(idx_ref, act_ref, hot_ref, yc_ref, dr_ref, dc_ref, wg_ref, wu_ref, wd_ref,
               out_ref, do_ref, de_ref, wout, wback):
        s = pl.program_id(0)
        i = idx_ref[0]

        @pl.when(s == 0)
        def _():
            wout[:part] = wd_ref[...].astype(BF16)
            wback[:part] = wg_ref[...].T
            wback[part : 2 * part] = wu_ref[...].T

        wout[part:] = yc_ref[...].reshape(2 * CAP, width)
        wback[2 * part :] = dr_ref[...].reshape(2 * CAP, width)
        one = hot_ref[0]
        place = one.T
        act = act_ref[0]
        out = nn(jnp.concatenate([act[:, :part], place], axis=1), wout[...])
        out_ref[0] = out.astype(BF16)
        dh = nn(jnp.concatenate([act[:, part:], place], axis=1), wback[...]).astype(BF16)
        dcv = dc_ref[...].reshape(2 * CAP, 128)[:, 0:1] * one.astype(F32)
        expert = lax.broadcasted_iota(jnp.int32, (16, length), 0)
        dp = jnp.zeros((16, length), F32)
        for le in range(2):
            row = jnp.sum(dcv[le * CAP : (le + 1) * CAP], axis=0, keepdims=True)
            dp = dp + jnp.where(expert == 2 * i + le, row, 0.0)

        def put(ref):
            ref[0, :length] = dh
            ref[0, length:] = jnp.zeros((16, width), BF16)
            ref[0, length:, :length] = dp.astype(BF16)

        @pl.when(s < 4)
        def _():
            put(do_ref)

        @pl.when(s >= 4)
        def _():
            put(de_ref)

    def odd(block):
        return pl.BlockSpec((1,) + block, lambda g, i: (jnp.minimum(g, 3), 0, 0))

    def even(block):
        return pl.BlockSpec((1,) + block, lambda g, i: (jnp.maximum(g - 4, 0), 0, 0))

    def slot_spec(last):
        return pl.BlockSpec((2, CAP, last), lambda g, i: (0, chip_order(g, i), 0))

    def device(g, i):
        return 2 * ((g & 3) ^ (i[0] >> 1)) + ((i[0] & 1) ^ jnp.where(g < 4, 1, 0))

    ext4 = sds((4, ext, width), BF16)
    return pl.pallas_call(
        kernel,
        out_shape=(sds((8, length, width), BF16), ext4, ext4),
        grid_spec=pltpu.PrefetchScalarGridSpec(
            num_scalar_prefetch=1,
            grid=(8,),
            in_specs=[
                pl.BlockSpec((1, length, 3 * part), lambda g, i: (chip_order(g, i), 0, 0)),
                pl.BlockSpec((1, 2 * CAP, length), lambda g, i: (chip_order(g, i), 0, 0)),
                slot_spec(width),
                slot_spec(width),
                slot_spec(128),
                whole_block((width, part)),
                whole_block((width, part)),
                whole_block((part, width)),
            ],
            out_specs=(
                pl.BlockSpec((1, length, width), lambda g, i: (device(g, i), 0, 0)),
                odd((ext, width)),
                even((ext, width)),
            ),
            scratch_shapes=[
                pltpu.VMEM((part + 2 * CAP, width), BF16),
                pltpu.VMEM((2 * part + 2 * CAP, width), BF16),
            ],
        ),
        compiler_params=params(60, ("arbitrary",)),
        cost_estimate=cost(10 * 8 * length * width * part, 18 << 20),
        name="combine",
    )(idx, act, hot, yc, dr, dc, *shared, down)


def attention_backward(idx, tokens, grad, live_row, gain1, gain2, saved, router_t, dh_parts,
                       pieces):
    layout = layout_of(pieces)
    n = len(layout)
    length, width = tokens.shape
    step = width // 8
    cosine, sine = rope_tables(length)
    h1, q, k, v, o, prob, x1, h2 = saved
    total = 4 * width + 128

    def kernel(idx_ref, x_ref, g_ref, lv_ref, g1_ref, g2_ref, cos_ref, sin_ref, h1_ref, q_ref,
               k_ref, v_ref, o_ref, p_ref, x1_ref, h2_ref, wr_ref, d0, d1, d2, d3, *refs):
        piece_refs, refs = refs[:n], refs[n:]
        gt_ref, odd_ref, even_ref, wbuf, dmix, dqkv, gbuf, sems, h1b, qkvb, probs, lsem, psem = refs
        i = idx_ref[0]
        late = [pltpu.make_async_copy(h1_ref, h1b, lsem.at[3])]
        for m, ref in enumerate((q_ref, k_ref, v_ref)):
            late.append(pltpu.make_async_copy(ref, qkvb.at[m], lsem.at[m]))

        def prob_copy(hp):
            pairs = pl.ds(2 * hp, 2)
            return pltpu.make_async_copy(p_ref.at[pairs], probs.at[pairs], psem.at[hp])

        copies = place_copies(i, layout, step, piece_refs, wbuf, sems)
        for c in copies + late:
            c.start()
        for hp in range(HEADS // 2):
            prob_copy(hp).start()
        x1v = x1_ref[...]
        r2 = norm_scale(x1v)
        wr = wr_ref[...]
        pr = router_probs(wr, h2_ref[...])
        came = add([d0[...], d1[...], d2[...], d3[...]])
        dp = came[length:, :length] * lv_ref[...]
        dl = (pr * (dp - jnp.sum(pr * dp, axis=0, keepdims=True))).astype(BF16)
        router_grad = nn(dl, h2_ref[...])
        dh2 = came[:length] + tn(dl, wr)
        gain2_grad = jnp.sum(dh2 * x1v * r2, axis=0, keepdims=True)
        weighted = dh2 * g2_ref[...]
        inner = jnp.mean(x1v * weighted, axis=-1, keepdims=True)
        dx1 = g_ref[...].astype(F32) + r2 * weighted - x1v * (r2 * r2 * r2) * inner
        da = dx1.astype(BF16)
        for c in copies:
            c.wait()
        gbuf[:, 3 * width : 4 * width] = tn(o_ref[...], da).astype(BF16)
        dmix[...] = nt(da, wbuf[:, 3 * width : 4 * width]).astype(BF16)
        first = lax.broadcasted_iota(jnp.int32, (length, 128), 1) < HEAD_DIM

        for c in late:
            c.wait()

        def pair(hp, carry):
            prob_copy(hp).wait()
            at = pl.multiple_of(hp * 128, 128)
            qv, kv, vv = (qkvb[m, :, pl.ds(at, 128)] for m in range(3))
            dov = dmix[:, pl.ds(at, 128)]
            p = probs[pl.ds(2 * hp, 2)]
            dos = split_heads(dov, first)
            dp = nt(dos, vv).reshape(2, length, length)
            dv = tn(p.astype(BF16).reshape(2 * length, length), dos)
            ds = p * (dp - jnp.sum(p * dp, axis=-1, keepdims=True))
            ds = (ds * SCALE).astype(BF16)
            dq = nn(jnp.concatenate([ds[0], ds[1]], axis=1), split_heads(kv, first))
            dk = tn(ds.reshape(2 * length, length), split_heads(qv, first))
            cosv, sinv = cos_ref[...], sin_ref[...]
            dqkv[:, pl.ds(at, 128)] = (dq * cosv - half_swap(dq) * sinv).astype(BF16)
            dqkv[:, pl.ds(at + width, 128)] = (dk * cosv - half_swap(dk) * sinv).astype(BF16)
            dqkv[:, pl.ds(at + 2 * width, 128)] = dv.astype(BF16)
            return carry

        lax.fori_loop(0, HEADS // 2, pair, 0)
        gbuf[:, : 3 * width] = tn(h1b[...], dqkv[...]).astype(BF16)
        dh1 = nt(dqkv[...], wbuf[:, : 3 * width])
        x = x_ref[...].astype(F32)
        r1 = norm_scale(x)
        gain1_grad = jnp.sum(dh1 * x * r1, axis=0, keepdims=True)
        weighted = dh1 * g1_ref[...]
        inner = jnp.mean(x * weighted, axis=-1, keepdims=True)
        gt_ref[...] = (dx1 + r1 * weighted - x * (r1 * r1 * r1) * inner).astype(BF16)
        small = jnp.concatenate(
            [router_grad, gain1_grad, gain2_grad, jnp.zeros((110, width), F32)], axis=0
        )
        gbuf[:, 4 * width :] = small.T.astype(BF16)
        leaving = []
        for kk in range(8):
            rows = gbuf.at[pl.ds(pl.multiple_of((i ^ kk) * step, 16), step), :]
            ref = odd_ref if kk % 2 else even_ref
            leaving.append(pltpu.make_async_copy(rows, ref.at[kk // 2], psem.at[8 + kk]))
        for c in leaving:
            c.start()
        for c in leaving:
            c.wait()

    blocks = sds((4, step, total), BF16)
    return pl.pallas_call(
        kernel,
        out_shape=(sds((length, width), BF16), blocks, blocks),
        in_specs=[SMEM_SPEC] + [VMEM_SPEC] * 7 + [ANY_SPEC] * 4 + [VMEM_SPEC, ANY_SPEC]
        + [VMEM_SPEC] * 7 + [ANY_SPEC] * n,
        out_specs=(VMEM_SPEC, ANY_SPEC, ANY_SPEC),
        scratch_shapes=[
            pltpu.VMEM((width, pieces[0][2].shape[1]), BF16),
            pltpu.VMEM((length, width), BF16),
            pltpu.VMEM((length, 3 * width), BF16),
            pltpu.VMEM((width, total), BF16),
            pltpu.SemaphoreType.DMA((n,)),
            pltpu.VMEM((length, width), BF16),
            pltpu.VMEM((3, length, width), BF16),
            pltpu.VMEM((HEADS, length, length), F32),
            pltpu.SemaphoreType.DMA((4,)),
            pltpu.SemaphoreType.DMA((16,)),
        ],
        compiler_params=params(60),
        cost_estimate=cost(20 * length * width * width, 24 << 20),
        name="attention_backward",
    )(idx, tokens, grad, live_row, gain1, gain2, cosine, sine, h1, q, k, v, o, prob, x1, h2,
      router_t, *dh_parts, *[p for _, _, p in pieces])


def expert_grads(idx, e, base, steps, own, others, weights, done=()):
    w_gate, w_up, w_down = weights
    a, dg, du, dy, xd = own
    x_o, dy_o, xd_o = others
    local, slots, hidden = a.shape
    many = x_o.shape[1]
    width = x_o.shape[2]
    piece = xd.shape[2]
    fc = 512
    tile = TILE

    def kernel(idx_ref, a_ref, dg_ref, du_ref, dy_ref, xd_ref, xo_ref, dyo_ref, xdo_ref,
               wg_ref, wu_ref, wd_ref, *refs):
        gg_ref, gu_ref, gd_ref, ao, dgo, duo, gds, gsem = refs[len(done) :]
        f = pl.program_id(0)
        wg, wu, wd = wg_ref[0], wu_ref[0], wd_ref[0]

        def rows(t, carry):
            at = pl.ds(pl.multiple_of(t * tile, tile), tile)
            g = nn(xo_ref[0, at], wg)
            u = nn(xo_ref[0, at], wu)
            da = nt(dyo_ref[0, at], wd)
            silu, slope = silu_parts(g)
            ao[at] = (silu * u).astype(BF16)
            dgo[at] = (da * u * slope).astype(BF16)
            duo[at] = (da * silu).astype(BF16)
            return carry

        lax.fori_loop(0, many // tile, rows, 0)
        gg_ref[0] = tn(xdo_ref[0], dgo[...]) + tn(xd_ref[0], dg_ref[0])
        gu_ref[0] = tn(xdo_ref[0], duo[...]) + tn(xd_ref[0], du_ref[0])

        @pl.when(base + f == idx_ref[1])
        def _():
            gds[...] = tn(ao[...], dyo_ref[0]) + tn(a_ref[0], dy_ref[0])
            copy = pltpu.make_async_copy(gds, gd_ref.at[e], gsem)
            copy.start()
            copy.wait()

    def mine(block):
        return pl.BlockSpec((1,) + block, lambda f, i: (e, 0, 0))

    def chunk(rows):
        return pl.BlockSpec((1, rows, fc), lambda f, i: (e, 0, base + f))

    return pl.pallas_call(
        kernel,
        out_shape=(
            sds((local, piece, hidden), F32),
            sds((local, piece, hidden), F32),
            sds((local, fc, width), F32),
        ),
        grid_spec=pltpu.PrefetchScalarGridSpec(
            num_scalar_prefetch=1,
            grid=(steps,),
            in_specs=[
                pl.BlockSpec((1, slots, fc), lambda f, i: (e, 0, i[1])),
                chunk(slots),
                chunk(slots),
                mine((slots, width)),
                mine((slots, piece)),
                mine((many, width)),
                mine((many, width)),
                mine((many, piece)),
                chunk(width),
                chunk(width),
                pl.BlockSpec((1, fc, width), lambda f, i: (e, base + f, 0)),
            ]
            + [ANY_SPEC] * len(done),
            out_specs=(chunk(piece), chunk(piece), ANY_SPEC),
            scratch_shapes=[pltpu.VMEM((many, fc), BF16) for _ in range(3)]
            + [pltpu.VMEM((fc, width), F32), pltpu.SemaphoreType.DMA],
        ),
        compiler_params=params(60, ("arbitrary",)),
        cost_estimate=cost(steps * fc * width * (6 * many + 2 * (many + slots)), 15 << 20),
        input_output_aliases={12 + m: m for m in range(len(done))},
        name="expert_grads",
    )(idx, a, dg, du, dy, xd, x_o, dy_o, xd_o, w_gate, w_up, w_down, *done)


def finish_shared(blocks, quarters, width):
    n, step, both = blocks.shape
    part, rows = both // 2, both // 8

    def kernel(s_ref, q_ref, gate_ref, up_ref, down_ref):
        for k in range(n):
            block = s_ref[k].astype(F32)
            gate_ref[:, k * part : (k + 1) * part] = block[:, :part]
            up_ref[:, k * part : (k + 1) * part] = block[:, part:]
        for q in range(4):
            low = q_ref[q, 2 * step :].astype(F32)
            at, half = q * rows, rows // 2
            down_ref[at : at + rows, :both] = low[:rows]
            down_ref[at : at + half, both:] = low[rows:, :part]
            down_ref[at + half : at + rows, both:] = low[rows:, part:]

    wide = sds((step, n * part), F32)
    return pl.pallas_call(
        kernel,
        out_shape=(wide, wide, sds((4 * rows, width), F32)),
        in_specs=[VMEM_SPEC] * 2,
        out_specs=(VMEM_SPEC,) * 3,
        compiler_params=params(60),
        name="finish_shared",
    )(blocks, quarters)


def finish_attention(idx, parts, width, experts_all):
    rows, total = parts[0].shape
    rest = total - width

    def kernel(idx_ref, s0, s1, s2, s3, q_ref, k_ref, v_ref, o_ref, r_ref, a_ref, f_ref, small):
        z = idx_ref[1]
        for r, s in enumerate((s0, s1, s2, s3)):
            small[(z - r + 4) & 3] = s[:, width:].astype(F32)
            for m, ref in enumerate((q_ref, k_ref, v_ref, o_ref)):

                @pl.when(((z - r + 4) & 3) == m)
                def _(ref=ref, s=s):
                    ref[...] = s[:, :width].astype(F32)

        low = small[0]
        square = jnp.concatenate([low, jnp.zeros((rows, 128 - rest), F32)], axis=1)
        square = jnp.concatenate([square, jnp.zeros((128 - rows, 128), F32)], axis=0).T
        r_ref[...] = square[:experts_all, :rows]
        a_ref[...] = square[experts_all : experts_all + 1, :rows]
        f_ref[...] = square[experts_all + 1 : experts_all + 2, :rows]

    flat = sds((rows, width), F32)
    line = sds((1, rows), F32)
    return pl.pallas_call(
        kernel,
        out_shape=(flat, flat, flat, flat, sds((experts_all, rows), F32), line, line),
        in_specs=[SMEM_SPEC] + [VMEM_SPEC] * 4,
        out_specs=(VMEM_SPEC,) * 7,
        scratch_shapes=[pltpu.VMEM((4, rows, rest), F32)],
        compiler_params=params(60),
        name="finish_attention",
    )(idx, *parts)


def on_device(
    tokens,
    segment_ids,
    padding,
    routes,
    w_query,
    w_key,
    w_value,
    w_out,
    w_router,
    shared_gate,
    shared_up,
    shared_down,
    gain_attn,
    gain_ffn,
    expert_gate,
    expert_up,
    expert_down,
    cotangent,
):
    length, width = tokens.shape
    planes = lax.axis_size("dp")
    i = lax.axis_index("expert").astype(jnp.int32)
    z = lax.axis_index("dp").astype(jnp.int32)
    idx = jnp.stack([i, z])
    step = width // 8
    part = shared_down.shape[0]
    spread = planes == 4

    attn_shard = pack_shard([w_query, w_key, w_value, w_out], w_router)

    live_row = padding.astype(F32)
    meta = jnp.concatenate([routes[:, 0], routes[:, 1], padding[0]]).astype(BF16)[None, :]
    grad_ext = jnp.concatenate([cotangent, meta, jnp.zeros((15, width), BF16)], axis=0)
    ext = grad_ext.shape[0]

    def others(columns):
        at = [(z - r) % planes for r in (1, 2, 3)]
        return jnp.concatenate([lax.dynamic_index_in_dim(columns, a, 0, False) for a in at], axis=0)

    def copies(rows):
        return jnp.broadcast_to(rows[None], (planes,) + rows.shape)

    def columns(blocks):
        return lax.all_to_all(blocks, "dp", split_axis=0, concat_axis=0, tiled=True)

    def dp_gather(rows):
        return lax.all_gather(rows, "dp", axis=0)

    g_mine = lax.all_gather(grad_ext, "expert", axis=0, axis_index_groups=same_core())
    g_far = [shift(grad_ext, k) for k in (1, 2, 3)] if spread else []
    attn_pieces = relay_gather(attn_shard)

    side = jnp.stack([shared_gate.astype(BF16), shared_up.astype(BF16)])
    side = side.reshape(2, step, 8, part).transpose(2, 0, 1, 3)
    side = after(side, attn_pieces[3][2], attn_pieces[4][2])
    side = lax.all_to_all(side, "expert", split_axis=0, concat_axis=0, tiled=True)

    gain1, gain2 = gain_attn[None, :], gain_ffn[None, :]
    *saved, router_t, h2_copies = attention_forward(
        idx, after(tokens, g_far), segment_ids, live_row, gain1, gain2, attn_pieces,
    )
    x1, h2 = saved[6], saved[7]

    g_plane = [g_mine, swap(g_mine, 1)]
    if spread:
        g_far = jnp.concatenate(after(g_far, h2), axis=0)
    side = after(side, h2)
    h_mine = chips_exchange(after(h2_copies, side))
    h_plane = [h_mine, swap(h_mine, 1)]
    if spread:
        h_columns = dp_gather(h2)
        at = (i // 2) ^ 3
        corner = [
            lax.dynamic_index_in_dim(rows, at, 0, False) for rows in after((g_mine, h_mine), h_plane)
        ]
        corner = dp_gather(jnp.concatenate(corner, axis=0))
        g_far = after(g_far, h_plane)
        g_far = [g_far, swap(g_far, 2), swap(g_far, 4)]

    cut = width // 4
    x_own, xd_own, gs_own, cs_own, hot = dispatch_plane(
        idx, router_t, h_plane, g_plane, cut
    )

    weights = (expert_gate, expert_up, expert_down)
    a, dg, du, dy, yc, dr, dc = experts(x_own, gs_own, cs_own, *weights)
    shared_w = [after(side, yc)[:, m].reshape(width, part) for m in range(2)]
    if spread:
        g_far, h_columns = after((g_far, h_columns), yc)
        shared_w = after(shared_w, g_far)
        g_far = both_cores(g_far)
        h_far = others(h_columns)
        h_far = [h_far, swap(h_far, 2), swap(h_far, 4)]
    act, side = shared_branch(idx, h_plane, g_plane, shared_w, shared_down)
    if spread:
        side = lax.psum_scatter(side, "dp", scatter_dimension=0)
    else:
        side = lax.psum(side, "dp")

    def exchanged(quarters):
        blocks = quarters[:, : 2 * step].reshape(8, step, 2 * part)
        return lax.all_to_all(blocks, "expert", split_axis=0, concat_axis=0, tiled=True)

    out_shares, dh_other, dh_mine = combine(
        idx, act, hot, yc, dr, dc, shared_w, shared_down
    )
    if spread:
        h_far = after(h_far, dh_other)
        dh_other = after(dh_other, h_far)
        h_far = both_cores(h_far)
    dh_came = swap(dh_other, 1)
    dh_sums = plane_near(dh_mine, dh_came)
    dh_parts = plane_far(dh_sums)
    if spread:
        h_far, g_far, corner = after((h_far, g_far, corner), dh_sums)
        corners = both_cores([others(corner)])
        x_far, xd_far, dy_far = dispatch_others(idx, router_t, h_far, g_far, corners, 3, cut)
        dh_parts = after(dh_parts, x_far)
    out_shares = out_shares.reshape(8 * length, width)
    grad_tokens, att_other, att_mine = attention_backward(
        idx, tokens, cotangent, live_row, gain1, gain2, saved, router_t, dh_parts, attn_pieces,
    )
    att_came = swap(att_other, 1)
    if spread:
        side = dp_gather(after(side, att_mine))
    att_sums = plane_near(att_mine, att_came)
    att_parts = plane_far(att_sums)
    def att_quarters(parts):
        att = add(parts).astype(BF16)
        small = att[:, 4 * width :]
        return jnp.stack(
            [
                jnp.concatenate(
                    [att[:, m * width : (m + 1) * width], small[:, 32 * m : 32 * (m + 1)]], axis=1
                )
                for m in range(4)
            ]
        )

    if spread:
        xs = (x_far, dy_far, xd_far)
        own = (a, dg, du, dy, xd_own)
        chunks = expert_gate.shape[2] // 512
        done = expert_grads(idx, 0, 0, chunks, own, after(xs, att_sums), weights)
        att_parts = after(att_parts, done)
        out_share = lax.psum_scatter(
            after(out_shares, att_sums), "expert", scatter_dimension=0, tiled=True
        )
        xs = after(xs, att_parts)
        att_scattered = dp_scatter(att_quarters(att_parts))
        done = expert_grads(idx, 1, 0, chunks // 2, own, xs, weights, done)
        att_scattered, side = after((att_scattered, side), done)
        moved = exchanged(side)
        xs = after(xs, att_scattered)
        att_spread = dp_spread(att_scattered)
        done = expert_grads(idx, 1, chunks // 2, chunks // 2, own, xs, weights, done)
        moved, side, att_spread, out_share = after((moved, side, att_spread, out_share), done)
        output = (x1 + out_share.astype(F32)).astype(BF16)
        g_gate, g_up, g_down = done
        order = idx
    else:
        att_spread = dp_whole(att_quarters(att_parts))
        moved = exchanged(side)
        out_share = lax.psum_scatter(out_shares, "expert", scatter_dimension=0, tiled=True)
        output = (x1 + out_share.astype(F32)).astype(BF16)
        order = idx * jnp.array([1, 0], jnp.int32)

        def scattered(left, right):
            local = jnp.einsum("end,enf->edf", left, right, preferred_element_type=F32)
            return lax.psum_scatter(
                local.astype(BF16), "dp", scatter_dimension=1, tiled=True
            ).astype(F32)

        g_gate, g_up, g_down = scattered(x_own, dg), scattered(x_own, du), scattered(a, dy)

    experts_all = w_router.shape[1]
    gq, gk, gv, go, g_router, g_gain1, g_gain2 = finish_attention(order, att_spread, width, experts_all)
    g_sgate, g_sup, g_sdown = finish_shared(moved, side, width)
    return (
        output,
        grad_tokens,
        gq,
        gk,
        gv,
        go,
        g_router.T,
        g_sgate,
        g_sup,
        g_sdown,
        g_gain1.reshape(step),
        g_gain2.reshape(step),
        g_gate,
        g_up,
        g_down,
    )


def solution(mesh):
    both = P(("dp", "expert"), None)
    one = P("expert", None)
    three = P("expert", None, None)
    sliced = P("expert", "dp", None)
    return jax.shard_map(
        on_device,
        mesh=mesh,
        in_specs=(both,) * 4 + (one,) * 8 + (P(), P()) + (three,) * 3 + (both,),
        out_specs=(both, both) + (one,) * 8 + (P("expert"), P("expert")) + (sliced,) * 3,
        check_vma=False,
    )
```

```python
import numpy as np

import jax
import jax.numpy as jnp
from jax import lax
from jax.experimental import pallas as pl
from jax.experimental.pallas import tpu as pltpu
from jax.sharding import PartitionSpec as P

HEADS = 12
HEAD_DIM = 64
CAP = 64
TILE = 1536
UNROLL = 2
EPS = 1e-06
ROPE_BASE = 10000.0
MASKED = -1e30
SCALE = HEAD_DIM**-0.5
F32 = jnp.float32
BF16 = jnp.bfloat16
MIB = 1 << 20
VMEM_SPEC = pl.BlockSpec(memory_space=pltpu.VMEM)
SMEM_SPEC = pl.BlockSpec(memory_space=pltpu.SMEM)
ANY_SPEC = pl.BlockSpec(memory_space=pl.ANY)


def nn(a, b):
    return jnp.dot(a, b, preferred_element_type=F32)


def nt(a, b):
    return lax.dot_general(a, b, (((1,), (1,)), ((), ())), preferred_element_type=F32)


def tn(a, b):
    return lax.dot_general(a, b, (((0,), (0,)), ((), ())), preferred_element_type=F32)


def sds(shape, dtype):
    return jax.ShapeDtypeStruct(shape, dtype)


def cost(flops, nbytes):
    return pl.CostEstimate(
        flops=int(flops * 0.02), bytes_accessed=int(nbytes * 0.02), transcendentals=0
    )


def params(mib, semantics=None):
    return pltpu.CompilerParams(vmem_limit_bytes=mib * MIB, dimension_semantics=semantics)


def swap(x, k):
    n = lax.axis_size("expert")
    return lax.ppermute(x, "expert", [(j, j ^ k) for j in range(n)])


def shift(x, k):
    n = lax.axis_size("dp")
    return lax.ppermute(x, "dp", [(j, (j + k) % n) for j in range(n)])


def after(value, *first):
    return lax.optimization_barrier((value, first))[0]


def relay_gather(x):
    half = x.shape[0] // 32 * 16
    a, b = swap(x, 2), swap(x, 4)
    d0, d1 = swap(a[:half], 4), swap(b[half:], 2)
    near = [(0, 0, x), (2, 0, a), (4, 0, b), (6, 0, d0), (6, half, d1)]
    return near + [(k + 1, at, swap(piece, 1)) for k, at, piece in near]


def same_core():
    n = lax.axis_size("expert")
    return [list(range(c, n, 2)) for c in range(2)]


def chips_exchange(blocks):
    return lax.all_to_all(
        blocks, "expert", split_axis=0, concat_axis=0, tiled=True, axis_index_groups=same_core()
    )


def both_cores(near):
    other = [swap(p, 1) for p in near]
    return [p for pair in zip(near, other) for p in pair]


def plane_near(even, came):
    return [add([even[j], came[j]]).astype(even.dtype) for j in range(4)]


def plane_far(sums):
    return [sums[0], swap(sums[1], 2), swap(sums[2], 4), swap(sums[3], 6)]


def dp_scatter(quarters):
    z = lax.axis_index("dp")
    parts = [lax.dynamic_index_in_dim(quarters, (z + k) % 4, 0, False) for k in range(4)]
    return [parts[0]] + [shift(parts[k], k) for k in (1, 2, 3)]


def dp_spread(parts):
    total = add(parts).astype(parts[0].dtype)
    return [total] + [shift(total, k) for k in (1, 2, 3)]


def dp_whole(quarters):
    whole = lax.psum(quarters, "dp")
    return [whole[0], whole[3], whole[2], whole[1]]


def add(parts):
    total = parts[0].astype(F32)
    for p in parts[1:]:
        total = total + p.astype(F32)
    return total


def norm_scale(values):
    return lax.rsqrt(jnp.mean(values * values, axis=-1, keepdims=True) + EPS)


def silu_parts(gate):
    logistic = 0.5 * jnp.tanh(0.5 * gate) + 0.5
    silu = gate * logistic
    return silu, logistic + silu * (1.0 - logistic)


def split_heads(x, first):
    zero = jnp.zeros_like(x)
    return jnp.concatenate([jnp.where(first, x, zero), jnp.where(first, zero, x)], axis=0)


def half_swap(x):
    lane = lax.broadcasted_iota(jnp.int32, x.shape, 1)
    half = HEAD_DIM // 2
    return jnp.where(
        lane % HEAD_DIM < half, pltpu.roll(x, x.shape[1] - half, 1), pltpu.roll(x, half, 1)
    )


def place_copies(i, layout, step, refs, target, sems):
    copies = []
    for n, ((k, at, rows), ref) in enumerate(zip(layout, refs)):
        start = pl.multiple_of((i ^ k) * step + at, 16)
        copies.append(pltpu.make_async_copy(ref, target.at[pl.ds(start, rows), :], sems.at[n]))
    return copies


def layout_of(pieces):
    return tuple((k, at, piece.shape[0]) for k, at, piece in pieces)


def rope_tables(length):
    half = HEAD_DIM // 2
    frequency = (ROPE_BASE ** (-(2.0 * np.arange(half, dtype=np.float32)) / HEAD_DIM)).astype(
        np.float32
    )
    angles = (np.arange(length, dtype=np.float32)[:, None] * frequency[None, :]).astype(np.float32)
    cosine, sine = np.cos(angles), np.sin(angles)
    return (
        np.concatenate([cosine] * 4, 1).astype(np.float32),
        np.concatenate([-sine, sine, -sine, sine], 1).astype(np.float32),
    )


def pack_shard(projections, router):
    rows, width = projections[0].shape
    n = len(projections)

    def kernel(*refs):
        out = refs[-1]
        for m in range(n):
            out[:, m * width : (m + 1) * width] = refs[m][...].astype(BF16)
        lines = jnp.concatenate(
            [refs[n][...], jnp.zeros((router.shape[0], 128 - rows), F32)], axis=1
        )
        lines = jnp.concatenate([lines, jnp.zeros((128 - router.shape[0], 128), F32)], axis=0)
        out[:, n * width :] = lines.T[:rows].astype(BF16)

    return pl.pallas_call(
        kernel,
        out_shape=sds((rows, n * width + 128), BF16),
        in_specs=[VMEM_SPEC] * (n + 1),
        out_specs=VMEM_SPEC,
        compiler_params=params(60),
        cost_estimate=cost(1, 1 << 20),
        name="pack_shard",
    )(*projections, router)


def pack_side(gate, up, part):
    step, wide = gate.shape

    def kernel(g_ref, u_ref, out_ref):
        for k in range(wide // part):
            out_ref[k, 0] = g_ref[:, k * part : (k + 1) * part].astype(BF16)
            out_ref[k, 1] = u_ref[:, k * part : (k + 1) * part].astype(BF16)

    return pl.pallas_call(
        kernel,
        out_shape=sds((wide // part, 2, step, part), BF16),
        in_specs=[VMEM_SPEC] * 2,
        out_specs=VMEM_SPEC,
        compiler_params=params(60),
        cost_estimate=cost(1, 1 << 20),
        name="pack_side",
    )(gate, up)


def attention_forward(idx, tokens, seg_row, live_row, gain1, gain2, pieces):
    layout = layout_of(pieces)
    n = len(layout)
    length, width = tokens.shape
    step = width // 8
    cosine, sine = rope_tables(length)

    def kernel(idx_ref, x_ref, sr_ref, lv_ref, g1_ref, g2_ref, cos_ref, sin_ref, *refs):
        piece_refs, refs = refs[:n], refs[n:]
        h1_ref, q_ref, k_ref, v_ref, o_ref, p_ref, x1_ref, h2_ref, wr_ref, h4_ref = refs[:10]
        wbuf, pre, probs, sems, psem = refs[10:]
        copies = place_copies(idx_ref[0], layout, step, piece_refs, wbuf, sems)
        for c in copies:
            c.start()
        x = x_ref[...].astype(F32)
        h1 = (x * norm_scale(x) * g1_ref[...]).astype(BF16)
        h1_ref[...] = h1
        row = lax.broadcasted_iota(jnp.int32, (length, length), 0)
        col = lax.broadcasted_iota(jnp.int32, (length, length), 1)
        seg = sr_ref[...].astype(F32)
        seg_col = jnp.broadcast_to(seg, (8, length)).T[:, 0:1]
        allowed = (col == row) | ((col <= row) & (seg == seg_col) & (lv_ref[...] > 0.0))
        bias = jnp.where(allowed, 0.0, MASKED)
        for c in copies:
            c.wait()
        pre[...] = nn(h1, wbuf[:, : 3 * width])
        first = lax.broadcasted_iota(jnp.int32, (length, 128), 1) < HEAD_DIM

        def pair(hp, carry):
            at = pl.multiple_of(hp * 128, 128)
            qp = pre[:, pl.ds(at, 128)]
            kp = pre[:, pl.ds(at + width, 128)]
            v = pre[:, pl.ds(at + 2 * width, 128)].astype(BF16)
            cosv, sinv = cos_ref[...], sin_ref[...]
            q = (qp * cosv + half_swap(qp) * sinv).astype(BF16)
            k = (kp * cosv + half_swap(kp) * sinv).astype(BF16)
            q_ref[:, pl.ds(at, 128)] = q
            k_ref[:, pl.ds(at, 128)] = k
            v_ref[:, pl.ds(at, 128)] = v
            scores = nt(split_heads(q, first), k) * SCALE
            scores = scores.reshape(2, length, length) + bias
            e = jnp.exp(scores - jnp.max(scores, axis=-1, keepdims=True))
            p = e / jnp.sum(e, axis=-1, keepdims=True)
            probs[pl.ds(2 * hp, 2)] = p
            pltpu.make_async_copy(
                probs.at[pl.ds(2 * hp, 2)], p_ref.at[pl.ds(2 * hp, 2)], psem.at[hp]
            ).start()
            low = p.astype(BF16)
            mixed = nn(jnp.concatenate([low[0], low[1]], axis=1), split_heads(v, first))
            o_ref[:, pl.ds(at, 128)] = mixed.astype(BF16)
            return carry

        lax.fori_loop(0, HEADS // 2, pair, 0, unroll=UNROLL)
        x1 = x + nn(o_ref[...], wbuf[:, 3 * width : 4 * width])
        x1_ref[...] = x1
        h2 = (x1 * norm_scale(x1) * g2_ref[...]).astype(BF16)
        h2_ref[...] = h2
        for chip in range(4):
            h4_ref[chip] = h2
        wr_ref[...] = wbuf[:, 4 * width :].astype(F32).T[:16].astype(BF16)
        for hp in range(HEADS // 2):
            pltpu.make_async_copy(
                probs.at[pl.ds(2 * hp, 2)], p_ref.at[pl.ds(2 * hp, 2)], psem.at[hp]
            ).wait()

    flat = sds((length, width), BF16)
    return pl.pallas_call(
        kernel,
        out_shape=(
            flat, flat, flat, flat, flat,
            sds((HEADS, length, length), F32),
            sds((length, width), F32),
            flat,
            sds((16, width), BF16),
            sds((4, length, width), BF16),
        ),
        in_specs=[SMEM_SPEC] + [VMEM_SPEC] * 7 + [ANY_SPEC] * n,
        out_specs=(VMEM_SPEC,) * 5 + (ANY_SPEC,) + (VMEM_SPEC,) * 4,
        scratch_shapes=[
            pltpu.VMEM((width, pieces[0][2].shape[1]), BF16),
            pltpu.VMEM((length, 3 * width), F32),
            pltpu.VMEM((HEADS, length, length), F32),
            pltpu.SemaphoreType.DMA((n,)),
            pltpu.SemaphoreType.DMA((HEADS // 2,)),
        ],
        compiler_params=params(60),
        cost_estimate=cost(8 * length * width * width, 12 << 20),
        name="attention_forward",
    )(idx, tokens, seg_row, live_row, gain1, gain2, cosine, sine,
      *[p for _, _, p in pieces])


def route_rows(meta, prob, le, i, upper, length):
    expert = (2 * i + le).astype(F32)
    hit = (meta[:, :length] == expert) | (meta[:, length : 2 * length] == expert)
    hot = jnp.where(hit, 1.0, 0.0)
    rank = nn(jnp.broadcast_to(hot, (16, length)).astype(BF16), upper)[0:1]
    slot = lax.broadcasted_iota(jnp.int32, (CAP, length), 0).astype(F32) + 1.0
    one = jnp.where((slot == rank) & hit, 1.0, 0.0)
    which = lax.broadcasted_iota(jnp.int32, prob.shape, 0) == 2 * i + le
    weight = jnp.sum(jnp.where(which, prob, 0.0), axis=0, keepdims=True)
    return one, weight * meta[:, 2 * length :]


def router_probs(router_t, rows):
    logits = nt(router_t, rows)
    e = jnp.exp(logits - jnp.max(logits, axis=0, keepdims=True))
    return e / jnp.sum(e, axis=0, keepdims=True)


def upper_ones(length):
    return jnp.where(
        lax.broadcasted_iota(jnp.int32, (length, length), 0)
        <= lax.broadcasted_iota(jnp.int32, (length, length), 1),
        1.0,
        0.0,
    ).astype(BF16)


def dispatch_plane(idx, router_t, rows, grads, piece):
    _, length, width = rows[0].shape
    slots = 8 * CAP
    ext = length + 16

    def kernel(idx_ref, wr_ref, *refs):
        hp, gp, refs = refs[:2], refs[2:4], refs[4:]
        x_ref, xd_ref, gs_ref, cs_ref, hot_ref, hall, gall, sems = refs
        i = idx_ref[0]
        copies = []
        for c in range(2):
            copies.append(pltpu.make_async_copy(hp[c], hall.at[pl.ds(4 * c, 4)], sems.at[c]))
            copies.append(pltpu.make_async_copy(gp[c], gall.at[pl.ds(4 * c, 4)], sems.at[2 + c]))
        for c in copies:
            c.start()
        upper = upper_ones(length)
        turn = (width - idx_ref[1] * piece) % width
        for c in copies:
            c.wait()

        def sequences(pair, carry):
            for k in (2 * pair, 2 * pair + 1):
                h = hall[k]
                prob = router_probs(wr_ref[...], h)
                meta = gall[k, length:ext][0:1].astype(F32)
                at = pl.multiple_of(k * CAP, CAP)
                ones = []
                for le in range(2):
                    one, weight = route_rows(meta, prob, le, i, upper, length)
                    col = jnp.sum(one * weight, axis=1, keepdims=True)
                    cs_ref[le, pl.ds(at, CAP), :] = jnp.broadcast_to(col, (CAP, 128))
                    ones.append(one.astype(BF16))
                hot = jnp.concatenate(ones, axis=0)
                hot_ref[k] = hot
                picked = nn(hot, h)
                cut = pltpu.roll(picked, turn, 1)[:, :piece].astype(BF16)
                picked = picked.astype(BF16)
                grads = nn(hot, gall[k, 0:length]).astype(BF16)
                for le in range(2):
                    mine = slice(le * CAP, (le + 1) * CAP)
                    x_ref[le, pl.ds(at, CAP), :] = picked[mine]
                    xd_ref[le, pl.ds(at, CAP), :] = cut[mine]
                    gs_ref[le, pl.ds(at, CAP), :] = grads[mine]
            return carry

        lax.fori_loop(0, 4, sequences, 0)

    return pl.pallas_call(
        kernel,
        out_shape=(
            sds((2, slots, width), BF16),
            sds((2, slots, piece), BF16),
            sds((2, slots, width), BF16),
            sds((2, slots, 128), F32),
            sds((8, 2 * CAP, length), BF16),
        ),
        in_specs=[SMEM_SPEC, VMEM_SPEC] + [ANY_SPEC] * 4,
        out_specs=(VMEM_SPEC,) * 5,
        scratch_shapes=[
            pltpu.VMEM((8, length, width), BF16),
            pltpu.VMEM((8, ext, width), BF16),
            pltpu.SemaphoreType.DMA((4,)),
        ],
        compiler_params=params(60),
        cost_estimate=cost(8 * 4 * 2 * CAP * length * width, 16 << 20),
        name="dispatch_plane",
    )(idx, router_t, *rows, *grads)


def dispatch_others(idx, router_t, h_pieces, g_pieces, corners, planes, piece):
    width = h_pieces[0].shape[1]
    length = h_pieces[0].shape[0] // planes
    ext = length + 16
    slots = 8 * planes * CAP

    def kernel(idx_ref, wr_ref, *refs):
        hp, gp, both, refs = refs[:6], refs[6:12], refs[12:14], refs[14:]
        x_out, xd_out, dy_out, hall, gall, hsems, gsems, x_ref, xd_ref, dy_ref, osems = refs
        i = idx_ref[0]

        def leaving(k):
            rows = pl.ds(pl.multiple_of(k * planes * CAP, CAP), planes * CAP)
            for m, (a, b) in enumerate(((x_ref, x_out), (xd_ref, xd_out), (dy_ref, dy_out))):
                yield pltpu.make_async_copy(a.at[:, rows], b.at[:, rows], osems.at[k, m])

        def copies(k):
            if k < 6:
                yield pltpu.make_async_copy(hp[k], hall.at[k], hsems.at[k, 0])
                yield pltpu.make_async_copy(gp[k], gall.at[k], gsems.at[k, 0])
                return
            for s in range(planes):
                plane = (idx_ref[1] - s + 3) & 3
                yield pltpu.make_async_copy(
                    both[k - 6].at[plane, pl.ds(0, ext)],
                    gall.at[k, pl.ds(s * ext, ext)],
                    gsems.at[k, s],
                )
                yield pltpu.make_async_copy(
                    both[k - 6].at[plane, pl.ds(ext, length)],
                    hall.at[k, pl.ds(s * length, length)],
                    hsems.at[k, s],
                )

        for k in range(8):
            for c in copies(k):
                c.start()
        upper = upper_ones(length)
        turn = (width - idx_ref[1] * piece) % width

        def column(k, carry):
            @pl.when(k < 6)
            def _():
                pltpu.make_async_copy(hall.at[k], hall.at[k], hsems.at[k, 0]).wait()
                pltpu.make_async_copy(gall.at[k], gall.at[k], gsems.at[k, 0]).wait()

            @pl.when(k >= 6)
            def _():
                for s in range(planes):
                    h = hall.at[k, pl.ds(s * length, length)]
                    g = gall.at[k, pl.ds(s * ext, ext)]
                    pltpu.make_async_copy(h, h, hsems.at[k, s]).wait()
                    pltpu.make_async_copy(g, g, gsems.at[k, s]).wait()

            for s in range(planes):
                h = hall[k, s * length : (s + 1) * length]
                g = gall[k, s * ext : s * ext + length]
                meta = gall[k, s * ext + length : (s + 1) * ext][0:1].astype(F32)
                prob = router_probs(wr_ref[...], h)
                ones, cols = [], []
                for le in range(2):
                    one, weight = route_rows(meta, prob, le, i, upper, length)
                    cols.append(jnp.sum(one * weight, axis=1, keepdims=True))
                    ones.append(one.astype(BF16))
                hot = jnp.concatenate(ones, axis=0)
                picked = nn(hot, h)
                cut = pltpu.roll(picked, turn, 1)[:, :piece].astype(BF16)
                picked = picked.astype(BF16)
                dy = (nn(hot, g) * jnp.concatenate(cols, axis=0)).astype(BF16)
                at = pl.ds(pl.multiple_of((k * planes + s) * CAP, CAP), CAP)
                for le in range(2):
                    mine = slice(le * CAP, (le + 1) * CAP)
                    x_ref[le, at] = picked[mine]
                    xd_ref[le, at] = cut[mine]
                    dy_ref[le, at] = dy[mine]
            for c in leaving(k):
                c.start()
            return carry

        lax.fori_loop(0, 8, column, 0)
        for k in range(8):
            for c in leaving(k):
                c.wait()

    return pl.pallas_call(
        kernel,
        out_shape=(
            sds((2, slots, width), BF16),
            sds((2, slots, piece), BF16),
            sds((2, slots, width), BF16),
        ),
        in_specs=[SMEM_SPEC, VMEM_SPEC] + [ANY_SPEC] * 14,
        out_specs=(ANY_SPEC,) * 3,
        scratch_shapes=[
            pltpu.VMEM((8, planes * length, width), BF16),
            pltpu.VMEM((8, planes * ext, width), BF16),
            pltpu.SemaphoreType.DMA((8, planes)),
            pltpu.SemaphoreType.DMA((8, planes)),
            pltpu.VMEM((2, slots, width), BF16),
            pltpu.VMEM((2, slots, piece), BF16),
            pltpu.VMEM((2, slots, width), BF16),
            pltpu.SemaphoreType.DMA((8, 3)),
        ],
        compiler_params=params(60),
        cost_estimate=cost(8 * planes * 4 * 2 * CAP * length * width, 28 << 20),
        name="dispatch_others",
    )(idx, router_t, *h_pieces, *g_pieces, *corners)


def experts(x, gs, cs, w_gate, w_up, w_down):
    local, slots, width = x.shape
    hidden = w_gate.shape[2]
    fc = 512
    steps = hidden // fc

    def kernel(x_ref, gs_ref, cs_ref, wg_ref, wu_ref, wd_ref,
               a_ref, dg_ref, du_ref, dy_ref, yc_ref, dr_ref, dc_ref, yacc, dracc):
        f = pl.program_id(1)

        @pl.when(f == 0)
        def _():
            weight = cs_ref[0][:, 0:1]
            dy_ref[0] = (weight * gs_ref[0].astype(F32)).astype(BF16)
            yacc[...] = jnp.zeros_like(yacc)
            dracc[...] = jnp.zeros_like(dracc)

        rows, dy = x_ref[0], dy_ref[0]
        wg, wu, wd = wg_ref[0], wu_ref[0], wd_ref[0]
        g = nn(rows, wg)
        u = nn(rows, wu)
        da = nt(dy, wd)
        silu, slope = silu_parts(g)
        a = (silu * u).astype(BF16)
        dg = (da * u * slope).astype(BF16)
        du = (da * silu).astype(BF16)
        a_ref[0] = a
        dg_ref[0] = dg
        du_ref[0] = du
        yacc[...] += nn(a, wd)
        dracc[...] += nt(dg, wg) + nt(du, wu)

        @pl.when(f == steps - 1)
        def _():
            y = yacc[...].astype(BF16).astype(F32)
            weight = cs_ref[0][:, 0:1]
            yc_ref[0] = (weight * y).astype(BF16)
            dr_ref[0] = dracc[...].astype(BF16)
            dc = jnp.sum(gs_ref[0].astype(F32) * y, axis=1, keepdims=True)
            dc_ref[0] = jnp.broadcast_to(dc, (slots, 128))

    def whole(last):
        return pl.BlockSpec((1, slots, last), lambda e, f: (e, 0, 0))

    chunk = pl.BlockSpec((1, slots, fc), lambda e, f: (e, 0, f))
    wide = sds((local, slots, hidden), BF16)
    row = sds((local, slots, width), BF16)
    return pl.pallas_call(
        kernel,
        grid=(local, steps),
        out_shape=(wide, wide, wide, row, row, row, sds((local, slots, 128), F32)),
        in_specs=[
            whole(width),
            whole(width),
            whole(128),
            pl.BlockSpec((1, width, fc), lambda e, f: (e, 0, f)),
            pl.BlockSpec((1, width, fc), lambda e, f: (e, 0, f)),
            pl.BlockSpec((1, fc, width), lambda e, f: (e, f, 0)),
        ],
        out_specs=(chunk, chunk, chunk, whole(width), whole(width), whole(width), whole(128)),
        scratch_shapes=[pltpu.VMEM((slots, width), F32), pltpu.VMEM((slots, width), F32)],
        compiler_params=params(60, ("arbitrary", "arbitrary")),
        cost_estimate=cost(12 * local * slots * width * hidden, 40 << 20),
        name="experts",
    )(x, gs, cs, w_gate, w_up, w_down)


def chip_order(g, i):
    return jnp.where(g < 4, 4, 0) + ((g & 3) ^ (i[0] >> 1))


def whole_block(shape):
    return pl.BlockSpec(shape, lambda g, i: (0,) * len(shape))


def shared_branch(idx, rows, grads, shared, down):
    _, length, width = rows[0].shape
    ext = grads[0].shape[1]
    part = down.shape[0]
    step = width // 8

    def kernel(idx_ref, h_mine, h_other, g_mine, g_other, ws_ref, wd_ref,
               act_ref, gs_ref, gdacc, gsacc, wdown):
        s = pl.program_id(0)

        @pl.when(s == 0)
        def _():
            gdacc[...] = jnp.zeros_like(gdacc)
            gsacc[...] = jnp.zeros_like(gsacc)
            wdown[...] = wd_ref[...].astype(BF16)

        h = jnp.where(s == 0, h_mine[...], h_other[...]).reshape(4 * length, width)
        grad = jnp.where(s == 0, g_mine[...], g_other[...])[:, :length].reshape(4 * length, width)
        gate = nn(h, ws_ref[:, 0].reshape(width, part))
        up = nn(h, ws_ref[:, 1].reshape(width, part))
        da = nt(grad, wdown[...])
        silu, slope = silu_parts(gate)
        a = (silu * up).astype(BF16)
        dg = (da * up * slope).astype(BF16)
        du = (da * silu).astype(BF16)
        both = jnp.concatenate([dg, du], axis=1)
        act_ref[:, :, :part] = a.reshape(4, length, part)
        act_ref[:, :, part:] = both.reshape(4, length, 2 * part)
        gdacc[...] += tn(a, grad)
        gsacc[...] += tn(h, both)

        @pl.when(s == 1)
        def _():
            rows, wide = part // 8, 2 * part
            for k in range(8):
                gs_ref[k, :step] = gsacc[k * step : (k + 1) * step, :].astype(BF16)
                low = gdacc[k * rows : (k + 1) * rows, :].astype(BF16)
                rest = [low[: rows // 2, wide:], low[rows // 2 :, wide:]]
                gs_ref[k, step : step + rows] = low[:, :wide]
                gs_ref[k, step + rows :] = jnp.concatenate(rest, axis=1)

    return pl.pallas_call(
        kernel,
        out_shape=(
            sds((8, length, 3 * part), BF16),
            sds((8, step + 3 * part // 16, 2 * part), BF16),
        ),
        grid_spec=pltpu.PrefetchScalarGridSpec(
            num_scalar_prefetch=1,
            grid=(2,),
            in_specs=[
                whole_block((4, length, width)),
                whole_block((4, length, width)),
                whole_block((4, ext, width)),
                whole_block((4, ext, width)),
                whole_block((8, 2, step, part)),
                whole_block((part, width)),
            ],
            out_specs=(
                pl.BlockSpec((4, length, 3 * part), lambda g, i: (g, 0, 0)),
                whole_block((8, step + 3 * part // 16, 2 * part)),
            ),
            scratch_shapes=[
                pltpu.VMEM((part, width), F32),
                pltpu.VMEM((width, 2 * part), F32),
                pltpu.VMEM((part, width), BF16),
            ],
        ),
        compiler_params=params(60, ("arbitrary",)),
        cost_estimate=cost(12 * 8 * length * width * part, 14 << 20),
        name="shared_branch",
    )(idx, *rows, *grads, shared, down)


def combine(idx, act, hot, yc, dr, dc, shared, down):
    _, length, _ = act.shape
    part, width = down.shape
    ext = length + 16

    def kernel(idx_ref, act_ref, hot_ref, yc_ref, dr_ref, dc_ref, ws_ref, wd_ref,
               out_ref, do_ref, de_ref, wout, wback):
        s = pl.program_id(0)
        i = idx_ref[0]

        @pl.when(s == 0)
        def _():
            wout[:part] = wd_ref[...].astype(BF16)
            wback[:part] = ws_ref[:, 0].reshape(width, part).T
            wback[part : 2 * part] = ws_ref[:, 1].reshape(width, part).T

        wout[part:] = yc_ref[...].reshape(2 * CAP, width)
        wback[2 * part :] = dr_ref[...].reshape(2 * CAP, width)
        one = hot_ref[0]
        place = one.T
        act = act_ref[0]
        out = nn(jnp.concatenate([act[:, :part], place], axis=1), wout[...])
        out_ref[0] = out.astype(BF16)
        dh = nn(jnp.concatenate([act[:, part:], place], axis=1), wback[...]).astype(BF16)
        dcv = dc_ref[...].reshape(2 * CAP, 128)[:, 0:1] * one.astype(F32)
        expert = lax.broadcasted_iota(jnp.int32, (16, length), 0)
        dp = jnp.zeros((16, length), F32)
        for le in range(2):
            row = jnp.sum(dcv[le * CAP : (le + 1) * CAP], axis=0, keepdims=True)
            dp = dp + jnp.where(expert == 2 * i + le, row, 0.0)

        def put(ref):
            ref[0, :length] = dh
            ref[0, length:] = jnp.zeros((16, width), BF16)
            ref[0, length:, :length] = dp.astype(BF16)

        @pl.when(s < 4)
        def _():
            put(do_ref)

        @pl.when(s >= 4)
        def _():
            put(de_ref)

    def odd(block):
        return pl.BlockSpec((1,) + block, lambda g, i: (jnp.minimum(g, 3), 0, 0))

    def even(block):
        return pl.BlockSpec((1,) + block, lambda g, i: (jnp.maximum(g - 4, 0), 0, 0))

    def slot_spec(last):
        return pl.BlockSpec((2, CAP, last), lambda g, i: (0, chip_order(g, i), 0))

    def device(g, i):
        return 2 * ((g & 3) ^ (i[0] >> 1)) + ((i[0] & 1) ^ jnp.where(g < 4, 1, 0))

    ext4 = sds((4, ext, width), BF16)
    return pl.pallas_call(
        kernel,
        out_shape=(sds((8, length, width), BF16), ext4, ext4),
        grid_spec=pltpu.PrefetchScalarGridSpec(
            num_scalar_prefetch=1,
            grid=(8,),
            in_specs=[
                pl.BlockSpec((1, length, 3 * part), lambda g, i: (chip_order(g, i), 0, 0)),
                pl.BlockSpec((1, 2 * CAP, length), lambda g, i: (chip_order(g, i), 0, 0)),
                slot_spec(width),
                slot_spec(width),
                slot_spec(128),
                whole_block(shared.shape),
                whole_block((part, width)),
            ],
            out_specs=(
                pl.BlockSpec((1, length, width), lambda g, i: (device(g, i), 0, 0)),
                odd((ext, width)),
                even((ext, width)),
            ),
            scratch_shapes=[
                pltpu.VMEM((part + 2 * CAP, width), BF16),
                pltpu.VMEM((2 * part + 2 * CAP, width), BF16),
            ],
        ),
        compiler_params=params(60, ("arbitrary",)),
        cost_estimate=cost(10 * 8 * length * width * part, 18 << 20),
        name="combine",
    )(idx, act, hot, yc, dr, dc, shared, down)


def attention_backward(idx, tokens, grad, live_row, gain1, gain2, saved, router_t, dh_parts,
                       pieces):
    layout = layout_of(pieces)
    n = len(layout)
    length, width = tokens.shape
    step = width // 8
    cosine, sine = rope_tables(length)
    h1, q, k, v, o, prob, x1, h2 = saved
    total = 4 * width + 128

    def kernel(idx_ref, x_ref, g_ref, lv_ref, g1_ref, g2_ref, cos_ref, sin_ref, h1_ref, q_ref,
               k_ref, v_ref, o_ref, p_ref, x1_ref, h2_ref, wr_ref, d0, d1, d2, d3, *refs):
        piece_refs, refs = refs[:n], refs[n:]
        gt_ref, odd_ref, even_ref, wbuf, dmix, dqkv, gbuf, sems, h1b, qkvb, probs, lsem, psem = refs
        i = idx_ref[0]
        late = [pltpu.make_async_copy(h1_ref, h1b, lsem.at[3])]
        for m, ref in enumerate((q_ref, k_ref, v_ref)):
            late.append(pltpu.make_async_copy(ref, qkvb.at[m], lsem.at[m]))

        def prob_copy(hp):
            pairs = pl.ds(2 * hp, 2)
            return pltpu.make_async_copy(p_ref.at[pairs], probs.at[pairs], psem.at[hp])

        copies = place_copies(i, layout, step, piece_refs, wbuf, sems)
        for c in copies + late:
            c.start()
        for hp in range(HEADS // 2):
            prob_copy(hp).start()
        x1v = x1_ref[...]
        r2 = norm_scale(x1v)
        wr = wr_ref[...]
        pr = router_probs(wr, h2_ref[...])
        came = add([d0[...], d1[...], d2[...], d3[...]])
        dp = came[length:, :length] * lv_ref[...]
        dl = (pr * (dp - jnp.sum(pr * dp, axis=0, keepdims=True))).astype(BF16)
        router_grad = nn(dl, h2_ref[...])
        dh2 = came[:length] + tn(dl, wr)
        gain2_grad = jnp.sum(dh2 * x1v * r2, axis=0, keepdims=True)
        weighted = dh2 * g2_ref[...]
        inner = jnp.mean(x1v * weighted, axis=-1, keepdims=True)
        dx1 = g_ref[...].astype(F32) + r2 * weighted - x1v * (r2 * r2 * r2) * inner
        da = dx1.astype(BF16)
        for c in copies:
            c.wait()
        gbuf[:, 3 * width : 4 * width] = tn(o_ref[...], da).astype(BF16)
        dmix[...] = nt(da, wbuf[:, 3 * width : 4 * width]).astype(BF16)
        first = lax.broadcasted_iota(jnp.int32, (length, 128), 1) < HEAD_DIM

        for c in late:
            c.wait()

        def pair(hp, carry):
            prob_copy(hp).wait()
            at = pl.multiple_of(hp * 128, 128)
            qv, kv, vv = (qkvb[m, :, pl.ds(at, 128)] for m in range(3))
            dov = dmix[:, pl.ds(at, 128)]
            p = probs[pl.ds(2 * hp, 2)]
            dos = split_heads(dov, first)
            dp = nt(dos, vv).reshape(2, length, length)
            dv = tn(p.astype(BF16).reshape(2 * length, length), dos)
            ds = p * (dp - jnp.sum(p * dp, axis=-1, keepdims=True))
            ds = (ds * SCALE).astype(BF16)
            dq = nn(jnp.concatenate([ds[0], ds[1]], axis=1), split_heads(kv, first))
            dk = tn(ds.reshape(2 * length, length), split_heads(qv, first))
            cosv, sinv = cos_ref[...], sin_ref[...]
            dqkv[:, pl.ds(at, 128)] = (dq * cosv - half_swap(dq) * sinv).astype(BF16)
            dqkv[:, pl.ds(at + width, 128)] = (dk * cosv - half_swap(dk) * sinv).astype(BF16)
            dqkv[:, pl.ds(at + 2 * width, 128)] = dv.astype(BF16)
            return carry

        lax.fori_loop(0, HEADS // 2, pair, 0, unroll=UNROLL)
        gbuf[:, : 3 * width] = tn(h1b[...], dqkv[...]).astype(BF16)
        dh1 = nt(dqkv[...], wbuf[:, : 3 * width])
        x = x_ref[...].astype(F32)
        r1 = norm_scale(x)
        gain1_grad = jnp.sum(dh1 * x * r1, axis=0, keepdims=True)
        weighted = dh1 * g1_ref[...]
        inner = jnp.mean(x * weighted, axis=-1, keepdims=True)
        gt_ref[...] = (dx1 + r1 * weighted - x * (r1 * r1 * r1) * inner).astype(BF16)
        small = jnp.concatenate(
            [router_grad, gain1_grad, gain2_grad, jnp.zeros((110, width), F32)], axis=0
        )
        gbuf[:, 4 * width :] = small.T.astype(BF16)
        leaving = []
        for kk in range(8):
            rows = gbuf.at[pl.ds(pl.multiple_of((i ^ kk) * step, 16), step), :]
            ref = odd_ref if kk % 2 else even_ref
            leaving.append(pltpu.make_async_copy(rows, ref.at[kk // 2], psem.at[8 + kk]))
        for c in leaving:
            c.start()
        for c in leaving:
            c.wait()

    blocks = sds((4, step, total), BF16)
    return pl.pallas_call(
        kernel,
        out_shape=(sds((length, width), BF16), blocks, blocks),
        in_specs=[SMEM_SPEC] + [VMEM_SPEC] * 7 + [ANY_SPEC] * 4 + [VMEM_SPEC, ANY_SPEC]
        + [VMEM_SPEC] * 7 + [ANY_SPEC] * n,
        out_specs=(VMEM_SPEC, ANY_SPEC, ANY_SPEC),
        scratch_shapes=[
            pltpu.VMEM((width, pieces[0][2].shape[1]), BF16),
            pltpu.VMEM((length, width), BF16),
            pltpu.VMEM((length, 3 * width), BF16),
            pltpu.VMEM((width, total), BF16),
            pltpu.SemaphoreType.DMA((n,)),
            pltpu.VMEM((length, width), BF16),
            pltpu.VMEM((3, length, width), BF16),
            pltpu.VMEM((HEADS, length, length), F32),
            pltpu.SemaphoreType.DMA((4,)),
            pltpu.SemaphoreType.DMA((16,)),
        ],
        compiler_params=params(60),
        cost_estimate=cost(20 * length * width * width, 24 << 20),
        name="attention_backward",
    )(idx, tokens, grad, live_row, gain1, gain2, cosine, sine, h1, q, k, v, o, prob, x1, h2,
      router_t, *dh_parts, *[p for _, _, p in pieces])


def expert_grads(idx, e, base, steps, own, others, weights, done=()):
    w_gate, w_up, w_down = weights
    a, dg, du, dy, xd = own
    x_o, dy_o, xd_o = others
    local, slots, hidden = a.shape
    many = x_o.shape[1]
    width = x_o.shape[2]
    piece = xd.shape[2]
    fc = 512
    tile = TILE

    def kernel(idx_ref, a_ref, dg_ref, du_ref, dy_ref, xd_ref, xo_ref, dyo_ref, xdo_ref,
               wg_ref, wu_ref, wd_ref, *refs):
        gg_ref, gu_ref, gd_ref, ao, dgo, duo, gds, gsem = refs[len(done) :]
        f = pl.program_id(0)
        wg, wu, wd = wg_ref[0], wu_ref[0], wd_ref[0]

        def rows(t, carry):
            at = pl.ds(pl.multiple_of(t * tile, tile), tile)
            g = nn(xo_ref[0, at], wg)
            u = nn(xo_ref[0, at], wu)
            da = nt(dyo_ref[0, at], wd)
            silu, slope = silu_parts(g)
            ao[at] = (silu * u).astype(BF16)
            dgo[at] = (da * u * slope).astype(BF16)
            duo[at] = (da * silu).astype(BF16)
            return carry

        lax.fori_loop(0, many // tile, rows, 0)
        gg_ref[0] = tn(xdo_ref[0], dgo[...]) + tn(xd_ref[0], dg_ref[0])
        gu_ref[0] = tn(xdo_ref[0], duo[...]) + tn(xd_ref[0], du_ref[0])

        @pl.when(base + f == idx_ref[1])
        def _():
            gds[...] = tn(ao[...], dyo_ref[0]) + tn(a_ref[0], dy_ref[0])
            copy = pltpu.make_async_copy(gds, gd_ref.at[e], gsem)
            copy.start()
            copy.wait()

    def mine(block):
        return pl.BlockSpec((1,) + block, lambda f, i: (e, 0, 0))

    def chunk(rows):
        return pl.BlockSpec((1, rows, fc), lambda f, i: (e, 0, base + f))

    return pl.pallas_call(
        kernel,
        out_shape=(
            sds((local, piece, hidden), F32),
            sds((local, piece, hidden), F32),
            sds((local, fc, width), F32),
        ),
        grid_spec=pltpu.PrefetchScalarGridSpec(
            num_scalar_prefetch=1,
            grid=(steps,),
            in_specs=[
                pl.BlockSpec((1, slots, fc), lambda f, i: (e, 0, i[1])),
                chunk(slots),
                chunk(slots),
                mine((slots, width)),
                mine((slots, piece)),
                mine((many, width)),
                mine((many, width)),
                mine((many, piece)),
                chunk(width),
                chunk(width),
                pl.BlockSpec((1, fc, width), lambda f, i: (e, base + f, 0)),
            ]
            + [ANY_SPEC] * len(done),
            out_specs=(chunk(piece), chunk(piece), ANY_SPEC),
            scratch_shapes=[pltpu.VMEM((many, fc), BF16) for _ in range(3)]
            + [pltpu.VMEM((fc, width), F32), pltpu.SemaphoreType.DMA],
        ),
        compiler_params=params(60, ("arbitrary",)),
        cost_estimate=cost(steps * fc * width * (6 * many + 2 * (many + slots)), 15 << 20),
        input_output_aliases={12 + m: m for m in range(len(done))},
        name="expert_grads",
    )(idx, a, dg, du, dy, xd, x_o, dy_o, xd_o, w_gate, w_up, w_down, *done)


def finish(idx, parts, moved, blocks, x1, share, experts_all):
    rows, total = parts[0].shape
    length, width = x1.shape
    rest = total - width
    n, _, both = blocks.shape
    part, low_rows = both // 2, both // 16

    def kernel(idx_ref, s0, s1, s2, s3, m_ref, b_ref, x_ref, sh_ref, out_ref, q_ref, k_ref, v_ref,
               o_ref, r_ref, a_ref, f_ref, gate_ref, up_ref, down_ref, small):
        out_ref[...] = (x_ref[...] + sh_ref[...].astype(F32)).astype(BF16)
        for k in range(n):
            block = m_ref[k, :rows].astype(F32)
            gate_ref[:, k * part : (k + 1) * part] = block[:, :part]
            up_ref[:, k * part : (k + 1) * part] = block[:, part:]
            low = b_ref[k, rows:].astype(F32)
            at, half = k * low_rows, low_rows // 2
            down_ref[at : at + low_rows, :both] = low[:low_rows]
            down_ref[at : at + half, both:] = low[low_rows:, :part]
            down_ref[at + half : at + low_rows, both:] = low[low_rows:, part:]
        z = idx_ref[1]
        for r, s in enumerate((s0, s1, s2, s3)):
            small[(z - r + 4) & 3] = s[:, width:].astype(F32)
            for m, ref in enumerate((q_ref, k_ref, v_ref, o_ref)):

                @pl.when(((z - r + 4) & 3) == m)
                def _(ref=ref, s=s):
                    ref[...] = s[:, :width].astype(F32)

        low = small[0]
        square = jnp.concatenate([low, jnp.zeros((rows, 128 - rest), F32)], axis=1)
        square = jnp.concatenate([square, jnp.zeros((128 - rows, 128), F32)], axis=0).T
        r_ref[...] = square[:experts_all, :rows]
        a_ref[...] = square[experts_all : experts_all + 1, :rows]
        f_ref[...] = square[experts_all + 1 : experts_all + 2, :rows]

    flat = sds((rows, width), F32)
    line = sds((1, rows), F32)
    wide = sds((rows, n * part), F32)
    return pl.pallas_call(
        kernel,
        out_shape=(
            sds((length, width), BF16),
            flat, flat, flat, flat,
            sds((experts_all, rows), F32),
            line, line,
            wide, wide, sds((n * low_rows, width), F32),
        ),
        in_specs=[SMEM_SPEC] + [VMEM_SPEC] * 8,
        out_specs=(VMEM_SPEC,) * 11,
        scratch_shapes=[pltpu.VMEM((4, rows, rest), F32)],
        compiler_params=params(60),
        name="finish",
    )(idx, *parts, moved, blocks, x1, share)


def on_device(
    tokens,
    segment_ids,
    padding,
    routes,
    w_query,
    w_key,
    w_value,
    w_out,
    w_router,
    shared_gate,
    shared_up,
    shared_down,
    gain_attn,
    gain_ffn,
    expert_gate,
    expert_up,
    expert_down,
    cotangent,
):
    length, width = tokens.shape
    planes = lax.axis_size("dp")
    i = lax.axis_index("expert").astype(jnp.int32)
    z = lax.axis_index("dp").astype(jnp.int32)
    idx = jnp.stack([i, z])
    step = width // 8
    part = shared_down.shape[0]
    spread = planes == 4

    attn_shard = pack_shard([w_query, w_key, w_value, w_out], w_router.T)

    live_row = padding.astype(F32)
    meta = jnp.concatenate([routes[:, 0], routes[:, 1], padding[0]]).astype(BF16)[None, :]
    grad_ext = jnp.concatenate([after(cotangent, attn_shard), meta, jnp.zeros((15, width), BF16)], axis=0)
    ext = grad_ext.shape[0]

    def others(columns):
        at = [(z - r) % planes for r in (1, 2, 3)]
        return jnp.concatenate([lax.dynamic_index_in_dim(columns, a, 0, False) for a in at], axis=0)

    def copies(rows):
        return jnp.broadcast_to(rows[None], (planes,) + rows.shape)

    def columns(blocks):
        return lax.all_to_all(blocks, "dp", split_axis=0, concat_axis=0, tiled=True)

    def dp_gather(rows):
        return lax.all_gather(rows, "dp", axis=0)

    g_mine = lax.all_gather(grad_ext, "expert", axis=0, axis_index_groups=same_core())
    g_far = [shift(grad_ext, k) for k in (1, 2, 3)] if spread else []
    attn_pieces = relay_gather(attn_shard)

    gain1, gain2 = gain_attn[None, :], gain_ffn[None, :]
    side = pack_side(shared_gate, shared_up, part)
    side = after(side, [p for _, _, p in attn_pieces], gain1, gain2, live_row, g_far)
    side = lax.all_to_all(side, "expert", split_axis=0, concat_axis=0, tiled=True)

    *saved, router_t, h2_copies = attention_forward(
        idx, tokens, segment_ids, live_row, gain1, gain2, attn_pieces,
    )
    x1, h2 = saved[6], saved[7]

    g_plane = [g_mine, swap(g_mine, 1)]
    if spread:
        g_far = jnp.concatenate(after(g_far, h2), axis=0)
    side = after(side, h2)
    h_mine = chips_exchange(after(h2_copies, side))
    if spread:
        h_mine = after(h_mine, g_far)
    h_plane = [h_mine, swap(h_mine, 1)]
    if spread:
        h_columns = dp_gather(h2)
        at = (i // 2) ^ 3
        corner = [
            lax.dynamic_index_in_dim(rows, at, 0, False) for rows in after((g_mine, h_mine), h_plane)
        ]
        corner = dp_gather(jnp.concatenate(corner, axis=0))
        g_far = after(g_far, h_plane)
        g_far = [g_far, swap(g_far, 2), swap(g_far, 4)]

    cut = width // 4
    x_own, xd_own, gs_own, cs_own, hot = dispatch_plane(
        idx, router_t, h_plane, g_plane, cut
    )

    weights = (expert_gate, expert_up, expert_down)
    a, dg, du, dy, yc, dr, dc = experts(x_own, gs_own, cs_own, *weights)
    shared_w = after(side, yc)
    if spread:
        g_far, h_columns = after((g_far, h_columns), yc)
        shared_w = after(shared_w, g_far)
        g_far = both_cores(g_far)
        h_far = others(h_columns)
        h_far = [h_far, swap(h_far, 2), swap(h_far, 4)]
    act, side = shared_branch(idx, h_plane, g_plane, shared_w, shared_down)
    if spread:
        side = lax.psum_scatter(side, "dp", scatter_dimension=0, tiled=True)
    else:
        side = lax.psum(side, "dp")

    def exchanged(blocks):
        return lax.all_to_all(blocks, "expert", split_axis=0, concat_axis=0, tiled=True)

    if spread:
        g_far = after(g_far, act)
        act = after(act, g_far)
    out_shares, dh_other, dh_mine = combine(
        idx, act, hot, yc, dr, dc, shared_w, shared_down
    )
    if spread:
        h_far = after(h_far, dh_other)
        dh_other = after(dh_other, h_far)
    dh_came = swap(dh_other, 1)
    if spread:
        h_far = both_cores(after(h_far, dh_came))
    dh_sums = plane_near(dh_mine, dh_came)
    dh_parts = plane_far(dh_sums)
    if spread:
        h_far, g_far, corner = after((h_far, g_far, corner), dh_sums)
        corners = both_cores([corner])
        x_far, xd_far, dy_far = dispatch_others(idx, router_t, h_far, g_far, corners, 3, cut)
        dh_parts = after(dh_parts, x_far)
    out_shares = out_shares.reshape(8 * length, width)
    grad_tokens, att_other, att_mine = attention_backward(
        idx, tokens, cotangent, live_row, gain1, gain2, saved, router_t, dh_parts, attn_pieces,
    )
    att_came = swap(att_other, 1)
    if spread:
        side = dp_gather(after(side, att_mine)).reshape(8, -1, 2 * part)
    att_sums = plane_near(att_mine, att_came)
    att_parts = plane_far(att_sums)
    def att_quarters(parts):
        att = add(parts).astype(BF16)
        small = att[:, 4 * width :]
        return jnp.stack(
            [
                jnp.concatenate(
                    [att[:, m * width : (m + 1) * width], small[:, 32 * m : 32 * (m + 1)]], axis=1
                )
                for m in range(4)
            ]
        )

    if spread:
        xs = (x_far, dy_far, xd_far)
        own = (a, dg, du, dy, xd_own)
        chunks = expert_gate.shape[2] // 512
        done = expert_grads(idx, 0, 0, chunks, own, after(xs, att_sums), weights)
        att_parts = after(att_parts, done)
        out_share = lax.psum_scatter(
            after(out_shares, att_sums), "expert", scatter_dimension=0, tiled=True
        )
        xs = after(xs, att_parts)
        att_scattered = dp_scatter(att_quarters(att_parts))
        done = expert_grads(idx, 1, 0, chunks // 2, own, xs, weights, done)
        att_scattered, side = after((att_scattered, side), done)
        moved = exchanged(side)
        xs = after(xs, att_scattered)
        att_spread = dp_spread(att_scattered)
        done = expert_grads(idx, 1, chunks // 2, chunks // 2, own, xs, weights, done)
        moved, side, att_spread, out_share = after((moved, side, att_spread, out_share), done)
        g_gate, g_up, g_down = done
        order = idx
    else:
        att_spread = dp_whole(att_quarters(att_parts))
        moved = exchanged(side)
        out_share = lax.psum_scatter(out_shares, "expert", scatter_dimension=0, tiled=True)
        order = idx * jnp.array([1, 0], jnp.int32)

        def scattered(left, right):
            local = jnp.einsum("end,enf->edf", left, right, preferred_element_type=F32)
            return lax.psum_scatter(
                local.astype(BF16), "dp", scatter_dimension=1, tiled=True
            ).astype(F32)

        g_gate, g_up, g_down = scattered(x_own, dg), scattered(x_own, du), scattered(a, dy)

    experts_all = w_router.shape[1]
    (
        output, gq, gk, gv, go, g_router, g_gain1, g_gain2, g_sgate, g_sup, g_sdown,
    ) = finish(order, att_spread, moved, side, x1, out_share, experts_all)
    return (
        output,
        grad_tokens,
        gq,
        gk,
        gv,
        go,
        g_router.T,
        g_sgate,
        g_sup,
        g_sdown,
        g_gain1.reshape(step),
        g_gain2.reshape(step),
        g_gate,
        g_up,
        g_down,
    )


def solution(mesh):
    both = P(("dp", "expert"), None)
    one = P("expert", None)
    three = P("expert", None, None)
    sliced = P("expert", "dp", None)
    return jax.shard_map(
        on_device,
        mesh=mesh,
        in_specs=(both,) * 4 + (one,) * 8 + (P(), P()) + (three,) * 3 + (both,),
        out_specs=(both, both) + (one,) * 8 + (P("expert"), P("expert")) + (sliced,) * 3,
        check_vma=False,
    )
```

```python
import numpy as np

import jax
import jax.numpy as jnp
from jax import lax
from jax.experimental import pallas as pl
from jax.experimental.pallas import tpu as pltpu
from jax.sharding import PartitionSpec as P

HEADS = 12
HEAD_DIM = 64
CAP = 64
TILE = 1536
UNROLL = 2
EPS = 1e-06
ROPE_BASE = 10000.0
MASKED = -1e30
SCALE = HEAD_DIM**-0.5
F32 = jnp.float32
BF16 = jnp.bfloat16
MIB = 1 << 20
VMEM_SPEC = pl.BlockSpec(memory_space=pltpu.VMEM)
SMEM_SPEC = pl.BlockSpec(memory_space=pltpu.SMEM)
ANY_SPEC = pl.BlockSpec(memory_space=pl.ANY)


def nn(a, b):
    return jnp.dot(a, b, preferred_element_type=F32)


def nt(a, b):
    return lax.dot_general(a, b, (((1,), (1,)), ((), ())), preferred_element_type=F32)


def tn(a, b):
    return lax.dot_general(a, b, (((0,), (0,)), ((), ())), preferred_element_type=F32)


def sds(shape, dtype):
    return jax.ShapeDtypeStruct(shape, dtype)


def cost(flops, nbytes):
    return pl.CostEstimate(flops=int(flops), bytes_accessed=int(nbytes), transcendentals=0)


def params(mib, semantics=None):
    return pltpu.CompilerParams(vmem_limit_bytes=mib * MIB, dimension_semantics=semantics)


def swap(x, k):
    n = lax.axis_size("expert")
    return lax.ppermute(x, "expert", [(j, j ^ k) for j in range(n)])


def shift(x, k):
    n = lax.axis_size("dp")
    return lax.ppermute(x, "dp", [(j, (j + k) % n) for j in range(n)])


def after(value, *first):
    return lax.optimization_barrier((value, first))[0]


def relay_gather(x):
    half = x.shape[0] // 32 * 16
    a, b = swap(x, 2), swap(x, 4)
    d0, d1 = swap(a[:half], 4), swap(b[half:], 2)
    near = [(0, 0, x), (2, 0, a), (4, 0, b), (6, 0, d0), (6, half, d1)]
    return near + [(k + 1, at, swap(piece, 1)) for k, at, piece in near]


def same_core():
    n = lax.axis_size("expert")
    return [list(range(c, n, 2)) for c in range(2)]


def chips_exchange(blocks):
    return lax.all_to_all(
        blocks, "expert", split_axis=0, concat_axis=0, tiled=True, axis_index_groups=same_core()
    )


def both_cores(near):
    other = [swap(p, 1) for p in near]
    return [p for pair in zip(near, other) for p in pair]


def plane_near(even, came):
    return [add([even[j], came[j]]).astype(even.dtype) for j in range(4)]


def plane_far(sums):
    return [sums[0], swap(sums[1], 2), swap(sums[2], 4), swap(sums[3], 6)]


def dp_scatter(quarters):
    z = lax.axis_index("dp")
    parts = [lax.dynamic_index_in_dim(quarters, (z + k) % 4, 0, False) for k in range(4)]
    return [parts[0]] + [shift(parts[k], k) for k in (1, 2, 3)]


def dp_spread(parts):
    total = add(parts).astype(parts[0].dtype)
    return [total] + [shift(total, k) for k in (1, 2, 3)]


def dp_whole(quarters):
    whole = lax.psum(quarters, "dp")
    return [whole[0], whole[3], whole[2], whole[1]]


def add(parts):
    total = parts[0].astype(F32)
    for p in parts[1:]:
        total = total + p.astype(F32)
    return total


def norm_scale(values):
    return lax.rsqrt(jnp.mean(values * values, axis=-1, keepdims=True) + EPS)


def silu_parts(gate):
    logistic = 0.5 * jnp.tanh(0.5 * gate) + 0.5
    silu = gate * logistic
    return silu, logistic + silu * (1.0 - logistic)


def split_heads(x, first):
    zero = jnp.zeros_like(x)
    return jnp.concatenate([jnp.where(first, x, zero), jnp.where(first, zero, x)], axis=0)


def half_swap(x):
    lane = lax.broadcasted_iota(jnp.int32, x.shape, 1)
    half = HEAD_DIM // 2
    return jnp.where(
        lane % HEAD_DIM < half, pltpu.roll(x, x.shape[1] - half, 1), pltpu.roll(x, half, 1)
    )


def place_copies(i, layout, step, refs, target, sems):
    copies = []
    for n, ((k, at, rows), ref) in enumerate(zip(layout, refs)):
        start = pl.multiple_of((i ^ k) * step + at, 16)
        copies.append(pltpu.make_async_copy(ref, target.at[pl.ds(start, rows), :], sems.at[n]))
    return copies


def layout_of(pieces):
    return tuple((k, at, piece.shape[0]) for k, at, piece in pieces)


def rope_tables(length):
    half = HEAD_DIM // 2
    frequency = (ROPE_BASE ** (-(2.0 * np.arange(half, dtype=np.float32)) / HEAD_DIM)).astype(
        np.float32
    )
    angles = (np.arange(length, dtype=np.float32)[:, None] * frequency[None, :]).astype(np.float32)
    cosine, sine = np.cos(angles), np.sin(angles)
    return (
        np.concatenate([cosine] * 4, 1).astype(np.float32),
        np.concatenate([-sine, sine, -sine, sine], 1).astype(np.float32),
    )


def pack_shard(projections, router):
    rows, width = projections[0].shape
    n = len(projections)

    def kernel(*refs):
        out = refs[-1]
        for m in range(n):
            out[:, m * width : (m + 1) * width] = refs[m][...].astype(BF16)
        lines = jnp.concatenate(
            [refs[n][...], jnp.zeros((router.shape[0], 128 - rows), F32)], axis=1
        )
        lines = jnp.concatenate([lines, jnp.zeros((128 - router.shape[0], 128), F32)], axis=0)
        out[:, n * width :] = lines.T[:rows].astype(BF16)

    return pl.pallas_call(
        kernel,
        out_shape=sds((rows, n * width + 128), BF16),
        in_specs=[VMEM_SPEC] * (n + 1),
        out_specs=VMEM_SPEC,
        compiler_params=params(60),
        cost_estimate=cost(1, 1 << 20),
        name="pack_shard",
    )(*projections, router)


def pack_side(gate, up, part):
    step, wide = gate.shape

    def kernel(g_ref, u_ref, out_ref):
        for k in range(wide // part):
            out_ref[k, 0] = g_ref[:, k * part : (k + 1) * part].astype(BF16)
            out_ref[k, 1] = u_ref[:, k * part : (k + 1) * part].astype(BF16)

    return pl.pallas_call(
        kernel,
        out_shape=sds((wide // part, 2, step, part), BF16),
        in_specs=[VMEM_SPEC] * 2,
        out_specs=VMEM_SPEC,
        compiler_params=params(60),
        cost_estimate=cost(1, 1 << 20),
        name="pack_side",
    )(gate, up)


def attention_forward(idx, tokens, seg_row, live_row, gain1, gain2, pieces):
    layout = layout_of(pieces)
    n = len(layout)
    length, width = tokens.shape
    step = width // 8
    cosine, sine = rope_tables(length)

    def kernel(idx_ref, x_ref, sr_ref, lv_ref, g1_ref, g2_ref, cos_ref, sin_ref, *refs):
        piece_refs, refs = refs[:n], refs[n:]
        h1_ref, q_ref, k_ref, v_ref, o_ref, p_ref, x1_ref, h2_ref, wr_ref, h4_ref = refs[:10]
        wbuf, pre, probs, sems, psem = refs[10:]
        copies = place_copies(idx_ref[0], layout, step, piece_refs, wbuf, sems)
        for c in copies:
            c.start()
        x = x_ref[...].astype(F32)
        h1 = (x * norm_scale(x) * g1_ref[...]).astype(BF16)
        h1_ref[...] = h1
        row = lax.broadcasted_iota(jnp.int32, (length, length), 0)
        col = lax.broadcasted_iota(jnp.int32, (length, length), 1)
        seg = sr_ref[...].astype(F32)
        seg_col = jnp.broadcast_to(seg, (8, length)).T[:, 0:1]
        allowed = (col == row) | ((col <= row) & (seg == seg_col) & (lv_ref[...] > 0.0))
        bias = jnp.where(allowed, 0.0, MASKED)
        for c in copies:
            c.wait()
        pre[...] = nn(h1, wbuf[:, : 3 * width])
        first = lax.broadcasted_iota(jnp.int32, (length, 128), 1) < HEAD_DIM

        def pair(hp, carry):
            at = pl.multiple_of(hp * 128, 128)
            qp = pre[:, pl.ds(at, 128)]
            kp = pre[:, pl.ds(at + width, 128)]
            v = pre[:, pl.ds(at + 2 * width, 128)].astype(BF16)
            cosv, sinv = cos_ref[...], sin_ref[...]
            q = (qp * cosv + half_swap(qp) * sinv).astype(BF16)
            k = (kp * cosv + half_swap(kp) * sinv).astype(BF16)
            q_ref[:, pl.ds(at, 128)] = q
            k_ref[:, pl.ds(at, 128)] = k
            v_ref[:, pl.ds(at, 128)] = v
            scores = nt(split_heads(q, first), k) * SCALE
            scores = scores.reshape(2, length, length) + bias
            e = jnp.exp(scores - jnp.max(scores, axis=-1, keepdims=True))
            p = e / jnp.sum(e, axis=-1, keepdims=True)
            probs[pl.ds(2 * hp, 2)] = p
            pltpu.make_async_copy(
                probs.at[pl.ds(2 * hp, 2)], p_ref.at[pl.ds(2 * hp, 2)], psem.at[hp]
            ).start()
            low = p.astype(BF16)
            mixed = nn(jnp.concatenate([low[0], low[1]], axis=1), split_heads(v, first))
            o_ref[:, pl.ds(at, 128)] = mixed.astype(BF16)
            return carry

        lax.fori_loop(0, HEADS // 2, pair, 0, unroll=UNROLL)
        x1 = x + nn(o_ref[...], wbuf[:, 3 * width : 4 * width])
        x1_ref[...] = x1
        h2 = (x1 * norm_scale(x1) * g2_ref[...]).astype(BF16)
        h2_ref[...] = h2
        for chip in range(4):
            h4_ref[chip] = h2
        wr_ref[...] = wbuf[:, 4 * width :].astype(F32).T[:16].astype(BF16)
        for hp in range(HEADS // 2):
            pltpu.make_async_copy(
                probs.at[pl.ds(2 * hp, 2)], p_ref.at[pl.ds(2 * hp, 2)], psem.at[hp]
            ).wait()

    flat = sds((length, width), BF16)
    return pl.pallas_call(
        kernel,
        out_shape=(
            flat, flat, flat, flat, flat,
            sds((HEADS, length, length), F32),
            sds((length, width), F32),
            flat,
            sds((16, width), BF16),
            sds((4, length, width), BF16),
        ),
        in_specs=[SMEM_SPEC] + [VMEM_SPEC] * 7 + [ANY_SPEC] * n,
        out_specs=(VMEM_SPEC,) * 5 + (ANY_SPEC,) + (VMEM_SPEC,) * 4,
        scratch_shapes=[
            pltpu.VMEM((width, pieces[0][2].shape[1]), BF16),
            pltpu.VMEM((length, 3 * width), F32),
            pltpu.VMEM((HEADS, length, length), F32),
            pltpu.SemaphoreType.DMA((n,)),
            pltpu.SemaphoreType.DMA((HEADS // 2,)),
        ],
        compiler_params=params(60),
        cost_estimate=cost(8 * length * width * width, 12 << 20),
        name="attention_forward",
    )(idx, tokens, seg_row, live_row, gain1, gain2, cosine, sine,
      *[p for _, _, p in pieces])


def route_rows(meta, prob, le, i, upper, length):
    expert = (2 * i + le).astype(F32)
    hit = (meta[:, :length] == expert) | (meta[:, length : 2 * length] == expert)
    hot = jnp.where(hit, 1.0, 0.0)
    rank = nn(jnp.broadcast_to(hot, (16, length)).astype(BF16), upper)[0:1]
    slot = lax.broadcasted_iota(jnp.int32, (CAP, length), 0).astype(F32) + 1.0
    one = jnp.where((slot == rank) & hit, 1.0, 0.0)
    which = lax.broadcasted_iota(jnp.int32, prob.shape, 0) == 2 * i + le
    weight = jnp.sum(jnp.where(which, prob, 0.0), axis=0, keepdims=True)
    return one, weight * meta[:, 2 * length :]


def router_probs(router_t, rows):
    logits = nt(router_t, rows)
    e = jnp.exp(logits - jnp.max(logits, axis=0, keepdims=True))
    return e / jnp.sum(e, axis=0, keepdims=True)


def upper_ones(length):
    return jnp.where(
        lax.broadcasted_iota(jnp.int32, (length, length), 0)
        <= lax.broadcasted_iota(jnp.int32, (length, length), 1),
        1.0,
        0.0,
    ).astype(BF16)


def dispatch_plane(idx, router_t, rows, grads, piece):
    _, length, width = rows[0].shape
    slots = 8 * CAP
    ext = length + 16

    def kernel(idx_ref, wr_ref, *refs):
        hp, gp, refs = refs[:2], refs[2:4], refs[4:]
        x_ref, xd_ref, gs_ref, cs_ref, hot_ref, hall, gall, sems = refs
        i = idx_ref[0]
        copies = []
        for c in range(2):
            copies.append(pltpu.make_async_copy(hp[c], hall.at[pl.ds(4 * c, 4)], sems.at[c]))
            copies.append(pltpu.make_async_copy(gp[c], gall.at[pl.ds(4 * c, 4)], sems.at[2 + c]))
        for c in copies:
            c.start()
        upper = upper_ones(length)
        turn = (width - idx_ref[1] * piece) % width
        for c in copies:
            c.wait()

        def sequences(pair, carry):
            for k in (2 * pair, 2 * pair + 1):
                h = hall[k]
                prob = router_probs(wr_ref[...], h)
                meta = gall[k, length:ext][0:1].astype(F32)
                at = pl.multiple_of(k * CAP, CAP)
                ones = []
                for le in range(2):
                    one, weight = route_rows(meta, prob, le, i, upper, length)
                    col = jnp.sum(one * weight, axis=1, keepdims=True)
                    cs_ref[le, pl.ds(at, CAP), :] = jnp.broadcast_to(col, (CAP, 128))
                    ones.append(one.astype(BF16))
                hot = jnp.concatenate(ones, axis=0)
                hot_ref[k] = hot
                picked = nn(hot, h)
                cut = pltpu.roll(picked, turn, 1)[:, :piece].astype(BF16)
                picked = picked.astype(BF16)
                grads = nn(hot, gall[k, 0:length]).astype(BF16)
                for le in range(2):
                    mine = slice(le * CAP, (le + 1) * CAP)
                    x_ref[le, pl.ds(at, CAP), :] = picked[mine]
                    xd_ref[le, pl.ds(at, CAP), :] = cut[mine]
                    gs_ref[le, pl.ds(at, CAP), :] = grads[mine]
            return carry

        lax.fori_loop(0, 4, sequences, 0)

    return pl.pallas_call(
        kernel,
        out_shape=(
            sds((2, slots, width), BF16),
            sds((2, slots, piece), BF16),
            sds((2, slots, width), BF16),
            sds((2, slots, 128), F32),
            sds((8, 2 * CAP, length), BF16),
        ),
        in_specs=[SMEM_SPEC, VMEM_SPEC] + [ANY_SPEC] * 4,
        out_specs=(VMEM_SPEC,) * 5,
        scratch_shapes=[
            pltpu.VMEM((8, length, width), BF16),
            pltpu.VMEM((8, ext, width), BF16),
            pltpu.SemaphoreType.DMA((4,)),
        ],
        compiler_params=params(60),
        cost_estimate=cost(8 * 4 * 2 * CAP * length * width, 16 << 20),
        name="dispatch_plane",
    )(idx, router_t, *rows, *grads)


def dispatch_others(idx, router_t, h_pieces, g_pieces, corners, planes, piece):
    width = h_pieces[0].shape[1]
    length = h_pieces[0].shape[0] // planes
    ext = length + 16
    slots = 8 * planes * CAP

    def kernel(idx_ref, wr_ref, *refs):
        hp, gp, both, refs = refs[:6], refs[6:12], refs[12:14], refs[14:]
        x_out, xd_out, dy_out, hall, gall, hsems, gsems, x_ref, xd_ref, dy_ref, osems = refs
        i = idx_ref[0]

        def leaving(k):
            rows = pl.ds(pl.multiple_of(k * planes * CAP, CAP), planes * CAP)
            for m, (a, b) in enumerate(((x_ref, x_out), (xd_ref, xd_out), (dy_ref, dy_out))):
                yield pltpu.make_async_copy(a.at[:, rows], b.at[:, rows], osems.at[k, m])

        def copies(k):
            if k < 6:
                yield pltpu.make_async_copy(hp[k], hall.at[k], hsems.at[k, 0])
                yield pltpu.make_async_copy(gp[k], gall.at[k], gsems.at[k, 0])
                return
            for s in range(planes):
                plane = (idx_ref[1] - s + 3) & 3
                yield pltpu.make_async_copy(
                    both[k - 6].at[plane, pl.ds(0, ext)],
                    gall.at[k, pl.ds(s * ext, ext)],
                    gsems.at[k, s],
                )
                yield pltpu.make_async_copy(
                    both[k - 6].at[plane, pl.ds(ext, length)],
                    hall.at[k, pl.ds(s * length, length)],
                    hsems.at[k, s],
                )

        for k in range(8):
            for c in copies(k):
                c.start()
        upper = upper_ones(length)
        turn = (width - idx_ref[1] * piece) % width

        def column(k, carry):
            @pl.when(k < 6)
            def _():
                pltpu.make_async_copy(hall.at[k], hall.at[k], hsems.at[k, 0]).wait()
                pltpu.make_async_copy(gall.at[k], gall.at[k], gsems.at[k, 0]).wait()

            @pl.when(k >= 6)
            def _():
                for s in range(planes):
                    h = hall.at[k, pl.ds(s * length, length)]
                    g = gall.at[k, pl.ds(s * ext, ext)]
                    pltpu.make_async_copy(h, h, hsems.at[k, s]).wait()
                    pltpu.make_async_copy(g, g, gsems.at[k, s]).wait()

            for s in range(planes):
                h = hall[k, s * length : (s + 1) * length]
                g = gall[k, s * ext : s * ext + length]
                meta = gall[k, s * ext + length : (s + 1) * ext][0:1].astype(F32)
                prob = router_probs(wr_ref[...], h)
                ones, cols = [], []
                for le in range(2):
                    one, weight = route_rows(meta, prob, le, i, upper, length)
                    cols.append(jnp.sum(one * weight, axis=1, keepdims=True))
                    ones.append(one.astype(BF16))
                hot = jnp.concatenate(ones, axis=0)
                picked = nn(hot, h)
                cut = pltpu.roll(picked, turn, 1)[:, :piece].astype(BF16)
                picked = picked.astype(BF16)
                dy = (nn(hot, g) * jnp.concatenate(cols, axis=0)).astype(BF16)
                at = pl.ds(pl.multiple_of((k * planes + s) * CAP, CAP), CAP)
                for le in range(2):
                    mine = slice(le * CAP, (le + 1) * CAP)
                    x_ref[le, at] = picked[mine]
                    xd_ref[le, at] = cut[mine]
                    dy_ref[le, at] = dy[mine]
            for c in leaving(k):
                c.start()
            return carry

        lax.fori_loop(0, 8, column, 0)
        for k in range(8):
            for c in leaving(k):
                c.wait()

    return pl.pallas_call(
        kernel,
        out_shape=(
            sds((2, slots, width), BF16),
            sds((2, slots, piece), BF16),
            sds((2, slots, width), BF16),
        ),
        in_specs=[SMEM_SPEC, VMEM_SPEC] + [ANY_SPEC] * 14,
        out_specs=(ANY_SPEC,) * 3,
        scratch_shapes=[
            pltpu.VMEM((8, planes * length, width), BF16),
            pltpu.VMEM((8, planes * ext, width), BF16),
            pltpu.SemaphoreType.DMA((8, planes)),
            pltpu.SemaphoreType.DMA((8, planes)),
            pltpu.VMEM((2, slots, width), BF16),
            pltpu.VMEM((2, slots, piece), BF16),
            pltpu.VMEM((2, slots, width), BF16),
            pltpu.SemaphoreType.DMA((8, 3)),
        ],
        compiler_params=params(60),
        cost_estimate=cost(8 * planes * 4 * 2 * CAP * length * width, 28 << 20),
        name="dispatch_others",
    )(idx, router_t, *h_pieces, *g_pieces, *corners)


def experts(x, gs, cs, w_gate, w_up, w_down):
    local, slots, width = x.shape
    hidden = w_gate.shape[2]
    fc = 512
    steps = hidden // fc

    def kernel(x_ref, gs_ref, cs_ref, wg_ref, wu_ref, wd_ref,
               a_ref, dg_ref, du_ref, dy_ref, yc_ref, dr_ref, dc_ref, yacc, dracc):
        f = pl.program_id(1)

        @pl.when(f == 0)
        def _():
            weight = cs_ref[0][:, 0:1]
            dy_ref[0] = (weight * gs_ref[0].astype(F32)).astype(BF16)
            yacc[...] = jnp.zeros_like(yacc)
            dracc[...] = jnp.zeros_like(dracc)

        rows, dy = x_ref[0], dy_ref[0]
        wg, wu, wd = wg_ref[0], wu_ref[0], wd_ref[0]
        g = nn(rows, wg)
        u = nn(rows, wu)
        da = nt(dy, wd)
        silu, slope = silu_parts(g)
        a = (silu * u).astype(BF16)
        dg = (da * u * slope).astype(BF16)
        du = (da * silu).astype(BF16)
        a_ref[0] = a
        dg_ref[0] = dg
        du_ref[0] = du
        yacc[...] += nn(a, wd)
        dracc[...] += nt(dg, wg) + nt(du, wu)

        @pl.when(f == steps - 1)
        def _():
            y = yacc[...].astype(BF16).astype(F32)
            weight = cs_ref[0][:, 0:1]
            yc_ref[0] = (weight * y).astype(BF16)
            dr_ref[0] = dracc[...].astype(BF16)
            dc = jnp.sum(gs_ref[0].astype(F32) * y, axis=1, keepdims=True)
            dc_ref[0] = jnp.broadcast_to(dc, (slots, 128))

    def whole(last):
        return pl.BlockSpec((1, slots, last), lambda e, f: (e, 0, 0))

    chunk = pl.BlockSpec((1, slots, fc), lambda e, f: (e, 0, f))
    wide = sds((local, slots, hidden), BF16)
    row = sds((local, slots, width), BF16)
    return pl.pallas_call(
        kernel,
        grid=(local, steps),
        out_shape=(wide, wide, wide, row, row, row, sds((local, slots, 128), F32)),
        in_specs=[
            whole(width),
            whole(width),
            whole(128),
            pl.BlockSpec((1, width, fc), lambda e, f: (e, 0, f)),
            pl.BlockSpec((1, width, fc), lambda e, f: (e, 0, f)),
            pl.BlockSpec((1, fc, width), lambda e, f: (e, f, 0)),
        ],
        out_specs=(chunk, chunk, chunk, whole(width), whole(width), whole(width), whole(128)),
        scratch_shapes=[pltpu.VMEM((slots, width), F32), pltpu.VMEM((slots, width), F32)],
        compiler_params=params(60, ("arbitrary", "arbitrary")),
        cost_estimate=cost(12 * local * slots * width * hidden, 40 << 20),
        name="experts",
    )(x, gs, cs, w_gate, w_up, w_down)


def chip_order(g, i):
    return jnp.where(g < 4, 4, 0) + ((g & 3) ^ (i[0] >> 1))


def whole_block(shape):
    return pl.BlockSpec(shape, lambda g, i: (0,) * len(shape))


def shared_branch(idx, rows, grads, shared, down):
    _, length, width = rows[0].shape
    ext = grads[0].shape[1]
    part = down.shape[0]
    step = width // 8

    def kernel(idx_ref, h_mine, h_other, g_mine, g_other, ws_ref, wd_ref,
               act_ref, gs_ref, gdacc, gsacc, wdown):
        s = pl.program_id(0)

        @pl.when(s == 0)
        def _():
            gdacc[...] = jnp.zeros_like(gdacc)
            gsacc[...] = jnp.zeros_like(gsacc)
            wdown[...] = wd_ref[...].astype(BF16)

        h = jnp.where(s == 0, h_mine[...], h_other[...]).reshape(4 * length, width)
        grad = jnp.where(s == 0, g_mine[...], g_other[...])[:, :length].reshape(4 * length, width)
        gate = nn(h, ws_ref[:, 0].reshape(width, part))
        up = nn(h, ws_ref[:, 1].reshape(width, part))
        da = nt(grad, wdown[...])
        silu, slope = silu_parts(gate)
        a = (silu * up).astype(BF16)
        dg = (da * up * slope).astype(BF16)
        du = (da * silu).astype(BF16)
        both = jnp.concatenate([dg, du], axis=1)
        act_ref[:, :, :part] = a.reshape(4, length, part)
        act_ref[:, :, part:] = both.reshape(4, length, 2 * part)
        gdacc[...] += tn(a, grad)
        gsacc[...] += tn(h, both)

        @pl.when(s == 1)
        def _():
            rows, wide = part // 8, 2 * part
            for k in range(8):
                gs_ref[k, :step] = gsacc[k * step : (k + 1) * step, :].astype(BF16)
                low = gdacc[k * rows : (k + 1) * rows, :].astype(BF16)
                rest = [low[: rows // 2, wide:], low[rows // 2 :, wide:]]
                gs_ref[k, step : step + rows] = low[:, :wide]
                gs_ref[k, step + rows :] = jnp.concatenate(rest, axis=1)

    return pl.pallas_call(
        kernel,
        out_shape=(
            sds((8, length, 3 * part), BF16),
            sds((8, step + 3 * part // 16, 2 * part), BF16),
        ),
        grid_spec=pltpu.PrefetchScalarGridSpec(
            num_scalar_prefetch=1,
            grid=(2,),
            in_specs=[
                whole_block((4, length, width)),
                whole_block((4, length, width)),
                whole_block((4, ext, width)),
                whole_block((4, ext, width)),
                whole_block((8, 2, step, part)),
                whole_block((part, width)),
            ],
            out_specs=(
                pl.BlockSpec((4, length, 3 * part), lambda g, i: (g, 0, 0)),
                whole_block((8, step + 3 * part // 16, 2 * part)),
            ),
            scratch_shapes=[
                pltpu.VMEM((part, width), F32),
                pltpu.VMEM((width, 2 * part), F32),
                pltpu.VMEM((part, width), BF16),
            ],
        ),
        compiler_params=params(60, ("arbitrary",)),
        cost_estimate=cost(12 * 8 * length * width * part, 14 << 20),
        name="shared_branch",
    )(idx, *rows, *grads, shared, down)


def combine(idx, act, hot, yc, dr, dc, shared, down):
    _, length, _ = act.shape
    part, width = down.shape
    ext = length + 16

    def kernel(idx_ref, act_ref, hot_ref, yc_ref, dr_ref, dc_ref, ws_ref, wd_ref,
               out_ref, do_ref, de_ref, wout, wback):
        s = pl.program_id(0)
        i = idx_ref[0]

        @pl.when(s == 0)
        def _():
            wout[:part] = wd_ref[...].astype(BF16)
            wback[:part] = ws_ref[:, 0].reshape(width, part).T
            wback[part : 2 * part] = ws_ref[:, 1].reshape(width, part).T

        wout[part:] = yc_ref[...].reshape(2 * CAP, width)
        wback[2 * part :] = dr_ref[...].reshape(2 * CAP, width)
        one = hot_ref[0]
        place = one.T
        act = act_ref[0]
        out = nn(jnp.concatenate([act[:, :part], place], axis=1), wout[...])
        out_ref[0] = out.astype(BF16)
        dh = nn(jnp.concatenate([act[:, part:], place], axis=1), wback[...]).astype(BF16)
        dcv = dc_ref[...].reshape(2 * CAP, 128)[:, 0:1] * one.astype(F32)
        expert = lax.broadcasted_iota(jnp.int32, (16, length), 0)
        dp = jnp.zeros((16, length), F32)
        for le in range(2):
            row = jnp.sum(dcv[le * CAP : (le + 1) * CAP], axis=0, keepdims=True)
            dp = dp + jnp.where(expert == 2 * i + le, row, 0.0)

        def put(ref):
            ref[0, :length] = dh
            ref[0, length:] = jnp.zeros((16, width), BF16)
            ref[0, length:, :length] = dp.astype(BF16)

        @pl.when(s < 4)
        def _():
            put(do_ref)

        @pl.when(s >= 4)
        def _():
            put(de_ref)

    def odd(block):
        return pl.BlockSpec((1,) + block, lambda g, i: (jnp.minimum(g, 3), 0, 0))

    def even(block):
        return pl.BlockSpec((1,) + block, lambda g, i: (jnp.maximum(g - 4, 0), 0, 0))

    def slot_spec(last):
        return pl.BlockSpec((2, CAP, last), lambda g, i: (0, chip_order(g, i), 0))

    def device(g, i):
        return 2 * ((g & 3) ^ (i[0] >> 1)) + ((i[0] & 1) ^ jnp.where(g < 4, 1, 0))

    ext4 = sds((4, ext, width), BF16)
    return pl.pallas_call(
        kernel,
        out_shape=(sds((8, length, width), BF16), ext4, ext4),
        grid_spec=pltpu.PrefetchScalarGridSpec(
            num_scalar_prefetch=1,
            grid=(8,),
            in_specs=[
                pl.BlockSpec((1, length, 3 * part), lambda g, i: (chip_order(g, i), 0, 0)),
                pl.BlockSpec((1, 2 * CAP, length), lambda g, i: (chip_order(g, i), 0, 0)),
                slot_spec(width),
                slot_spec(width),
                slot_spec(128),
                whole_block(shared.shape),
                whole_block((part, width)),
            ],
            out_specs=(
                pl.BlockSpec((1, length, width), lambda g, i: (device(g, i), 0, 0)),
                odd((ext, width)),
                even((ext, width)),
            ),
            scratch_shapes=[
                pltpu.VMEM((part + 2 * CAP, width), BF16),
                pltpu.VMEM((2 * part + 2 * CAP, width), BF16),
            ],
        ),
        compiler_params=params(60, ("arbitrary",)),
        cost_estimate=cost(10 * 8 * length * width * part, 18 << 20),
        name="combine",
    )(idx, act, hot, yc, dr, dc, shared, down)


def attention_backward(idx, tokens, grad, live_row, gain1, gain2, saved, router_t, dh_parts,
                       pieces):
    layout = layout_of(pieces)
    n = len(layout)
    length, width = tokens.shape
    step = width // 8
    cosine, sine = rope_tables(length)
    h1, q, k, v, o, prob, x1, h2 = saved
    total = 4 * width + 128

    def kernel(idx_ref, x_ref, g_ref, lv_ref, g1_ref, g2_ref, cos_ref, sin_ref, h1_ref, q_ref,
               k_ref, v_ref, o_ref, p_ref, x1_ref, h2_ref, wr_ref, d0, d1, d2, d3, *refs):
        piece_refs, refs = refs[:n], refs[n:]
        gt_ref, odd_ref, even_ref, wbuf, dmix, dqkv, gbuf, sems, h1b, qkvb, probs, lsem, psem = refs
        i = idx_ref[0]
        late = [pltpu.make_async_copy(h1_ref, h1b, lsem.at[3])]
        for m, ref in enumerate((q_ref, k_ref, v_ref)):
            late.append(pltpu.make_async_copy(ref, qkvb.at[m], lsem.at[m]))

        def prob_copy(hp):
            pairs = pl.ds(2 * hp, 2)
            return pltpu.make_async_copy(p_ref.at[pairs], probs.at[pairs], psem.at[hp])

        copies = place_copies(i, layout, step, piece_refs, wbuf, sems)
        for c in copies + late:
            c.start()
        for hp in range(HEADS // 2):
            prob_copy(hp).start()
        x1v = x1_ref[...]
        r2 = norm_scale(x1v)
        wr = wr_ref[...]
        pr = router_probs(wr, h2_ref[...])
        came = add([d0[...], d1[...], d2[...], d3[...]])
        dp = came[length:, :length] * lv_ref[...]
        dl = (pr * (dp - jnp.sum(pr * dp, axis=0, keepdims=True))).astype(BF16)
        router_grad = nn(dl, h2_ref[...])
        dh2 = came[:length] + tn(dl, wr)
        gain2_grad = jnp.sum(dh2 * x1v * r2, axis=0, keepdims=True)
        weighted = dh2 * g2_ref[...]
        inner = jnp.mean(x1v * weighted, axis=-1, keepdims=True)
        dx1 = g_ref[...].astype(F32) + r2 * weighted - x1v * (r2 * r2 * r2) * inner
        da = dx1.astype(BF16)
        for c in copies:
            c.wait()
        gbuf[:, 3 * width : 4 * width] = tn(o_ref[...], da).astype(BF16)
        dmix[...] = nt(da, wbuf[:, 3 * width : 4 * width]).astype(BF16)
        first = lax.broadcasted_iota(jnp.int32, (length, 128), 1) < HEAD_DIM

        for c in late:
            c.wait()

        def pair(hp, carry):
            prob_copy(hp).wait()
            at = pl.multiple_of(hp * 128, 128)
            qv, kv, vv = (qkvb[m, :, pl.ds(at, 128)] for m in range(3))
            dov = dmix[:, pl.ds(at, 128)]
            p = probs[pl.ds(2 * hp, 2)]
            dos = split_heads(dov, first)
            dp = nt(dos, vv).reshape(2, length, length)
            dv = tn(p.astype(BF16).reshape(2 * length, length), dos)
            ds = p * (dp - jnp.sum(p * dp, axis=-1, keepdims=True))
            ds = (ds * SCALE).astype(BF16)
            dq = nn(jnp.concatenate([ds[0], ds[1]], axis=1), split_heads(kv, first))
            dk = tn(ds.reshape(2 * length, length), split_heads(qv, first))
            cosv, sinv = cos_ref[...], sin_ref[...]
            dqkv[:, pl.ds(at, 128)] = (dq * cosv - half_swap(dq) * sinv).astype(BF16)
            dqkv[:, pl.ds(at + width, 128)] = (dk * cosv - half_swap(dk) * sinv).astype(BF16)
            dqkv[:, pl.ds(at + 2 * width, 128)] = dv.astype(BF16)
            return carry

        lax.fori_loop(0, HEADS // 2, pair, 0, unroll=UNROLL)
        gbuf[:, : 3 * width] = tn(h1b[...], dqkv[...]).astype(BF16)
        dh1 = nt(dqkv[...], wbuf[:, : 3 * width])
        x = x_ref[...].astype(F32)
        r1 = norm_scale(x)
        gain1_grad = jnp.sum(dh1 * x * r1, axis=0, keepdims=True)
        weighted = dh1 * g1_ref[...]
        inner = jnp.mean(x * weighted, axis=-1, keepdims=True)
        gt_ref[...] = (dx1 + r1 * weighted - x * (r1 * r1 * r1) * inner).astype(BF16)
        small = jnp.concatenate(
            [router_grad, gain1_grad, gain2_grad, jnp.zeros((110, width), F32)], axis=0
        )
        gbuf[:, 4 * width :] = small.T.astype(BF16)
        leaving = []
        for kk in range(8):
            rows = gbuf.at[pl.ds(pl.multiple_of((i ^ kk) * step, 16), step), :]
            ref = odd_ref if kk % 2 else even_ref
            leaving.append(pltpu.make_async_copy(rows, ref.at[kk // 2], psem.at[8 + kk]))
        for c in leaving:
            c.start()
        for c in leaving:
            c.wait()

    blocks = sds((4, step, total), BF16)
    return pl.pallas_call(
        kernel,
        out_shape=(sds((length, width), BF16), blocks, blocks),
        in_specs=[SMEM_SPEC] + [VMEM_SPEC] * 7 + [ANY_SPEC] * 4 + [VMEM_SPEC, ANY_SPEC]
        + [VMEM_SPEC] * 7 + [ANY_SPEC] * n,
        out_specs=(VMEM_SPEC, ANY_SPEC, ANY_SPEC),
        scratch_shapes=[
            pltpu.VMEM((width, pieces[0][2].shape[1]), BF16),
            pltpu.VMEM((length, width), BF16),
            pltpu.VMEM((length, 3 * width), BF16),
            pltpu.VMEM((width, total), BF16),
            pltpu.SemaphoreType.DMA((n,)),
            pltpu.VMEM((length, width), BF16),
            pltpu.VMEM((3, length, width), BF16),
            pltpu.VMEM((HEADS, length, length), F32),
            pltpu.SemaphoreType.DMA((4,)),
            pltpu.SemaphoreType.DMA((16,)),
        ],
        compiler_params=params(60),
        cost_estimate=cost(20 * length * width * width, 24 << 20),
        name="attention_backward",
    )(idx, tokens, grad, live_row, gain1, gain2, cosine, sine, h1, q, k, v, o, prob, x1, h2,
      router_t, *dh_parts, *[p for _, _, p in pieces])


def expert_grads(idx, e, base, steps, own, others, weights, done=()):
    w_gate, w_up, w_down = weights
    a, dg, du, dy, xd = own
    x_o, dy_o, xd_o = others
    local, slots, hidden = a.shape
    many = x_o.shape[1]
    width = x_o.shape[2]
    piece = xd.shape[2]
    fc = 512
    tile = TILE

    def kernel(idx_ref, a_ref, dg_ref, du_ref, dy_ref, xd_ref, xo_ref, dyo_ref, xdo_ref,
               wg_ref, wu_ref, wd_ref, *refs):
        gg_ref, gu_ref, gd_ref, ao, dgo, duo, gds, gsem = refs[len(done) :]
        f = pl.program_id(0)
        wg, wu, wd = wg_ref[0], wu_ref[0], wd_ref[0]

        def rows(t, carry):
            at = pl.ds(pl.multiple_of(t * tile, tile), tile)
            g = nn(xo_ref[0, at], wg)
            u = nn(xo_ref[0, at], wu)
            da = nt(dyo_ref[0, at], wd)
            silu, slope = silu_parts(g)
            ao[at] = (silu * u).astype(BF16)
            dgo[at] = (da * u * slope).astype(BF16)
            duo[at] = (da * silu).astype(BF16)
            return carry

        lax.fori_loop(0, many // tile, rows, 0)
        gg_ref[0] = tn(xdo_ref[0], dgo[...]) + tn(xd_ref[0], dg_ref[0])
        gu_ref[0] = tn(xdo_ref[0], duo[...]) + tn(xd_ref[0], du_ref[0])

        @pl.when(base + f == idx_ref[1])
        def _():
            gds[...] = tn(ao[...], dyo_ref[0]) + tn(a_ref[0], dy_ref[0])
            copy = pltpu.make_async_copy(gds, gd_ref.at[e], gsem)
            copy.start()
            copy.wait()

    def mine(block):
        return pl.BlockSpec((1,) + block, lambda f, i: (e, 0, 0))

    def chunk(rows):
        return pl.BlockSpec((1, rows, fc), lambda f, i: (e, 0, base + f))

    return pl.pallas_call(
        kernel,
        out_shape=(
            sds((local, piece, hidden), F32),
            sds((local, piece, hidden), F32),
            sds((local, fc, width), F32),
        ),
        grid_spec=pltpu.PrefetchScalarGridSpec(
            num_scalar_prefetch=1,
            grid=(steps,),
            in_specs=[
                pl.BlockSpec((1, slots, fc), lambda f, i: (e, 0, i[1])),
                chunk(slots),
                chunk(slots),
                mine((slots, width)),
                mine((slots, piece)),
                mine((many, width)),
                mine((many, width)),
                mine((many, piece)),
                chunk(width),
                chunk(width),
                pl.BlockSpec((1, fc, width), lambda f, i: (e, base + f, 0)),
            ]
            + [ANY_SPEC] * len(done),
            out_specs=(chunk(piece), chunk(piece), ANY_SPEC),
            scratch_shapes=[pltpu.VMEM((many, fc), BF16) for _ in range(3)]
            + [pltpu.VMEM((fc, width), F32), pltpu.SemaphoreType.DMA],
        ),
        compiler_params=params(60, ("arbitrary",)),
        cost_estimate=cost(steps * fc * width * (6 * many + 2 * (many + slots)), 15 << 20),
        input_output_aliases={12 + m: m for m in range(len(done))},
        name="expert_grads",
    )(idx, a, dg, du, dy, xd, x_o, dy_o, xd_o, w_gate, w_up, w_down, *done)


def finish(idx, parts, moved, blocks, x1, share, experts_all):
    rows, total = parts[0].shape
    length, width = x1.shape
    rest = total - width
    n, _, both = blocks.shape
    part, low_rows = both // 2, both // 16

    def kernel(idx_ref, s0, s1, s2, s3, m_ref, b_ref, x_ref, sh_ref, out_ref, q_ref, k_ref, v_ref,
               o_ref, r_ref, a_ref, f_ref, gate_ref, up_ref, down_ref, small):
        out_ref[...] = (x_ref[...] + sh_ref[...].astype(F32)).astype(BF16)
        for k in range(n):
            block = m_ref[k, :rows].astype(F32)
            gate_ref[:, k * part : (k + 1) * part] = block[:, :part]
            up_ref[:, k * part : (k + 1) * part] = block[:, part:]
            low = b_ref[k, rows:].astype(F32)
            at, half = k * low_rows, low_rows // 2
            down_ref[at : at + low_rows, :both] = low[:low_rows]
            down_ref[at : at + half, both:] = low[low_rows:, :part]
            down_ref[at + half : at + low_rows, both:] = low[low_rows:, part:]
        z = idx_ref[1]
        for r, s in enumerate((s0, s1, s2, s3)):
            small[(z - r + 4) & 3] = s[:, width:].astype(F32)
            for m, ref in enumerate((q_ref, k_ref, v_ref, o_ref)):

                @pl.when(((z - r + 4) & 3) == m)
                def _(ref=ref, s=s):
                    ref[...] = s[:, :width].astype(F32)

        low = small[0]
        square = jnp.concatenate([low, jnp.zeros((rows, 128 - rest), F32)], axis=1)
        square = jnp.concatenate([square, jnp.zeros((128 - rows, 128), F32)], axis=0).T
        r_ref[...] = square[:experts_all, :rows]
        a_ref[...] = square[experts_all : experts_all + 1, :rows]
        f_ref[...] = square[experts_all + 1 : experts_all + 2, :rows]

    flat = sds((rows, width), F32)
    line = sds((1, rows), F32)
    wide = sds((rows, n * part), F32)
    return pl.pallas_call(
        kernel,
        out_shape=(
            sds((length, width), BF16),
            flat, flat, flat, flat,
            sds((experts_all, rows), F32),
            line, line,
            wide, wide, sds((n * low_rows, width), F32),
        ),
        in_specs=[SMEM_SPEC] + [VMEM_SPEC] * 8,
        out_specs=(VMEM_SPEC,) * 11,
        scratch_shapes=[pltpu.VMEM((4, rows, rest), F32)],
        compiler_params=params(60),
        name="finish",
    )(idx, *parts, moved, blocks, x1, share)


def on_device(
    tokens,
    segment_ids,
    padding,
    routes,
    w_query,
    w_key,
    w_value,
    w_out,
    w_router,
    shared_gate,
    shared_up,
    shared_down,
    gain_attn,
    gain_ffn,
    expert_gate,
    expert_up,
    expert_down,
    cotangent,
):
    length, width = tokens.shape
    planes = lax.axis_size("dp")
    i = lax.axis_index("expert").astype(jnp.int32)
    z = lax.axis_index("dp").astype(jnp.int32)
    idx = jnp.stack([i, z])
    step = width // 8
    part = shared_down.shape[0]
    spread = planes == 4

    attn_shard = pack_shard([w_query, w_key, w_value, w_out], w_router.T)

    live_row = padding.astype(F32)
    meta = jnp.concatenate([routes[:, 0], routes[:, 1], padding[0]]).astype(BF16)[None, :]
    grad_ext = jnp.concatenate([after(cotangent, attn_shard), meta, jnp.zeros((15, width), BF16)], axis=0)
    ext = grad_ext.shape[0]

    def others(columns):
        at = [(z - r) % planes for r in (1, 2, 3)]
        return jnp.concatenate([lax.dynamic_index_in_dim(columns, a, 0, False) for a in at], axis=0)

    def copies(rows):
        return jnp.broadcast_to(rows[None], (planes,) + rows.shape)

    def columns(blocks):
        return lax.all_to_all(blocks, "dp", split_axis=0, concat_axis=0, tiled=True)

    def dp_gather(rows):
        return lax.all_gather(rows, "dp", axis=0)

    g_mine = lax.all_gather(grad_ext, "expert", axis=0, axis_index_groups=same_core())
    g_far = [shift(grad_ext, k) for k in (1, 2, 3)] if spread else []
    attn_pieces = relay_gather(attn_shard)

    gain1, gain2 = gain_attn[None, :], gain_ffn[None, :]
    side = pack_side(shared_gate, shared_up, part)
    side = after(side, [p for _, _, p in attn_pieces], gain1, gain2, live_row, g_far)
    side = lax.all_to_all(side, "expert", split_axis=0, concat_axis=0, tiled=True)

    *saved, router_t, h2_copies = attention_forward(
        idx, tokens, segment_ids, live_row, gain1, gain2, attn_pieces,
    )
    x1, h2 = saved[6], saved[7]

    g_plane = [g_mine, swap(g_mine, 1)]
    if spread:
        g_far = jnp.concatenate(after(g_far, h2), axis=0)
    side = after(side, h2)
    h_mine = chips_exchange(after(h2_copies, side))
    if spread:
        h_mine = after(h_mine, g_far)
    h_plane = [h_mine, swap(h_mine, 1)]
    if spread:
        h_columns = dp_gather(h2)
        at = (i // 2) ^ 3
        corner = [
            lax.dynamic_index_in_dim(rows, at, 0, False) for rows in after((g_mine, h_mine), h_plane)
        ]
        corner = dp_gather(jnp.concatenate(corner, axis=0))
        g_far = after(g_far, h_plane)
        g_far = [g_far, swap(g_far, 2), swap(g_far, 4)]

    cut = width // 4
    x_own, xd_own, gs_own, cs_own, hot = dispatch_plane(
        idx, router_t, h_plane, g_plane, cut
    )

    weights = (expert_gate, expert_up, expert_down)
    a, dg, du, dy, yc, dr, dc = experts(x_own, gs_own, cs_own, *weights)
    shared_w = after(side, yc)
    if spread:
        g_far, h_columns = after((g_far, h_columns), yc)
        shared_w = after(shared_w, g_far)
        g_far = both_cores(g_far)
        h_far = others(h_columns)
        h_far = [h_far, swap(h_far, 2), swap(h_far, 4)]
    act, side = shared_branch(idx, h_plane, g_plane, shared_w, shared_down)
    if spread:
        side = lax.psum_scatter(side, "dp", scatter_dimension=0, tiled=True)
    else:
        side = lax.psum(side, "dp")

    def exchanged(blocks):
        return lax.all_to_all(blocks, "expert", split_axis=0, concat_axis=0, tiled=True)

    if spread:
        g_far = after(g_far, act)
        act = after(act, g_far)
    out_shares, dh_other, dh_mine = combine(
        idx, act, hot, yc, dr, dc, shared_w, shared_down
    )
    if spread:
        h_far = after(h_far, dh_other)
        dh_other = after(dh_other, h_far)
    dh_came = swap(dh_other, 1)
    if spread:
        h_far = both_cores(after(h_far, dh_came))
    dh_sums = plane_near(dh_mine, dh_came)
    dh_parts = plane_far(dh_sums)
    if spread:
        h_far, g_far, corner = after((h_far, g_far, corner), dh_sums)
        corners = both_cores([corner])
        x_far, xd_far, dy_far = dispatch_others(idx, router_t, h_far, g_far, corners, 3, cut)
        dh_parts = after(dh_parts, x_far)
    out_shares = out_shares.reshape(8 * length, width)
    grad_tokens, att_other, att_mine = attention_backward(
        idx, tokens, cotangent, live_row, gain1, gain2, saved, router_t, dh_parts, attn_pieces,
    )
    att_came = swap(att_other, 1)
    if spread:
        side = dp_gather(after(side, att_mine)).reshape(8, -1, 2 * part)
    att_sums = plane_near(att_mine, att_came)
    att_parts = plane_far(att_sums)
    def att_quarters(parts):
        att = add(parts).astype(BF16)
        small = att[:, 4 * width :]
        return jnp.stack(
            [
                jnp.concatenate(
                    [att[:, m * width : (m + 1) * width], small[:, 32 * m : 32 * (m + 1)]], axis=1
                )
                for m in range(4)
            ]
        )

    if spread:
        xs = (x_far, dy_far, xd_far)
        own = (a, dg, du, dy, xd_own)
        chunks = expert_gate.shape[2] // 512
        done = expert_grads(idx, 0, 0, chunks, own, after(xs, att_sums), weights)
        att_parts = after(att_parts, done)
        out_share = lax.psum_scatter(
            after(out_shares, att_sums), "expert", scatter_dimension=0, tiled=True
        )
        xs = after(xs, att_parts)
        att_scattered = dp_scatter(att_quarters(att_parts))
        done = expert_grads(idx, 1, 0, chunks // 2, own, xs, weights, done)
        att_scattered, side = after((att_scattered, side), done)
        moved = exchanged(side)
        xs = after(xs, att_scattered)
        att_spread = dp_spread(att_scattered)
        done = expert_grads(idx, 1, chunks // 2, chunks // 2, own, xs, weights, done)
        moved, side, att_spread, out_share = after((moved, side, att_spread, out_share), done)
        g_gate, g_up, g_down = done
        order = idx
    else:
        att_spread = dp_whole(att_quarters(att_parts))
        moved = exchanged(side)
        out_share = lax.psum_scatter(out_shares, "expert", scatter_dimension=0, tiled=True)
        order = idx * jnp.array([1, 0], jnp.int32)

        def scattered(left, right):
            local = jnp.einsum("end,enf->edf", left, right, preferred_element_type=F32)
            return lax.psum_scatter(
                local.astype(BF16), "dp", scatter_dimension=1, tiled=True
            ).astype(F32)

        g_gate, g_up, g_down = scattered(x_own, dg), scattered(x_own, du), scattered(a, dy)

    experts_all = w_router.shape[1]
    (
        output, gq, gk, gv, go, g_router, g_gain1, g_gain2, g_sgate, g_sup, g_sdown,
    ) = finish(order, att_spread, moved, side, x1, out_share, experts_all)
    return (
        output,
        grad_tokens,
        gq,
        gk,
        gv,
        go,
        g_router.T,
        g_sgate,
        g_sup,
        g_sdown,
        g_gain1.reshape(step),
        g_gain2.reshape(step),
        g_gate,
        g_up,
        g_down,
    )


def solution(mesh):
    both = P(("dp", "expert"), None)
    one = P("expert", None)
    three = P("expert", None, None)
    sliced = P("expert", "dp", None)
    return jax.shard_map(
        on_device,
        mesh=mesh,
        in_specs=(both,) * 4 + (one,) * 8 + (P(), P()) + (three,) * 3 + (both,),
        out_specs=(both, both) + (one,) * 8 + (P("expert"), P("expert")) + (sliced,) * 3,
        check_vma=False,
    )
```

```python
import numpy as np

import jax
import jax.numpy as jnp
from jax import lax
from jax.experimental import pallas as pl
from jax.experimental.pallas import tpu as pltpu
from jax.sharding import PartitionSpec as P

HEADS = 12
HEAD_DIM = 64
CAP = 64
TILE = 1536
UNROLL = 2
EPS = 1e-06
ROPE_BASE = 10000.0
MASKED = -1e30
SCALE = HEAD_DIM**-0.5
F32 = jnp.float32
BF16 = jnp.bfloat16
MIB = 1 << 20
VMEM_SPEC = pl.BlockSpec(memory_space=pltpu.VMEM)
SMEM_SPEC = pl.BlockSpec(memory_space=pltpu.SMEM)
ANY_SPEC = pl.BlockSpec(memory_space=pl.ANY)


def nn(a, b):
    return jnp.dot(a, b, preferred_element_type=F32)


def nt(a, b):
    return lax.dot_general(a, b, (((1,), (1,)), ((), ())), preferred_element_type=F32)


def tn(a, b):
    return lax.dot_general(a, b, (((0,), (0,)), ((), ())), preferred_element_type=F32)


def sds(shape, dtype):
    return jax.ShapeDtypeStruct(shape, dtype)


def cost(flops, nbytes):
    return pl.CostEstimate(flops=int(flops), bytes_accessed=int(nbytes), transcendentals=0)


def params(mib, semantics=None):
    return pltpu.CompilerParams(vmem_limit_bytes=mib * MIB, dimension_semantics=semantics)


def swap(x, k):
    n = lax.axis_size("expert")
    return lax.ppermute(x, "expert", [(j, j ^ k) for j in range(n)])


def shift(x, k):
    n = lax.axis_size("dp")
    return lax.ppermute(x, "dp", [(j, (j + k) % n) for j in range(n)])


def after(value, *first):
    return lax.optimization_barrier((value, first))[0]


def relay_gather(x):
    half = x.shape[0] // 32 * 16
    a, b = swap(x, 2), swap(x, 4)
    d0, d1 = swap(a[:half], 4), swap(b[half:], 2)
    near = [(0, 0, x), (2, 0, a), (4, 0, b), (6, 0, d0), (6, half, d1)]
    return near + [(k + 1, at, swap(piece, 1)) for k, at, piece in near]


def same_core():
    n = lax.axis_size("expert")
    return [list(range(c, n, 2)) for c in range(2)]


def chips_exchange(blocks):
    return lax.all_to_all(
        blocks, "expert", split_axis=0, concat_axis=0, tiled=True, axis_index_groups=same_core()
    )


def both_cores(near):
    other = [swap(p, 1) for p in near]
    return [p for pair in zip(near, other) for p in pair]


def plane_near(even, came):
    return [add([even[j], came[j]]).astype(even.dtype) for j in range(4)]


def plane_far(sums):
    return [sums[0], swap(sums[1], 2), swap(sums[2], 4), swap(sums[3], 6)]


def dp_scatter(quarters):
    z = lax.axis_index("dp")
    parts = [lax.dynamic_index_in_dim(quarters, (z + k) % 4, 0, False) for k in range(4)]
    return [parts[0]] + [shift(parts[k], k) for k in (1, 2, 3)]


def dp_spread(parts):
    total = add(parts).astype(parts[0].dtype)
    return [total] + [shift(total, k) for k in (1, 2, 3)]


def dp_whole(quarters):
    whole = lax.psum(quarters, "dp")
    return [whole[0], whole[3], whole[2], whole[1]]


def add(parts):
    total = parts[0].astype(F32)
    for p in parts[1:]:
        total = total + p.astype(F32)
    return total


def norm_scale(values):
    return lax.rsqrt(jnp.mean(values * values, axis=-1, keepdims=True) + EPS)


def silu_parts(gate):
    logistic = 0.5 * jnp.tanh(0.5 * gate) + 0.5
    silu = gate * logistic
    return silu, logistic + silu * (1.0 - logistic)


def split_heads(x, first):
    zero = jnp.zeros_like(x)
    return jnp.concatenate([jnp.where(first, x, zero), jnp.where(first, zero, x)], axis=0)


def half_swap(x):
    lane = lax.broadcasted_iota(jnp.int32, x.shape, 1)
    half = HEAD_DIM // 2
    return jnp.where(
        lane % HEAD_DIM < half, pltpu.roll(x, x.shape[1] - half, 1), pltpu.roll(x, half, 1)
    )


def place_copies(i, layout, step, refs, target, sems):
    copies = []
    for n, ((k, at, rows), ref) in enumerate(zip(layout, refs)):
        start = pl.multiple_of((i ^ k) * step + at, 16)
        copies.append(pltpu.make_async_copy(ref, target.at[pl.ds(start, rows), :], sems.at[n]))
    return copies


def layout_of(pieces):
    return tuple((k, at, piece.shape[0]) for k, at, piece in pieces)


def rope_tables(length):
    half = HEAD_DIM // 2
    frequency = (ROPE_BASE ** (-(2.0 * np.arange(half, dtype=np.float32)) / HEAD_DIM)).astype(
        np.float32
    )
    angles = (np.arange(length, dtype=np.float32)[:, None] * frequency[None, :]).astype(np.float32)
    cosine, sine = np.cos(angles), np.sin(angles)
    return (
        np.concatenate([cosine] * 4, 1).astype(np.float32),
        np.concatenate([-sine, sine, -sine, sine], 1).astype(np.float32),
    )


def pack_shard(projections, router):
    rows, width = projections[0].shape
    n = len(projections)

    def kernel(*refs):
        out = refs[-1]
        for m in range(n):
            out[:, m * width : (m + 1) * width] = refs[m][...].astype(BF16)
        lines = jnp.concatenate(
            [refs[n][...], jnp.zeros((router.shape[0], 128 - rows), F32)], axis=1
        )
        lines = jnp.concatenate([lines, jnp.zeros((128 - router.shape[0], 128), F32)], axis=0)
        out[:, n * width :] = lines.T[:rows].astype(BF16)

    return pl.pallas_call(
        kernel,
        out_shape=sds((rows, n * width + 128), BF16),
        in_specs=[VMEM_SPEC] * (n + 1),
        out_specs=VMEM_SPEC,
        compiler_params=params(60),
        cost_estimate=cost(1, 1 << 20),
        name="pack_shard",
    )(*projections, router)


def pack_side(gate, up, part):
    step, wide = gate.shape

    def kernel(g_ref, u_ref, out_ref):
        for k in range(wide // part):
            out_ref[k, 0] = g_ref[:, k * part : (k + 1) * part].astype(BF16)
            out_ref[k, 1] = u_ref[:, k * part : (k + 1) * part].astype(BF16)

    return pl.pallas_call(
        kernel,
        out_shape=sds((wide // part, 2, step, part), BF16),
        in_specs=[VMEM_SPEC] * 2,
        out_specs=VMEM_SPEC,
        compiler_params=params(60),
        cost_estimate=cost(1, 1 << 20),
        name="pack_side",
    )(gate, up)


def attention_forward(idx, tokens, seg_row, live_row, gain1, gain2, pieces):
    layout = layout_of(pieces)
    n = len(layout)
    length, width = tokens.shape
    step = width // 8
    cosine, sine = rope_tables(length)

    def kernel(idx_ref, x_ref, sr_ref, lv_ref, g1_ref, g2_ref, cos_ref, sin_ref, *refs):
        piece_refs, refs = refs[:n], refs[n:]
        h1_ref, q_ref, k_ref, v_ref, o_ref, p_ref, x1_ref, h2_ref, wr_ref, h4_ref = refs[:10]
        wbuf, pre, probs, sems, psem = refs[10:]
        copies = place_copies(idx_ref[0], layout, step, piece_refs, wbuf, sems)
        for c in copies:
            c.start()
        x = x_ref[...].astype(F32)
        h1 = (x * norm_scale(x) * g1_ref[...]).astype(BF16)
        h1_ref[...] = h1
        row = lax.broadcasted_iota(jnp.int32, (length, length), 0)
        col = lax.broadcasted_iota(jnp.int32, (length, length), 1)
        seg = sr_ref[...].astype(F32)
        seg_col = jnp.broadcast_to(seg, (8, length)).T[:, 0:1]
        allowed = (col == row) | ((col <= row) & (seg == seg_col) & (lv_ref[...] > 0.0))
        bias = jnp.where(allowed, 0.0, MASKED)
        for c in copies:
            c.wait()
        pre[...] = nn(h1, wbuf[:, : 3 * width])
        first = lax.broadcasted_iota(jnp.int32, (length, 128), 1) < HEAD_DIM

        def pair(hp, carry):
            at = pl.multiple_of(hp * 128, 128)
            qp = pre[:, pl.ds(at, 128)]
            kp = pre[:, pl.ds(at + width, 128)]
            v = pre[:, pl.ds(at + 2 * width, 128)].astype(BF16)
            cosv, sinv = cos_ref[...], sin_ref[...]
            q = (qp * cosv + half_swap(qp) * sinv).astype(BF16)
            k = (kp * cosv + half_swap(kp) * sinv).astype(BF16)
            q_ref[:, pl.ds(at, 128)] = q
            k_ref[:, pl.ds(at, 128)] = k
            v_ref[:, pl.ds(at, 128)] = v
            scores = nt(split_heads(q, first), k) * SCALE
            scores = scores.reshape(2, length, length) + bias
            e = jnp.exp(scores - jnp.max(scores, axis=-1, keepdims=True))
            p = e / jnp.sum(e, axis=-1, keepdims=True)
            probs[pl.ds(2 * hp, 2)] = p
            pltpu.make_async_copy(
                probs.at[pl.ds(2 * hp, 2)], p_ref.at[pl.ds(2 * hp, 2)], psem.at[hp]
            ).start()
            low = p.astype(BF16)
            mixed = nn(jnp.concatenate([low[0], low[1]], axis=1), split_heads(v, first))
            o_ref[:, pl.ds(at, 128)] = mixed.astype(BF16)
            return carry

        lax.fori_loop(0, HEADS // 2, pair, 0, unroll=UNROLL)
        x1 = x + nn(o_ref[...], wbuf[:, 3 * width : 4 * width])
        x1_ref[...] = x1
        h2 = (x1 * norm_scale(x1) * g2_ref[...]).astype(BF16)
        h2_ref[...] = h2
        for chip in range(4):
            h4_ref[chip] = h2
        wr_ref[...] = wbuf[:, 4 * width :].astype(F32).T[:16].astype(BF16)
        for hp in range(HEADS // 2):
            pltpu.make_async_copy(
                probs.at[pl.ds(2 * hp, 2)], p_ref.at[pl.ds(2 * hp, 2)], psem.at[hp]
            ).wait()

    flat = sds((length, width), BF16)
    return pl.pallas_call(
        kernel,
        out_shape=(
            flat, flat, flat, flat, flat,
            sds((HEADS, length, length), F32),
            sds((length, width), F32),
            flat,
            sds((16, width), BF16),
            sds((4, length, width), BF16),
        ),
        in_specs=[SMEM_SPEC] + [VMEM_SPEC] * 7 + [ANY_SPEC] * n,
        out_specs=(VMEM_SPEC,) * 5 + (ANY_SPEC,) + (VMEM_SPEC,) * 4,
        scratch_shapes=[
            pltpu.VMEM((width, pieces[0][2].shape[1]), BF16),
            pltpu.VMEM((length, 3 * width), F32),
            pltpu.VMEM((HEADS, length, length), F32),
            pltpu.SemaphoreType.DMA((n,)),
            pltpu.SemaphoreType.DMA((HEADS // 2,)),
        ],
        compiler_params=params(60),
        cost_estimate=cost(8 * length * width * width, 12 << 20),
        name="attention_forward",
    )(idx, tokens, seg_row, live_row, gain1, gain2, cosine, sine,
      *[p for _, _, p in pieces])


def route_rows(meta, prob, le, i, upper, length):
    expert = (2 * i + le).astype(F32)
    hit = (meta[:, :length] == expert) | (meta[:, length : 2 * length] == expert)
    hot = jnp.where(hit, 1.0, 0.0)
    rank = nn(jnp.broadcast_to(hot, (16, length)).astype(BF16), upper)[0:1]
    slot = lax.broadcasted_iota(jnp.int32, (CAP, length), 0).astype(F32) + 1.0
    one = jnp.where((slot == rank) & hit, 1.0, 0.0)
    which = lax.broadcasted_iota(jnp.int32, prob.shape, 0) == 2 * i + le
    weight = jnp.sum(jnp.where(which, prob, 0.0), axis=0, keepdims=True)
    return one, weight * meta[:, 2 * length :]


def router_probs(router_t, rows):
    logits = nt(router_t, rows)
    e = jnp.exp(logits - jnp.max(logits, axis=0, keepdims=True))
    return e / jnp.sum(e, axis=0, keepdims=True)


def upper_ones(length):
    return jnp.where(
        lax.broadcasted_iota(jnp.int32, (length, length), 0)
        <= lax.broadcasted_iota(jnp.int32, (length, length), 1),
        1.0,
        0.0,
    ).astype(BF16)


def dispatch_plane(idx, router_t, rows, grads, piece):
    _, length, width = rows[0].shape
    slots = 8 * CAP
    ext = length + 16

    def kernel(idx_ref, wr_ref, *refs):
        hp, gp, refs = refs[:2], refs[2:4], refs[4:]
        x_ref, xd_ref, gs_ref, cs_ref, hot_ref, hall, gall, sems = refs
        i = idx_ref[0]
        copies = []
        for c in range(2):
            copies.append(pltpu.make_async_copy(hp[c], hall.at[pl.ds(4 * c, 4)], sems.at[c]))
            copies.append(pltpu.make_async_copy(gp[c], gall.at[pl.ds(4 * c, 4)], sems.at[2 + c]))
        for c in copies:
            c.start()
        upper = upper_ones(length)
        turn = (width - idx_ref[1] * piece) % width
        for c in copies:
            c.wait()

        def sequences(pair, carry):
            for k in (2 * pair, 2 * pair + 1):
                h = hall[k]
                prob = router_probs(wr_ref[...], h)
                meta = gall[k, length:ext][0:1].astype(F32)
                at = pl.multiple_of(k * CAP, CAP)
                ones = []
                for le in range(2):
                    one, weight = route_rows(meta, prob, le, i, upper, length)
                    col = jnp.sum(one * weight, axis=1, keepdims=True)
                    cs_ref[le, pl.ds(at, CAP), :] = jnp.broadcast_to(col, (CAP, 128))
                    ones.append(one.astype(BF16))
                hot = jnp.concatenate(ones, axis=0)
                hot_ref[k] = hot
                picked = nn(hot, h)
                cut = pltpu.roll(picked, turn, 1)[:, :piece].astype(BF16)
                picked = picked.astype(BF16)
                grads = nn(hot, gall[k, 0:length]).astype(BF16)
                for le in range(2):
                    mine = slice(le * CAP, (le + 1) * CAP)
                    x_ref[le, pl.ds(at, CAP), :] = picked[mine]
                    xd_ref[le, pl.ds(at, CAP), :] = cut[mine]
                    gs_ref[le, pl.ds(at, CAP), :] = grads[mine]
            return carry

        lax.fori_loop(0, 4, sequences, 0, unroll=UNROLL)

    return pl.pallas_call(
        kernel,
        out_shape=(
            sds((2, slots, width), BF16),
            sds((2, slots, piece), BF16),
            sds((2, slots, width), BF16),
            sds((2, slots, 128), F32),
            sds((8, 2 * CAP, length), BF16),
        ),
        in_specs=[SMEM_SPEC, VMEM_SPEC] + [ANY_SPEC] * 4,
        out_specs=(VMEM_SPEC,) * 5,
        scratch_shapes=[
            pltpu.VMEM((8, length, width), BF16),
            pltpu.VMEM((8, ext, width), BF16),
            pltpu.SemaphoreType.DMA((4,)),
        ],
        compiler_params=params(60),
        cost_estimate=cost(8 * 4 * 2 * CAP * length * width, 16 << 20),
        name="dispatch_plane",
    )(idx, router_t, *rows, *grads)


def dispatch_others(idx, router_t, h_pieces, g_pieces, corners, planes, piece):
    width = h_pieces[0].shape[1]
    length = h_pieces[0].shape[0] // planes
    ext = length + 16
    slots = 8 * planes * CAP

    def kernel(idx_ref, wr_ref, *refs):
        hp, gp, both, refs = refs[:6], refs[6:12], refs[12:14], refs[14:]
        x_out, xd_out, dy_out, hall, gall, hsems, gsems, x_ref, xd_ref, dy_ref, osems = refs
        i = idx_ref[0]

        def leaving(k):
            rows = pl.ds(pl.multiple_of(k * planes * CAP, CAP), planes * CAP)
            for m, (a, b) in enumerate(((x_ref, x_out), (xd_ref, xd_out), (dy_ref, dy_out))):
                yield pltpu.make_async_copy(a.at[:, rows], b.at[:, rows], osems.at[k, m])

        def copies(k):
            if k < 6:
                yield pltpu.make_async_copy(hp[k], hall.at[k], hsems.at[k, 0])
                yield pltpu.make_async_copy(gp[k], gall.at[k], gsems.at[k, 0])
                return
            for s in range(planes):
                plane = (idx_ref[1] - s + 3) & 3
                yield pltpu.make_async_copy(
                    both[k - 6].at[plane, pl.ds(0, ext)],
                    gall.at[k, pl.ds(s * ext, ext)],
                    gsems.at[k, s],
                )
                yield pltpu.make_async_copy(
                    both[k - 6].at[plane, pl.ds(ext, length)],
                    hall.at[k, pl.ds(s * length, length)],
                    hsems.at[k, s],
                )

        for k in range(8):
            for c in copies(k):
                c.start()
        upper = upper_ones(length)
        turn = (width - idx_ref[1] * piece) % width

        def column(k, carry):
            @pl.when(k < 6)
            def _():
                pltpu.make_async_copy(hall.at[k], hall.at[k], hsems.at[k, 0]).wait()
                pltpu.make_async_copy(gall.at[k], gall.at[k], gsems.at[k, 0]).wait()

            @pl.when(k >= 6)
            def _():
                for s in range(planes):
                    h = hall.at[k, pl.ds(s * length, length)]
                    g = gall.at[k, pl.ds(s * ext, ext)]
                    pltpu.make_async_copy(h, h, hsems.at[k, s]).wait()
                    pltpu.make_async_copy(g, g, gsems.at[k, s]).wait()

            for s in range(planes):
                h = hall[k, s * length : (s + 1) * length]
                g = gall[k, s * ext : s * ext + length]
                meta = gall[k, s * ext + length : (s + 1) * ext][0:1].astype(F32)
                prob = router_probs(wr_ref[...], h)
                ones, cols = [], []
                for le in range(2):
                    one, weight = route_rows(meta, prob, le, i, upper, length)
                    cols.append(jnp.sum(one * weight, axis=1, keepdims=True))
                    ones.append(one.astype(BF16))
                hot = jnp.concatenate(ones, axis=0)
                picked = nn(hot, h)
                cut = pltpu.roll(picked, turn, 1)[:, :piece].astype(BF16)
                picked = picked.astype(BF16)
                dy = (nn(hot, g) * jnp.concatenate(cols, axis=0)).astype(BF16)
                at = pl.ds(pl.multiple_of((k * planes + s) * CAP, CAP), CAP)
                for le in range(2):
                    mine = slice(le * CAP, (le + 1) * CAP)
                    x_ref[le, at] = picked[mine]
                    xd_ref[le, at] = cut[mine]
                    dy_ref[le, at] = dy[mine]
            for c in leaving(k):
                c.start()
            return carry

        lax.fori_loop(0, 8, column, 0, unroll=UNROLL)
        for k in range(8):
            for c in leaving(k):
                c.wait()

    return pl.pallas_call(
        kernel,
        out_shape=(
            sds((2, slots, width), BF16),
            sds((2, slots, piece), BF16),
            sds((2, slots, width), BF16),
        ),
        in_specs=[SMEM_SPEC, VMEM_SPEC] + [ANY_SPEC] * 14,
        out_specs=(ANY_SPEC,) * 3,
        scratch_shapes=[
            pltpu.VMEM((8, planes * length, width), BF16),
            pltpu.VMEM((8, planes * ext, width), BF16),
            pltpu.SemaphoreType.DMA((8, planes)),
            pltpu.SemaphoreType.DMA((8, planes)),
            pltpu.VMEM((2, slots, width), BF16),
            pltpu.VMEM((2, slots, piece), BF16),
            pltpu.VMEM((2, slots, width), BF16),
            pltpu.SemaphoreType.DMA((8, 3)),
        ],
        compiler_params=params(60),
        cost_estimate=cost(8 * planes * 4 * 2 * CAP * length * width, 28 << 20),
        name="dispatch_others",
    )(idx, router_t, *h_pieces, *g_pieces, *corners)


def experts(x, gs, cs, w_gate, w_up, w_down):
    local, slots, width = x.shape
    hidden = w_gate.shape[2]
    fc = 512
    steps = hidden // fc

    def kernel(x_ref, gs_ref, cs_ref, wg_ref, wu_ref, wd_ref,
               a_ref, dg_ref, du_ref, dy_ref, yc_ref, dr_ref, dc_ref, yacc, dracc):
        f = pl.program_id(1)

        @pl.when(f == 0)
        def _():
            weight = cs_ref[0][:, 0:1]
            dy_ref[0] = (weight * gs_ref[0].astype(F32)).astype(BF16)
            yacc[...] = jnp.zeros_like(yacc)
            dracc[...] = jnp.zeros_like(dracc)

        rows, dy = x_ref[0], dy_ref[0]
        wg, wu, wd = wg_ref[0], wu_ref[0], wd_ref[0]
        g = nn(rows, wg)
        u = nn(rows, wu)
        da = nt(dy, wd)
        silu, slope = silu_parts(g)
        a = (silu * u).astype(BF16)
        dg = (da * u * slope).astype(BF16)
        du = (da * silu).astype(BF16)
        a_ref[0] = a
        dg_ref[0] = dg
        du_ref[0] = du
        yacc[...] += nn(a, wd)
        dracc[...] += nt(dg, wg) + nt(du, wu)

        @pl.when(f == steps - 1)
        def _():
            y = yacc[...].astype(BF16).astype(F32)
            weight = cs_ref[0][:, 0:1]
            yc_ref[0] = (weight * y).astype(BF16)
            dr_ref[0] = dracc[...].astype(BF16)
            dc = jnp.sum(gs_ref[0].astype(F32) * y, axis=1, keepdims=True)
            dc_ref[0] = jnp.broadcast_to(dc, (slots, 128))

    def whole(last):
        return pl.BlockSpec((1, slots, last), lambda e, f: (e, 0, 0))

    chunk = pl.BlockSpec((1, slots, fc), lambda e, f: (e, 0, f))
    wide = sds((local, slots, hidden), BF16)
    row = sds((local, slots, width), BF16)
    return pl.pallas_call(
        kernel,
        grid=(local, steps),
        out_shape=(wide, wide, wide, row, row, row, sds((local, slots, 128), F32)),
        in_specs=[
            whole(width),
            whole(width),
            whole(128),
            pl.BlockSpec((1, width, fc), lambda e, f: (e, 0, f)),
            pl.BlockSpec((1, width, fc), lambda e, f: (e, 0, f)),
            pl.BlockSpec((1, fc, width), lambda e, f: (e, f, 0)),
        ],
        out_specs=(chunk, chunk, chunk, whole(width), whole(width), whole(width), whole(128)),
        scratch_shapes=[pltpu.VMEM((slots, width), F32), pltpu.VMEM((slots, width), F32)],
        compiler_params=params(60, ("arbitrary", "arbitrary")),
        cost_estimate=cost(12 * local * slots * width * hidden, 40 << 20),
        name="experts",
    )(x, gs, cs, w_gate, w_up, w_down)


def chip_order(g, i):
    return jnp.where(g < 4, 4, 0) + ((g & 3) ^ (i[0] >> 1))


def whole_block(shape):
    return pl.BlockSpec(shape, lambda g, i: (0,) * len(shape))


def shared_branch(idx, rows, grads, shared, down):
    _, length, width = rows[0].shape
    ext = grads[0].shape[1]
    part = down.shape[0]
    step = width // 8

    def kernel(idx_ref, h_mine, h_other, g_mine, g_other, ws_ref, wd_ref,
               act_ref, gs_ref, gdacc, gsacc, wdown):
        s = pl.program_id(0)

        @pl.when(s == 0)
        def _():
            gdacc[...] = jnp.zeros_like(gdacc)
            gsacc[...] = jnp.zeros_like(gsacc)
            wdown[...] = wd_ref[...].astype(BF16)

        h = jnp.where(s == 0, h_mine[...], h_other[...]).reshape(4 * length, width)
        grad = jnp.where(s == 0, g_mine[...], g_other[...])[:, :length].reshape(4 * length, width)
        gate = nn(h, ws_ref[:, 0].reshape(width, part))
        up = nn(h, ws_ref[:, 1].reshape(width, part))
        da = nt(grad, wdown[...])
        silu, slope = silu_parts(gate)
        a = (silu * up).astype(BF16)
        dg = (da * up * slope).astype(BF16)
        du = (da * silu).astype(BF16)
        both = jnp.concatenate([dg, du], axis=1)
        act_ref[:, :, :part] = a.reshape(4, length, part)
        act_ref[:, :, part:] = both.reshape(4, length, 2 * part)
        gdacc[...] += tn(a, grad)
        gsacc[...] += tn(h, both)

        @pl.when(s == 1)
        def _():
            rows, wide = part // 8, 2 * part
            for k in range(8):
                gs_ref[k, :step] = gsacc[k * step : (k + 1) * step, :].astype(BF16)
                low = gdacc[k * rows : (k + 1) * rows, :].astype(BF16)
                rest = [low[: rows // 2, wide:], low[rows // 2 :, wide:]]
                gs_ref[k, step : step + rows] = low[:, :wide]
                gs_ref[k, step + rows :] = jnp.concatenate(rest, axis=1)

    return pl.pallas_call(
        kernel,
        out_shape=(
            sds((8, length, 3 * part), BF16),
            sds((8, step + 3 * part // 16, 2 * part), BF16),
        ),
        grid_spec=pltpu.PrefetchScalarGridSpec(
            num_scalar_prefetch=1,
            grid=(2,),
            in_specs=[
                whole_block((4, length, width)),
                whole_block((4, length, width)),
                whole_block((4, ext, width)),
                whole_block((4, ext, width)),
                whole_block((8, 2, step, part)),
                whole_block((part, width)),
            ],
            out_specs=(
                pl.BlockSpec((4, length, 3 * part), lambda g, i: (g, 0, 0)),
                whole_block((8, step + 3 * part // 16, 2 * part)),
            ),
            scratch_shapes=[
                pltpu.VMEM((part, width), F32),
                pltpu.VMEM((width, 2 * part), F32),
                pltpu.VMEM((part, width), BF16),
            ],
        ),
        compiler_params=params(60, ("arbitrary",)),
        cost_estimate=cost(12 * 8 * length * width * part, 14 << 20),
        name="shared_branch",
    )(idx, *rows, *grads, shared, down)


def combine(idx, act, hot, yc, dr, dc, shared, down):
    _, length, _ = act.shape
    part, width = down.shape
    ext = length + 16

    def kernel(idx_ref, act_ref, hot_ref, yc_ref, dr_ref, dc_ref, ws_ref, wd_ref,
               out_ref, do_ref, de_ref, wout, wback):
        s = pl.program_id(0)
        i = idx_ref[0]

        @pl.when(s == 0)
        def _():
            wout[:part] = wd_ref[...].astype(BF16)
            wback[:part] = ws_ref[:, 0].reshape(width, part).T
            wback[part : 2 * part] = ws_ref[:, 1].reshape(width, part).T

        wout[part:] = yc_ref[...].reshape(2 * CAP, width)
        wback[2 * part :] = dr_ref[...].reshape(2 * CAP, width)
        one = hot_ref[0]
        place = one.T
        act = act_ref[0]
        out = nn(jnp.concatenate([act[:, :part], place], axis=1), wout[...])
        out_ref[0] = out.astype(BF16)
        dh = nn(jnp.concatenate([act[:, part:], place], axis=1), wback[...]).astype(BF16)
        dcv = dc_ref[...].reshape(2 * CAP, 128)[:, 0:1] * one.astype(F32)
        expert = lax.broadcasted_iota(jnp.int32, (16, length), 0)
        dp = jnp.zeros((16, length), F32)
        for le in range(2):
            row = jnp.sum(dcv[le * CAP : (le + 1) * CAP], axis=0, keepdims=True)
            dp = dp + jnp.where(expert == 2 * i + le, row, 0.0)

        def put(ref):
            ref[0, :length] = dh
            ref[0, length:] = jnp.zeros((16, width), BF16)
            ref[0, length:, :length] = dp.astype(BF16)

        @pl.when(s < 4)
        def _():
            put(do_ref)

        @pl.when(s >= 4)
        def _():
            put(de_ref)

    def odd(block):
        return pl.BlockSpec((1,) + block, lambda g, i: (jnp.minimum(g, 3), 0, 0))

    def even(block):
        return pl.BlockSpec((1,) + block, lambda g, i: (jnp.maximum(g - 4, 0), 0, 0))

    def slot_spec(last):
        return pl.BlockSpec((2, CAP, last), lambda g, i: (0, chip_order(g, i), 0))

    def device(g, i):
        return 2 * ((g & 3) ^ (i[0] >> 1)) + ((i[0] & 1) ^ jnp.where(g < 4, 1, 0))

    ext4 = sds((4, ext, width), BF16)
    return pl.pallas_call(
        kernel,
        out_shape=(sds((8, length, width), BF16), ext4, ext4),
        grid_spec=pltpu.PrefetchScalarGridSpec(
            num_scalar_prefetch=1,
            grid=(8,),
            in_specs=[
                pl.BlockSpec((1, length, 3 * part), lambda g, i: (chip_order(g, i), 0, 0)),
                pl.BlockSpec((1, 2 * CAP, length), lambda g, i: (chip_order(g, i), 0, 0)),
                slot_spec(width),
                slot_spec(width),
                slot_spec(128),
                whole_block(shared.shape),
                whole_block((part, width)),
            ],
            out_specs=(
                pl.BlockSpec((1, length, width), lambda g, i: (device(g, i), 0, 0)),
                odd((ext, width)),
                even((ext, width)),
            ),
            scratch_shapes=[
                pltpu.VMEM((part + 2 * CAP, width), BF16),
                pltpu.VMEM((2 * part + 2 * CAP, width), BF16),
            ],
        ),
        compiler_params=params(60, ("arbitrary",)),
        cost_estimate=cost(10 * 8 * length * width * part, 18 << 20),
        name="combine",
    )(idx, act, hot, yc, dr, dc, shared, down)


def attention_backward(idx, tokens, grad, live_row, gain1, gain2, saved, router_t, dh_parts,
                       pieces):
    layout = layout_of(pieces)
    n = len(layout)
    length, width = tokens.shape
    step = width // 8
    cosine, sine = rope_tables(length)
    h1, q, k, v, o, prob, x1, h2 = saved
    total = 4 * width + 128

    def kernel(idx_ref, x_ref, g_ref, lv_ref, g1_ref, g2_ref, cos_ref, sin_ref, h1_ref, q_ref,
               k_ref, v_ref, o_ref, p_ref, x1_ref, h2_ref, wr_ref, d0, d1, d2, d3, *refs):
        piece_refs, refs = refs[:n], refs[n:]
        gt_ref, odd_ref, even_ref, wbuf, dmix, dqkv, gbuf, sems, h1b, qkvb, probs, lsem, psem = refs
        i = idx_ref[0]
        late = [pltpu.make_async_copy(h1_ref, h1b, lsem.at[3])]
        for m, ref in enumerate((q_ref, k_ref, v_ref)):
            late.append(pltpu.make_async_copy(ref, qkvb.at[m], lsem.at[m]))

        def prob_copy(hp):
            pairs = pl.ds(2 * hp, 2)
            return pltpu.make_async_copy(p_ref.at[pairs], probs.at[pairs], psem.at[hp])

        copies = place_copies(i, layout, step, piece_refs, wbuf, sems)
        for c in copies + late:
            c.start()
        for hp in range(HEADS // 2):
            prob_copy(hp).start()
        x1v = x1_ref[...]
        r2 = norm_scale(x1v)
        wr = wr_ref[...]
        pr = router_probs(wr, h2_ref[...])
        came = add([d0[...], d1[...], d2[...], d3[...]])
        dp = came[length:, :length] * lv_ref[...]
        dl = (pr * (dp - jnp.sum(pr * dp, axis=0, keepdims=True))).astype(BF16)
        router_grad = nn(dl, h2_ref[...])
        dh2 = came[:length] + tn(dl, wr)
        gain2_grad = jnp.sum(dh2 * x1v * r2, axis=0, keepdims=True)
        weighted = dh2 * g2_ref[...]
        inner = jnp.mean(x1v * weighted, axis=-1, keepdims=True)
        dx1 = g_ref[...].astype(F32) + r2 * weighted - x1v * (r2 * r2 * r2) * inner
        da = dx1.astype(BF16)
        for c in copies:
            c.wait()
        gbuf[:, 3 * width : 4 * width] = tn(o_ref[...], da).astype(BF16)
        dmix[...] = nt(da, wbuf[:, 3 * width : 4 * width]).astype(BF16)
        first = lax.broadcasted_iota(jnp.int32, (length, 128), 1) < HEAD_DIM

        for c in late:
            c.wait()

        def pair(hp, carry):
            prob_copy(hp).wait()
            at = pl.multiple_of(hp * 128, 128)
            qv, kv, vv = (qkvb[m, :, pl.ds(at, 128)] for m in range(3))
            dov = dmix[:, pl.ds(at, 128)]
            p = probs[pl.ds(2 * hp, 2)]
            dos = split_heads(dov, first)
            dp = nt(dos, vv).reshape(2, length, length)
            dv = tn(p.astype(BF16).reshape(2 * length, length), dos)
            ds = p * (dp - jnp.sum(p * dp, axis=-1, keepdims=True))
            ds = (ds * SCALE).astype(BF16)
            dq = nn(jnp.concatenate([ds[0], ds[1]], axis=1), split_heads(kv, first))
            dk = tn(ds.reshape(2 * length, length), split_heads(qv, first))
            cosv, sinv = cos_ref[...], sin_ref[...]
            dqkv[:, pl.ds(at, 128)] = (dq * cosv - half_swap(dq) * sinv).astype(BF16)
            dqkv[:, pl.ds(at + width, 128)] = (dk * cosv - half_swap(dk) * sinv).astype(BF16)
            dqkv[:, pl.ds(at + 2 * width, 128)] = dv.astype(BF16)
            return carry

        lax.fori_loop(0, HEADS // 2, pair, 0, unroll=UNROLL)
        gbuf[:, : 3 * width] = tn(h1b[...], dqkv[...]).astype(BF16)
        dh1 = nt(dqkv[...], wbuf[:, : 3 * width])
        x = x_ref[...].astype(F32)
        r1 = norm_scale(x)
        gain1_grad = jnp.sum(dh1 * x * r1, axis=0, keepdims=True)
        weighted = dh1 * g1_ref[...]
        inner = jnp.mean(x * weighted, axis=-1, keepdims=True)
        gt_ref[...] = (dx1 + r1 * weighted - x * (r1 * r1 * r1) * inner).astype(BF16)
        small = jnp.concatenate(
            [router_grad, gain1_grad, gain2_grad, jnp.zeros((110, width), F32)], axis=0
        )
        gbuf[:, 4 * width :] = small.T.astype(BF16)
        leaving = []
        for kk in range(8):
            rows = gbuf.at[pl.ds(pl.multiple_of((i ^ kk) * step, 16), step), :]
            ref = odd_ref if kk % 2 else even_ref
            leaving.append(pltpu.make_async_copy(rows, ref.at[kk // 2], psem.at[8 + kk]))
        for c in leaving:
            c.start()
        for c in leaving:
            c.wait()

    blocks = sds((4, step, total), BF16)
    return pl.pallas_call(
        kernel,
        out_shape=(sds((length, width), BF16), blocks, blocks),
        in_specs=[SMEM_SPEC] + [VMEM_SPEC] * 7 + [ANY_SPEC] * 4 + [VMEM_SPEC, ANY_SPEC]
        + [VMEM_SPEC] * 7 + [ANY_SPEC] * n,
        out_specs=(VMEM_SPEC, ANY_SPEC, ANY_SPEC),
        scratch_shapes=[
            pltpu.VMEM((width, pieces[0][2].shape[1]), BF16),
            pltpu.VMEM((length, width), BF16),
            pltpu.VMEM((length, 3 * width), BF16),
            pltpu.VMEM((width, total), BF16),
            pltpu.SemaphoreType.DMA((n,)),
            pltpu.VMEM((length, width), BF16),
            pltpu.VMEM((3, length, width), BF16),
            pltpu.VMEM((HEADS, length, length), F32),
            pltpu.SemaphoreType.DMA((4,)),
            pltpu.SemaphoreType.DMA((16,)),
        ],
        compiler_params=params(60),
        cost_estimate=cost(20 * length * width * width, 24 << 20),
        name="attention_backward",
    )(idx, tokens, grad, live_row, gain1, gain2, cosine, sine, h1, q, k, v, o, prob, x1, h2,
      router_t, *dh_parts, *[p for _, _, p in pieces])


def expert_grads(idx, e, base, steps, own, others, weights, done=()):
    w_gate, w_up, w_down = weights
    a, dg, du, dy, xd = own
    x_o, dy_o, xd_o = others
    local, slots, hidden = a.shape
    many = x_o.shape[1]
    width = x_o.shape[2]
    piece = xd.shape[2]
    fc = 512
    tile = TILE

    def kernel(idx_ref, a_ref, dg_ref, du_ref, dy_ref, xd_ref, xo_ref, dyo_ref, xdo_ref,
               wg_ref, wu_ref, wd_ref, *refs):
        gg_ref, gu_ref, gd_ref, ao, dgo, duo, gds, gsem = refs[len(done) :]
        f = pl.program_id(0)
        wg, wu, wd = wg_ref[0], wu_ref[0], wd_ref[0]

        def rows(t, carry):
            at = pl.ds(pl.multiple_of(t * tile, tile), tile)
            g = nn(xo_ref[0, at], wg)
            u = nn(xo_ref[0, at], wu)
            da = nt(dyo_ref[0, at], wd)
            silu, slope = silu_parts(g)
            ao[at] = (silu * u).astype(BF16)
            dgo[at] = (da * u * slope).astype(BF16)
            duo[at] = (da * silu).astype(BF16)
            return carry

        lax.fori_loop(0, many // tile, rows, 0)
        gg_ref[0] = tn(xdo_ref[0], dgo[...]) + tn(xd_ref[0], dg_ref[0])
        gu_ref[0] = tn(xdo_ref[0], duo[...]) + tn(xd_ref[0], du_ref[0])

        @pl.when(base + f == idx_ref[1])
        def _():
            gds[...] = tn(ao[...], dyo_ref[0]) + tn(a_ref[0], dy_ref[0])
            copy = pltpu.make_async_copy(gds, gd_ref.at[e], gsem)
            copy.start()
            copy.wait()

    def mine(block):
        return pl.BlockSpec((1,) + block, lambda f, i: (e, 0, 0))

    def chunk(rows):
        return pl.BlockSpec((1, rows, fc), lambda f, i: (e, 0, base + f))

    return pl.pallas_call(
        kernel,
        out_shape=(
            sds((local, piece, hidden), F32),
            sds((local, piece, hidden), F32),
            sds((local, fc, width), F32),
        ),
        grid_spec=pltpu.PrefetchScalarGridSpec(
            num_scalar_prefetch=1,
            grid=(steps,),
            in_specs=[
                pl.BlockSpec((1, slots, fc), lambda f, i: (e, 0, i[1])),
                chunk(slots),
                chunk(slots),
                mine((slots, width)),
                mine((slots, piece)),
                mine((many, width)),
                mine((many, width)),
                mine((many, piece)),
                chunk(width),
                chunk(width),
                pl.BlockSpec((1, fc, width), lambda f, i: (e, base + f, 0)),
            ]
            + [ANY_SPEC] * len(done),
            out_specs=(chunk(piece), chunk(piece), ANY_SPEC),
            scratch_shapes=[pltpu.VMEM((many, fc), BF16) for _ in range(3)]
            + [pltpu.VMEM((fc, width), F32), pltpu.SemaphoreType.DMA],
        ),
        compiler_params=params(60, ("arbitrary",)),
        cost_estimate=cost(steps * fc * width * (6 * many + 2 * (many + slots)), 15 << 20),
        input_output_aliases={12 + m: m for m in range(len(done))},
        name="expert_grads",
    )(idx, a, dg, du, dy, xd, x_o, dy_o, xd_o, w_gate, w_up, w_down, *done)


def finish(idx, parts, moved, blocks, x1, share, experts_all):
    rows, total = parts[0].shape
    length, width = x1.shape
    rest = total - width
    n, _, both = blocks.shape
    part, low_rows = both // 2, both // 16

    def kernel(idx_ref, s0, s1, s2, s3, m_ref, b_ref, x_ref, sh_ref, out_ref, q_ref, k_ref, v_ref,
               o_ref, r_ref, a_ref, f_ref, gate_ref, up_ref, down_ref, small):
        out_ref[...] = (x_ref[...] + sh_ref[...].astype(F32)).astype(BF16)
        for k in range(n):
            block = m_ref[k, :rows].astype(F32)
            gate_ref[:, k * part : (k + 1) * part] = block[:, :part]
            up_ref[:, k * part : (k + 1) * part] = block[:, part:]
            low = b_ref[k, rows:].astype(F32)
            at, half = k * low_rows, low_rows // 2
            down_ref[at : at + low_rows, :both] = low[:low_rows]
            down_ref[at : at + half, both:] = low[low_rows:, :part]
            down_ref[at + half : at + low_rows, both:] = low[low_rows:, part:]
        z = idx_ref[1]
        for r, s in enumerate((s0, s1, s2, s3)):
            small[(z - r + 4) & 3] = s[:, width:].astype(F32)
            for m, ref in enumerate((q_ref, k_ref, v_ref, o_ref)):

                @pl.when(((z - r + 4) & 3) == m)
                def _(ref=ref, s=s):
                    ref[...] = s[:, :width].astype(F32)

        low = small[0]
        square = jnp.concatenate([low, jnp.zeros((rows, 128 - rest), F32)], axis=1)
        square = jnp.concatenate([square, jnp.zeros((128 - rows, 128), F32)], axis=0).T
        r_ref[...] = square[:experts_all, :rows]
        a_ref[...] = square[experts_all : experts_all + 1, :rows]
        f_ref[...] = square[experts_all + 1 : experts_all + 2, :rows]

    flat = sds((rows, width), F32)
    line = sds((1, rows), F32)
    wide = sds((rows, n * part), F32)
    return pl.pallas_call(
        kernel,
        out_shape=(
            sds((length, width), BF16),
            flat, flat, flat, flat,
            sds((experts_all, rows), F32),
            line, line,
            wide, wide, sds((n * low_rows, width), F32),
        ),
        in_specs=[SMEM_SPEC] + [VMEM_SPEC] * 8,
        out_specs=(VMEM_SPEC,) * 11,
        scratch_shapes=[pltpu.VMEM((4, rows, rest), F32)],
        compiler_params=params(60),
        name="finish",
    )(idx, *parts, moved, blocks, x1, share)


def on_device(
    tokens,
    segment_ids,
    padding,
    routes,
    w_query,
    w_key,
    w_value,
    w_out,
    w_router,
    shared_gate,
    shared_up,
    shared_down,
    gain_attn,
    gain_ffn,
    expert_gate,
    expert_up,
    expert_down,
    cotangent,
):
    length, width = tokens.shape
    planes = lax.axis_size("dp")
    i = lax.axis_index("expert").astype(jnp.int32)
    z = lax.axis_index("dp").astype(jnp.int32)
    idx = jnp.stack([i, z])
    step = width // 8
    part = shared_down.shape[0]
    spread = planes == 4

    attn_shard = pack_shard([w_query, w_key, w_value, w_out], w_router.T)

    live_row = padding.astype(F32)
    meta = jnp.concatenate([routes[:, 0], routes[:, 1], padding[0]]).astype(BF16)[None, :]
    grad_ext = jnp.concatenate([after(cotangent, attn_shard), meta, jnp.zeros((15, width), BF16)], axis=0)
    ext = grad_ext.shape[0]

    def others(columns):
        at = [(z - r) % planes for r in (1, 2, 3)]
        return jnp.concatenate([lax.dynamic_index_in_dim(columns, a, 0, False) for a in at], axis=0)

    def copies(rows):
        return jnp.broadcast_to(rows[None], (planes,) + rows.shape)

    def columns(blocks):
        return lax.all_to_all(blocks, "dp", split_axis=0, concat_axis=0, tiled=True)

    def dp_gather(rows):
        return lax.all_gather(rows, "dp", axis=0)

    g_mine = lax.all_gather(grad_ext, "expert", axis=0, axis_index_groups=same_core())
    g_far = [shift(grad_ext, k) for k in (1, 2, 3)] if spread else []
    attn_pieces = relay_gather(attn_shard)

    gain1, gain2 = gain_attn[None, :], gain_ffn[None, :]
    side = pack_side(shared_gate, shared_up, part)
    side = after(side, [p for _, _, p in attn_pieces], gain1, gain2, live_row, g_far)
    side = lax.all_to_all(side, "expert", split_axis=0, concat_axis=0, tiled=True)

    *saved, router_t, h2_copies = attention_forward(
        idx, tokens, segment_ids, live_row, gain1, gain2, attn_pieces,
    )
    x1, h2 = saved[6], saved[7]

    g_plane = [g_mine, swap(g_mine, 1)]
    if spread:
        g_far = jnp.concatenate(after(g_far, h2), axis=0)
    side = after(side, h2)
    h_mine = chips_exchange(after(h2_copies, side))
    if spread:
        h_mine = after(h_mine, g_far)
    h_plane = [h_mine, swap(h_mine, 1)]
    if spread:
        h_columns = dp_gather(h2)
        at = (i // 2) ^ 3
        corner = [
            lax.dynamic_index_in_dim(rows, at, 0, False) for rows in after((g_mine, h_mine), h_plane)
        ]
        corner = dp_gather(jnp.concatenate(corner, axis=0))
        g_far = after(g_far, h_plane)
        g_far = [g_far, swap(g_far, 2), swap(g_far, 4)]

    cut = width // 4
    x_own, xd_own, gs_own, cs_own, hot = dispatch_plane(
        idx, router_t, h_plane, g_plane, cut
    )

    weights = (expert_gate, expert_up, expert_down)
    a, dg, du, dy, yc, dr, dc = experts(x_own, gs_own, cs_own, *weights)
    shared_w = after(side, yc)
    if spread:
        g_far, h_columns = after((g_far, h_columns), yc)
        shared_w = after(shared_w, g_far)
        g_far = both_cores(g_far)
        h_far = others(h_columns)
        h_far = [h_far, swap(h_far, 2), swap(h_far, 4)]
    act, side = shared_branch(idx, h_plane, g_plane, shared_w, shared_down)
    if spread:
        side = lax.psum_scatter(side, "dp", scatter_dimension=0, tiled=True)
    else:
        side = lax.psum(side, "dp")

    def exchanged(blocks):
        return lax.all_to_all(blocks, "expert", split_axis=0, concat_axis=0, tiled=True)

    if spread:
        g_far = after(g_far, act)
        act = after(act, g_far)
    out_shares, dh_other, dh_mine = combine(
        idx, act, hot, yc, dr, dc, shared_w, shared_down
    )
    if spread:
        h_far = after(h_far, dh_other)
        dh_other = after(dh_other, h_far)
    dh_came = swap(dh_other, 1)
    if spread:
        h_far = both_cores(after(h_far, dh_came))
    dh_sums = plane_near(dh_mine, dh_came)
    dh_parts = plane_far(dh_sums)
    if spread:
        h_far, g_far, corner = after((h_far, g_far, corner), dh_sums)
        corners = both_cores([corner])
        x_far, xd_far, dy_far = dispatch_others(idx, router_t, h_far, g_far, corners, 3, cut)
        dh_parts = after(dh_parts, x_far)
    out_shares = out_shares.reshape(8 * length, width)
    grad_tokens, att_other, att_mine = attention_backward(
        idx, tokens, cotangent, live_row, gain1, gain2, saved, router_t, dh_parts, attn_pieces,
    )
    att_came = swap(att_other, 1)
    if spread:
        side = dp_gather(after(side, att_mine)).reshape(8, -1, 2 * part)
    att_sums = plane_near(att_mine, att_came)
    att_parts = plane_far(att_sums)
    def att_quarters(parts):
        att = add(parts).astype(BF16)
        small = att[:, 4 * width :]
        return jnp.stack(
            [
                jnp.concatenate(
                    [att[:, m * width : (m + 1) * width], small[:, 32 * m : 32 * (m + 1)]], axis=1
                )
                for m in range(4)
            ]
        )

    if spread:
        xs = (x_far, dy_far, xd_far)
        own = (a, dg, du, dy, xd_own)
        chunks = expert_gate.shape[2] // 512
        done = expert_grads(idx, 0, 0, chunks, own, after(xs, att_sums), weights)
        att_parts = after(att_parts, done)
        out_share = lax.psum_scatter(
            after(out_shares, att_sums), "expert", scatter_dimension=0, tiled=True
        )
        xs = after(xs, att_parts)
        att_scattered = dp_scatter(att_quarters(att_parts))
        done = expert_grads(idx, 1, 0, chunks // 2, own, xs, weights, done)
        att_scattered, side = after((att_scattered, side), done)
        moved = exchanged(side)
        xs = after(xs, att_scattered)
        att_spread = dp_spread(att_scattered)
        done = expert_grads(idx, 1, chunks // 2, chunks // 2, own, xs, weights, done)
        moved, side, att_spread, out_share = after((moved, side, att_spread, out_share), done)
        g_gate, g_up, g_down = done
        order = idx
    else:
        att_spread = dp_whole(att_quarters(att_parts))
        moved = exchanged(side)
        out_share = lax.psum_scatter(out_shares, "expert", scatter_dimension=0, tiled=True)
        order = idx * jnp.array([1, 0], jnp.int32)

        def scattered(left, right):
            local = jnp.einsum("end,enf->edf", left, right, preferred_element_type=F32)
            return lax.psum_scatter(
                local.astype(BF16), "dp", scatter_dimension=1, tiled=True
            ).astype(F32)

        g_gate, g_up, g_down = scattered(x_own, dg), scattered(x_own, du), scattered(a, dy)

    experts_all = w_router.shape[1]
    (
        output, gq, gk, gv, go, g_router, g_gain1, g_gain2, g_sgate, g_sup, g_sdown,
    ) = finish(order, att_spread, moved, side, x1, out_share, experts_all)
    return (
        output,
        grad_tokens,
        gq,
        gk,
        gv,
        go,
        g_router.T,
        g_sgate,
        g_sup,
        g_sdown,
        g_gain1.reshape(step),
        g_gain2.reshape(step),
        g_gate,
        g_up,
        g_down,
    )


def solution(mesh):
    both = P(("dp", "expert"), None)
    one = P("expert", None)
    three = P("expert", None, None)
    sliced = P("expert", "dp", None)
    return jax.shard_map(
        on_device,
        mesh=mesh,
        in_specs=(both,) * 4 + (one,) * 8 + (P(), P()) + (three,) * 3 + (both,),
        out_specs=(both, both) + (one,) * 8 + (P("expert"), P("expert")) + (sliced,) * 3,
        check_vma=False,
    )
```
